128 devices in a mesh: gx: 16 (over y_hi, x, core), gz: 8 (over z, y_lo).
Axes of the slice: x: 4, y: 4 (y_hi: 2, y_lo: 2; y = y_hi * 2 + y_lo), z: 4, core: 2. Of those that a mesh axis runs over, the one named last changes fastest.
Arguments:
- adjoint: float32 [3, 256, 128, 1024], P(None, 'gx', None, 'gz'), may hold values from -6 to 6
- velocity: float32 [3, 256, 128, 1024], P(None, 'gx', None, 'gz'), may hold values from -0.45 to 0.45
- viscosity: float32 [256, 128, 1024], P('gx', None, 'gz'), may hold values from 0.02 to 0.15
- filters: bfloat16 [512, 512, 512], P(('gx', 'gz')), may hold values from -0.25 to 0.25
- block_tiles: int32 [256, 8], replicated, may hold values from 0 to 511, all different within a row
- tile_place: int32 [512], replicated, may hold values from 0 to 511, each once
Outputs:
- adjoint_out: float32 [3, 256, 128, 1024], P(None, 'gx', None, 'gz')
- generator_tile_gradient: float32 [512, 3, 512], P(('gx', 'gz'))
The draws below stay inside these ranges and needn't reach their ends.
Inputs may be any that keep to these rules, and one draw needn't show every extreme that they name: `block_tiles`: each row lists 8 different tiles; every tile is listed by some block. `tile_place`: each tile exactly once.
All inputs are finite; a program needn't handle non-finite values.
Results may differ from the reference program's by a relative error of at most 0.0003.
Values sent between devices are 32-bit elements; how exact they have to be, the bound alone decides.
No kernel may reach another device: no remote copies, remote signals or barrier semaphores. Data moves between devices by JAX's collectives and lax.ppermute only.
A program may use at most 192 MiB of HBM per device.

```python
import math
import jax
import jax.numpy as jnp
from jax import lax

BY = 4
BZ = 128
LIST = 8
BLK = 512
NB = 256
TILES = 512
NX = 256
NY = 128
NZ = 1024
N_GZ = 8


def steps_of(rng, shape, shards, least, largest):
    factor_of, own = 1.0, jax.random.fold_in(rng, 6)
    for position, shards_of in shards:
        draws = jnp.exp(jax.random.uniform(jax.random.fold_in(own, position), (shards_of,), jnp.float32, least / len(shards), largest / len(shards)))
        factor_of = factor_of * jnp.repeat(draws, shape[position] // shards_of).reshape([-1 if axis == position else 1 for axis in range(len(shape))])
    return factor_of


def different_ones(rng, rows, amount, top, lift):
    sequence = jax.random.permutation(jax.random.fold_in(rng, 1), amount)
    favour = sequence
    for power in range(3):
        favour = favour * favour // amount
    favour = favour * lift // amount
    chance = jax.random.randint(jax.random.fold_in(rng, 2), (rows, amount), 0, 4096) + favour
    fixed_rows = jax.random.permutation(jax.random.fold_in(rng, 3), rows)[jnp.arange(amount) % rows]
    chance = jnp.where(jnp.arange(rows)[:, None] == fixed_rows[None, :], 1 << 14, chance)
    priority = chance * amount + jnp.arange(amount)
    return lax.top_k(priority.astype(jnp.int32), top)[1].astype(jnp.int32)


def normal_values(key, dims, spread, limit, cuts=(), dtype=jnp.bfloat16):
    level = steps_of(key, dims, cuts, -0.22, 0.18) if cuts else 1.0
    array = jax.random.normal(key, dims, jnp.float32) * spread * level
    return jnp.minimum(jnp.maximum(array, -limit), limit).astype(dtype)


def setup_inputs(seed: int = 0) -> dict:
    splits = jax.random.split(jax.random.key(seed), 7)
    return {
        "adjoint": normal_values(splits[0], (3, NX, NY, NZ), 1.0, 6.0, ((1, 16), (3, 8)), jnp.float32),
        "velocity": normal_values(splits[1], (3, NX, NY, NZ), 0.15, 0.45, ((1, 16), (3, 8)), jnp.float32),
        "viscosity": jnp.clip(jnp.exp(math.log(0.15) - 2.014903 * jax.random.uniform(splits[2], (NX, NY, NZ), jnp.float32) ** steps_of(splits[2], (NX, NY, NZ), ((0, 16), (2, 8)), -0.2, 0.2)), 0.02, 0.15),
        "filters": normal_values(splits[3], (TILES, BLK, BLK), BLK ** -0.5, 0.25, ((0, 128),)),
        "block_tiles": different_ones(splits[4], NB, TILES, LIST, 256),
        "tile_place": jax.random.permutation(splits[5], TILES).astype(jnp.int32),
    }


def advance(padded, visc_pad, velocity):
    centre = padded[..., 1:-1, 1:-1, 1:-1]
    east_cell = padded[..., 2:, 1:-1, 1:-1]
    west_cell = padded[..., :-2, 1:-1, 1:-1]
    north_cell = padded[..., 1:-1, 2:, 1:-1]
    south_cell = padded[..., 1:-1, :-2, 1:-1]
    upper_cell = padded[..., 1:-1, 1:-1, 2:]
    lower_cell = padded[..., 1:-1, 1:-1, :-2]
    visc_mid = visc_pad[1:-1, 1:-1, 1:-1]
    east_face = 0.5 * (visc_mid + visc_pad[2:, 1:-1, 1:-1])
    west_face = 0.5 * (visc_mid + visc_pad[:-2, 1:-1, 1:-1])
    north_face = 0.5 * (visc_mid + visc_pad[1:-1, 2:, 1:-1])
    south_face = 0.5 * (visc_mid + visc_pad[1:-1, :-2, 1:-1])
    upper_face = 0.5 * (visc_mid + visc_pad[1:-1, 1:-1, 2:])
    lower_face = 0.5 * (visc_mid + visc_pad[1:-1, 1:-1, :-2])
    transport = 0.5 * (velocity[0] * (east_cell - west_cell) + velocity[1] * (north_cell - south_cell) + velocity[2] * (upper_cell - lower_cell))
    diffusion = east_face * (east_cell - centre) - west_face * (centre - west_cell)
    diffusion = diffusion + north_face * (north_cell - centre) - south_face * (centre - south_cell)
    diffusion = diffusion + upper_face * (upper_cell - centre) - lower_face * (centre - lower_cell)
    return centre + transport + diffusion


def pad_field(field):
    wrapped = jnp.pad(field, ((0, 0), (0, 0), (1, 1)), mode="wrap")
    return jnp.pad(wrapped, ((1, 1), (1, 1), (0, 0)))


def cut_blocks(face, group_list):
    comps, rows_all, cols_all = face.shape
    reshaped_array = face.reshape(comps, rows_all // BY, BY, group_list, cols_all // (group_list * BZ), BZ)
    return reshaped_array.transpose(3, 1, 4, 0, 2, 5).reshape(-1, comps * BY * BZ)


def reference(adjoint, velocity, viscosity, filters, block_tiles, tile_place):
    visc_pad = pad_field(viscosity)

    def two_steps(component):
        middle = advance(pad_field(component), visc_pad, velocity)
        return advance(pad_field(middle), visc_pad, velocity)

    adjoint_out = lax.map(two_steps, adjoint)
    face = adjoint_out[:, 0]
    blocks = cut_blocks(face, N_GZ)
    slots = tile_place[block_tiles].reshape(-1)
    sums = jnp.zeros((TILES, 3 * BLK), jnp.float32).at[slots].add(jnp.repeat(blocks, LIST, axis=0))
    tile_view = sums.reshape(TILES, 3, BLK)
    generator_tile_gradient = jnp.einsum("gvl,gls->gvs", tile_view, filters.astype(jnp.float32), precision=lax.Precision.HIGHEST)
    return adjoint_out, generator_tile_gradient
```

```python
import functools

import jax
import jax.numpy as jnp
from jax import lax
from jax.experimental import pallas as pl
from jax.experimental.pallas import tpu as pltpu
from jax.sharding import PartitionSpec as P

F32 = jnp.float32
BF16 = jnp.bfloat16
ANY = pl.BlockSpec(memory_space=pl.ANY)
VM = pl.BlockSpec(memory_space=pltpu.VMEM)
SM = pl.BlockSpec(memory_space=pltpu.SMEM)
VLIM = 40 * 1024 * 1024
ROWS = 32


def lanes(shape):
    return lax.broadcasted_iota(jnp.int32, shape, len(shape) - 1)


def roll(x, shift, axis):
    if isinstance(shift, int):
        shift = shift % x.shape[axis]
    return pltpu.roll(x, shift, axis)


def pack_kernel(adj, vel, visc, zl, zr, acc_l, acc_r):
    x = pl.program_id(0)
    lane = lanes((128, 128))
    pair = lane >> 1
    pair_l = ((lane + 2) & 127) >> 1
    planes = [adj[c, 0] for c in range(3)] + [visc[0]] + [vel[c, 0] for c in range(3)]
    for k, plane in enumerate(planes):
        block, m = (0, k * 16 + x) if k < 4 else (1, (k - 4) * 16 + x)
        turned = roll(plane, 2 * m, 1)
        acc_r[block] = jnp.where(pair == m, turned, acc_r[block])
        acc_l[block] = jnp.where(pair_l == m, turned, acc_l[block])

    @pl.when(x == 15)
    def _():
        for block in range(2):
            zr[block] = acc_r[block]
            zl[block] = roll(acc_l[block], 2, 1)


def pack(adj, vel, visc):
    out = jax.ShapeDtypeStruct((2, 128, 128), F32)
    whole = pl.BlockSpec((2, 128, 128), lambda x: (0, 0, 0))
    return pl.pallas_call(
        pack_kernel,
        grid=(16,),
        in_specs=[
            pl.BlockSpec((3, 1, 128, 128), lambda x: (0, x, 0, 0)),
            pl.BlockSpec((3, 1, 128, 128), lambda x: (0, x, 0, 0)),
            pl.BlockSpec((1, 128, 128), lambda x: (x, 0, 0)),
        ],
        out_specs=[whole, whole],
        out_shape=[out, out],
        scratch_shapes=[pltpu.VMEM((2, 128, 128), F32), pltpu.VMEM((2, 128, 128), F32)],
        name="pack",
    )(adj, vel, visc)


def spread(a, group):
    kept = jnp.where((lanes(a.shape) >> 5) == group, a, 0.0)
    kept = kept + roll(kept, 32, 1)
    return kept + roll(kept, 64, 1)


def shift_rows(a, by):
    row = lax.broadcasted_iota(jnp.int32, a.shape, 0)
    moved = roll(a, by, 0)
    edge = 0 if by > 0 else a.shape[0] - 1
    return jnp.where(row == edge, 0.0, moved)


def edge_centre(hl, hr):
    odd = (lanes((128, 128)) & 1) == 1
    return jnp.where(odd, hl[0], hr[0])


def edge_middle(hl, hr, zl, zr, low=None, high=None):
    lane = lanes((128, 128))
    odd = (lane & 1) == 1
    x = (lane >> 1) & 15
    centre = jnp.where(odd, hl[0], hr[0])
    minus = jnp.where(odd, roll(hl[0], 1, 1), roll(zl[0], -1, 1))
    plus = jnp.where(odd, roll(zr[0], 1, 1), roll(hr[0], -1, 1))
    velocity = jnp.where(odd, hl[1], hr[1])
    west = roll(centre, 2, 1)
    east = roll(centre, -2, 1)
    west = jnp.where(x == 0, 0.0 if low is None else roll(low, -30, 1), west)
    east = jnp.where(x == 15, 0.0 if high is None else roll(high, 30, 1), east)
    north = shift_rows(centre, -1)
    south = shift_rows(centre, 1)
    visc = spread(centre, 3)
    total = 0.0
    result = 0.0
    for d, (up, down) in enumerate(((east, west), (north, south), (plus, minus))):
        v = spread(velocity, d)
        a_up = 0.5 * ((visc + spread(up, 3)) + v)
        a_down = 0.5 * ((visc + spread(down, 3)) - v)
        total = total + (a_up + a_down)
        result = result + (a_up * up + a_down * down)
    return result + (1.0 - total) * centre


def coefficients(visc_s, vel_s, edge, coef_s, q):
    lane = lanes((ROWS, 128))
    for r in range(0, 128, ROWS):
        centre = visc_s[q, pl.ds(8 + r, ROWS), :]
        ends = roll(edge[pl.ds(r, ROWS), :], 127 - 2 * (48 + q), 1)
        up = jnp.where(lane == 127, ends, roll(centre, -1, 1))
        down = jnp.where(lane == 0, ends, roll(centre, 1, 1))
        pairs = (
            (visc_s[q + 1, pl.ds(8 + r, ROWS), :], visc_s[q - 1, pl.ds(8 + r, ROWS), :]),
            (visc_s[q, pl.ds(9 + r, ROWS), :], visc_s[q, pl.ds(7 + r, ROWS), :]),
            (up, down),
        )
        total = 0.0
        for d, (plus, minus) in enumerate(pairs):
            v = vel_s[d, q, pl.ds(r, ROWS), :]
            a_plus = 0.5 * ((centre + plus) + v)
            a_minus = 0.5 * ((centre + minus) - v)
            coef_s[2 * d, q, pl.ds(r, ROWS), :] = a_plus
            coef_s[2 * d + 1, q, pl.ds(r, ROWS), :] = a_minus
            total = total + (a_plus + a_minus)
        coef_s[6, q, pl.ds(r, ROWS), :] = 1.0 - total


def apply_step(src, edge, coef_s, q, store):
    lane = lanes((ROWS, 128))
    for r in range(0, 128, ROWS):
        a = [coef_s[k, q, pl.ds(r, ROWS), :] for k in range(7)]
        for c in range(3):
            centre = src[c, q, pl.ds(8 + r, ROWS), :]
            ends = roll(edge[pl.ds(r, ROWS), :], 127 - 2 * (c * 16 + q), 1)
            up = jnp.where(lane == 127, ends, roll(centre, -1, 1))
            down = jnp.where(lane == 0, ends, roll(centre, 1, 1))
            out = a[6] * centre
            out = out + a[0] * src[c, q + 1, pl.ds(8 + r, ROWS), :]
            out = out + a[1] * src[c, q - 1, pl.ds(8 + r, ROWS), :]
            out = out + a[2] * src[c, q, pl.ds(9 + r, ROWS), :]
            out = out + a[3] * src[c, q, pl.ds(7 + r, ROWS), :]
            out = out + a[4] * up
            out = out + a[5] * down
            store(c, r, out)


def clear_walls(ref, lead):
    for index in lead:
        ref[(*index, pl.ds(0, 8), slice(None))] = jnp.zeros((8, 128), F32)
        ref[(*index, pl.ds(136, 8), slice(None))] = jnp.zeros((8, 128), F32)


def scratch(nq):
    return [
        pltpu.VMEM((3, nq, 144, 128), F32),
        pltpu.VMEM((nq, 144, 128), F32),
        pltpu.VMEM((3, nq, 128, 128), F32),
        pltpu.VMEM((3, nq, 144, 128), F32),
        pltpu.VMEM((7, nq, 128, 128), F32),
        pltpu.VMEM((2, 128, 128), F32),
    ]


def begin(copies, sems):
    started = [pltpu.make_async_copy(s, t, sems.at[i]) for i, (s, t) in enumerate(copies)]
    for copy in started:
        copy.start()
    return started


def main_copies(adj, vel, visc, adj_s, visc_s, vel_s, x0, q0, n):
    rows = pl.ds(8, 128)
    pairs = [(adj.at[c, pl.ds(x0, n)], adj_s.at[c, pl.ds(q0, n), rows]) for c in range(3)]
    pairs += [(vel.at[c, pl.ds(x0, n)], vel_s.at[c, pl.ds(q0, n)]) for c in range(3)]
    pairs += [(visc.at[pl.ds(x0, n)], visc_s.at[pl.ds(q0, n), rows])]
    return pairs


def run_steps(adj_s, visc_s, vel_s, mid_s, coef_s, edges, mids, finals, put, after_mid=None):
    for lo, hi in mids:

        def first(q, _):
            coefficients(visc_s, vel_s, edges.at[0], coef_s, q)

            def store(c, r, v):
                mid_s[c, q, pl.ds(8 + r, ROWS), :] = v

            apply_step(adj_s, edges.at[0], coef_s, q, store)
            return 0

        lax.fori_loop(lo, hi, first, 0)
    if after_mid:
        after_mid()
    for lo, hi in finals:

        def second(q, _):
            apply_step(mid_s, edges.at[1], coef_s, q, put(q))
            return 0

        lax.fori_loop(lo, hi, second, 0)


def face_kernel(
    adj, vel, visc, hl, hr, zl, zr,
    face, centre, middle, msg_lo, msg_hi,
    adj_s, visc_s, vel_s, mid_s, coef_s, edges, sems, sems_x, sem_c,
):
    started = begin(main_copies(adj, vel, visc, adj_s, visc_s, vel_s, 0, 1, 3), sems)
    moved = []
    for msg, x, vx in ((msg_lo, 0, 0), (msg_hi, 14, 15)):
        for c in range(3):
            moved.append((adj.at[c, pl.ds(x, 2)], msg.at[pl.ds(2 * c, 2)]))
            moved.append((vel.at[c, pl.ds(vx, 1)], msg.at[pl.ds(6 + c, 1)]))
        moved.append((visc.at[pl.ds(x, 2)], msg.at[pl.ds(9, 2)]))
    moved = begin(moved, sems_x)
    cen = edge_centre(hl, hr)
    centre[0] = cen
    corners = begin([(centre, msg_lo.at[pl.ds(11, 1)]), (centre, msg_hi.at[pl.ds(11, 1)])], sem_c)
    mid = edge_middle(hl, hr, zl, zr)
    middle[...] = mid
    edges[0] = roll(cen, 2, 1)
    edges[1] = roll(mid, 2, 1)
    for c in range(3):
        adj_s[c, 0] = jnp.zeros((144, 128), F32)
        mid_s[c, 0] = jnp.zeros((144, 128), F32)
    visc_s[0] = jnp.zeros((144, 128), F32)
    clear_walls(adj_s, [(c, q) for c in range(3) for q in range(1, 4)])
    clear_walls(mid_s, [(c, q) for c in range(3) for q in range(1, 3)])
    clear_walls(visc_s, [(q,) for q in range(1, 4)])
    for copy in started:
        copy.wait()

    def put(q):
        def store(c, r, v):
            face[c, pl.ds(r, ROWS), :] = v

        return store

    run_steps(adj_s, visc_s, vel_s, mid_s, coef_s, edges, [(1, 3)], [(1, 2)], put)
    for copy in corners + moved:
        copy.wait()


def face_call(adj, vel, visc, hl, hr, zl, zr):
    msg = jax.ShapeDtypeStruct((12, 128, 128), F32)
    return pl.pallas_call(
        face_kernel,
        in_specs=[ANY, ANY, ANY, VM, VM, VM, VM],
        out_specs=[VM, VM, VM, ANY, ANY],
        out_shape=[
            jax.ShapeDtypeStruct((3, 128, 128), F32),
            jax.ShapeDtypeStruct((1, 128, 128), F32),
            jax.ShapeDtypeStruct((128, 128), F32),
            msg,
            msg,
        ],
        scratch_shapes=scratch(4)
        + [
            pltpu.SemaphoreType.DMA((7,)),
            pltpu.SemaphoreType.DMA((14,)),
            pltpu.SemaphoreType.DMA((2,)),
        ],
        compiler_params=pltpu.CompilerParams(vmem_limit_bytes=VLIM),
        name="face",
    )(adj, vel, visc, hl, hr, zl, zr)


def inner_kernel(
    x0, nq, first, adj, vel, visc, centre, middle, *rest
):
    if not first:
        rest = rest[1:]
    out, adj_s, visc_s, vel_s, mid_s, coef_s, edges, out_s, sems, sems_o = rest
    started = begin(main_copies(adj, vel, visc, adj_s, visc_s, vel_s, x0, 0, nq), sems)
    edges[0] = roll(centre[0], -2 * x0, 1)
    edges[1] = roll(middle[...], -2 * x0, 1)
    clear_walls(adj_s, [(c, q) for c in range(3) for q in range(nq)])
    clear_walls(mid_s, [(c, q) for c in range(3) for q in range(nq)])
    clear_walls(visc_s, [(q,) for q in range(nq)])
    for copy in started:
        copy.wait()

    def put(q):
        def store(c, r, v):
            out_s[c, q, pl.ds(r, ROWS), :] = v

        return store

    run_steps(adj_s, visc_s, vel_s, mid_s, coef_s, edges, [(1, nq - 1)], [(2, nq - 2)], put)
    n = nq - 4
    for copy in begin(
        [(out_s.at[c, pl.ds(2, n)], out.at[c, pl.ds(x0 + 2, n)]) for c in range(3)], sems_o
    ):
        copy.wait()


def inner(x0, nq, adj, vel, visc, centre, middle, out=None):
    first = out is None
    args = [adj, vel, visc, centre, middle] + ([] if first else [out])
    return pl.pallas_call(
        functools.partial(inner_kernel, x0, nq, first),
        in_specs=[ANY, ANY, ANY, VM, VM] + ([] if first else [ANY]),
        out_specs=ANY,
        out_shape=jax.ShapeDtypeStruct((3, 16, 128, 128), F32),
        scratch_shapes=scratch(nq)
        + [
            pltpu.VMEM((3, nq, 128, 128), F32),
            pltpu.SemaphoreType.DMA((7,)),
            pltpu.SemaphoreType.DMA((3,)),
        ],
        input_output_aliases={} if first else {5: 0},
        compiler_params=pltpu.CompilerParams(vmem_limit_bytes=VLIM),
        name="inner",
    )(*args)


def outer_kernel(
    place, adj, vel, visc, hl, hr, zl, zr, low, high, _,
    out, adj_s, visc_s, vel_s, mid_s, coef_s, edges, out_s, corner, sems, sems_o, sems_c,
):
    rows = pl.ds(8, 128)
    corners = begin([(low.at[pl.ds(11, 1)], corner.at[pl.ds(0, 1)]), (high.at[pl.ds(11, 1)], corner.at[pl.ds(1, 1)])], sems_c)
    pairs = main_copies(adj, vel, visc, adj_s, visc_s, vel_s, 0, 2, 4)
    pairs += main_copies(adj, vel, visc, adj_s, visc_s, vel_s, 12, 6, 4)
    for msg, q, qv in ((low, 0, 1), (high, 10, 10)):
        for c in range(3):
            pairs.append((msg.at[pl.ds(2 * c, 2)], adj_s.at[c, pl.ds(q, 2), rows]))
            pairs.append((msg.at[pl.ds(6 + c, 1)], vel_s.at[c, pl.ds(qv, 1)]))
        pairs.append((msg.at[pl.ds(9, 2)], visc_s.at[pl.ds(q, 2), rows]))
    started = begin(pairs, sems)
    clear_walls(adj_s, [(c, q) for c in range(3) for q in range(12)])
    clear_walls(mid_s, [(c, q) for c in range(3) for q in range(12)])
    clear_walls(visc_s, [(q,) for q in range(12)])
    for copy in corners:
        copy.wait()
    x = (lanes((128, 128)) >> 1) & 15
    cen = edge_centre(hl, hr)
    mid = edge_middle(hl, hr, zl, zr, corner[0], corner[1])
    turned = jnp.where(x < 6, roll(cen, 4, 1), roll(cen, -12, 1))
    turned = jnp.where(x == 1, roll(corner[0], -28, 1), turned)
    edges[0] = jnp.where(x == 10, roll(corner[1], 20, 1), turned)
    edges[1] = jnp.where(x < 6, roll(mid, 4, 1), roll(mid, -12, 1))
    for copy in started:
        copy.wait()

    def walls():
        @pl.when(place[0] == 0)
        def _():
            for c in range(3):
                mid_s[c, 1] = jnp.zeros((144, 128), F32)

        @pl.when(place[0] == place[1] - 1)
        def _():
            for c in range(3):
                mid_s[c, 10] = jnp.zeros((144, 128), F32)

    def put(q):
        def store(c, r, v):
            out_s[c, q, pl.ds(r, ROWS), :] = v

        return store

    run_steps(
        adj_s, visc_s, vel_s, mid_s, coef_s, edges, [(1, 5), (7, 11)], [(2, 4), (8, 10)], put, walls
    )
    pairs = [(out_s.at[c, pl.ds(2, 2)], out.at[c, pl.ds(0, 2)]) for c in range(3)]
    pairs += [(out_s.at[c, pl.ds(8, 2)], out.at[c, pl.ds(14, 2)]) for c in range(3)]
    for copy in begin(pairs, sems_o):
        copy.wait()


def outer(place, adj, vel, visc, hl, hr, zl, zr, low, high, out):
    return pl.pallas_call(
        outer_kernel,
        in_specs=[SM, ANY, ANY, ANY, VM, VM, VM, VM, ANY, ANY, ANY],
        out_specs=ANY,
        out_shape=jax.ShapeDtypeStruct((3, 16, 128, 128), F32),
        scratch_shapes=scratch(12)
        + [
            pltpu.VMEM((3, 12, 128, 128), F32),
            pltpu.VMEM((2, 128, 128), F32),
            pltpu.SemaphoreType.DMA((28,)),
            pltpu.SemaphoreType.DMA((6,)),
            pltpu.SemaphoreType.DMA((2,)),
        ],
        input_output_aliases={10: 0},
        compiler_params=pltpu.CompilerParams(vmem_limit_bytes=VLIM),
        name="outer",
    )(place, adj, vel, visc, hl, hr, zl, zr, low, high, out)


def pieces(a):
    high = a.astype(BF16)
    rest = a - high.astype(F32)
    mid = rest.astype(BF16)
    low = (rest - mid.astype(F32)).astype(BF16)
    return high, mid, low


def sums_kernel(select, face, out):
    chosen = select[...].astype(BF16)
    for c in range(3):
        total = 0.0
        for piece in pieces(face[c]):
            total = total + jnp.dot(chosen, piece, preferred_element_type=F32)
        for g in range(8):
            out[g, c] = total[g * 16 : g * 16 + 16]


def partial_sums(select, face):
    return pl.pallas_call(
        sums_kernel,
        in_specs=[VM, VM],
        out_specs=VM,
        out_shape=jax.ShapeDtypeStruct((8, 3, 16, 128), F32),
        name="sums",
    )(select, face)


def product_kernel(parts, filters, out, sums):
    total = parts[0]
    for g in range(1, 8):
        total = total + parts[g]
    sums[...] = total
    for p in range(4):
        view = jnp.concatenate([sums[:, p * 4 + i, :] for i in range(4)], axis=1)
        stacked = jnp.concatenate(pieces(view), axis=0)
        wide = jnp.dot(stacked, filters[p], preferred_element_type=F32)
        out[p] = wide[0:3] + (wide[3:6] + wide[6:9])


def product(parts, filters):
    return pl.pallas_call(
        product_kernel,
        in_specs=[VM, VM],
        out_specs=VM,
        out_shape=jax.ShapeDtypeStruct((4, 3, 512), F32),
        scratch_shapes=[pltpu.VMEM((3, 16, 128), F32)],
        compiler_params=pltpu.CompilerParams(vmem_limit_bytes=VLIM),
        name="product",
    )(parts, filters)


def shards(adjoint, velocity, viscosity, filters, block_tiles, tile_place):
    gx = lax.axis_index("gx")
    gz = lax.axis_index("gz")
    nx = lax.axis_size("gx")
    nz = lax.axis_size("gz")
    ring = [(i, (i + 1) % nz) for i in range(nz)]
    back = [(b, a) for a, b in ring]
    along = [(i, i + 1) for i in range(nx - 1)]
    against = [(b, a) for a, b in along]

    lists = lax.dynamic_slice_in_dim(block_tiles, gz * 32, 32, 0)
    tiles = jnp.arange(512, dtype=jnp.int32)
    places = jnp.sum(jnp.where(lists[:, :, None] == tiles, tile_place, 0), axis=2)
    wanted = gx * 32 + jnp.arange(32, dtype=jnp.int32)
    chosen = jnp.sum((places[None] == wanted[:, None, None]).astype(F32), axis=2)
    select = (chosen[:, None, :, None] * jnp.eye(4, dtype=F32)[None, :, None, :]).reshape(128, 128)

    zl, zr = pack(adjoint, velocity, viscosity)
    hl = lax.ppermute(zl, "gz", ring)
    hr = lax.ppermute(zr, "gz", back)
    face, centre, middle, msg_lo, msg_hi = face_call(
        adjoint, velocity, viscosity, hl, hr, zl, zr
    )
    face = jnp.where(gx == 0, face, 0.0)
    got = [lax.ppermute(face, "gx", [(0, k)]) for k in (8, 2, 6)]
    low = lax.ppermute(msg_hi, "gx", along)
    high = lax.ppermute(msg_lo, "gx", against)
    out = inner(0, 10, adjoint, velocity, viscosity, centre, middle)
    face = face + ((got[0] + got[1]) + got[2])
    face = face + lax.ppermute(face, "gx", [(0, 4), (2, 10), (6, 14), (8, 12)])
    out = inner(6, 10, adjoint, velocity, viscosity, centre, middle, out)
    face = face + lax.ppermute(face, "gx", [(i, i + 1) for i in range(0, nx, 2)])
    parts = lax.all_to_all(partial_sums(select, face), "gz", 0, 0)
    gradient = product(parts, filters)
    place = jnp.stack([gx, jnp.int32(nx)]).astype(jnp.int32)
    out = outer(place, adjoint, velocity, viscosity, hl, hr, zl, zr, low, high, out)
    return out, gradient


def solution(mesh):
    placed = (
        P(None, "gx", None, "gz"),
        P(None, "gx", None, "gz"),
        P("gx", None, "gz"),
        P(("gx", "gz"), None, None),
        P(),
        P(),
    )
    return jax.shard_map(
        shards,
        mesh=mesh,
        in_specs=placed,
        out_specs=(P(None, "gx", None, "gz"), P(("gx", "gz"), None, None)),
        check_vma=False,
    )
```

```python
import functools

import jax
import jax.numpy as jnp
from jax import lax
from jax.experimental import pallas as pl
from jax.experimental.pallas import tpu as pltpu
from jax.sharding import PartitionSpec as P

F32 = jnp.float32
BF16 = jnp.bfloat16
ANY = pl.BlockSpec(memory_space=pl.ANY)
VM = pl.BlockSpec(memory_space=pltpu.VMEM)
SM = pl.BlockSpec(memory_space=pltpu.SMEM)
MIB = 1024 * 1024
ROWS = 32


def lanes(shape):
    return lax.broadcasted_iota(jnp.int32, shape, len(shape) - 1)


def roll(x, shift, axis):
    if isinstance(shift, int):
        shift = shift % x.shape[axis]
    return pltpu.roll(x, shift, axis)


def in_vmem(shape):
    return pltpu.VMEM(shape, F32)


STATE = {
    "adj": (3, 20, 144, 128),
    "visc": (20, 144, 128),
    "vel": (3, 18, 128, 128),
    "mid": (3, 18, 144, 128),
    "coef": (7, 18, 128, 128),
}


def params(mib):
    return pltpu.CompilerParams(vmem_limit_bytes=mib * MIB)


def hbm(x):
    return pltpu.with_memory_space_constraint(x, pltpu.HBM)


def vmem(x):
    return pltpu.with_memory_space_constraint(x, pltpu.VMEM)


def clear_walls(ref, lead):
    for index in lead:
        ref[(*index, pl.ds(0, 8), slice(None))] = jnp.zeros((8, 128), F32)
        ref[(*index, pl.ds(136, 8), slice(None))] = jnp.zeros((8, 128), F32)


def begin(copies, sems):
    started = [pltpu.make_async_copy(s, t, sems.at[i]) for i, (s, t) in enumerate(copies)]
    for copy in started:
        copy.start()
    return started


def pack_kernel(adj, vel, visc, adj_s, visc_s, vel_s, zl, zr, acc_l, acc_r, sems):
    def copies(g):
        rows = pl.ds(g * 32, 32)
        padded = pl.ds(8 + g * 32, 32)
        return (
            (adj.at[:, :, rows], adj_s.at[:, pl.ds(2, 16), padded]),
            (visc.at[:, rows], visc_s.at[pl.ds(2, 16), padded]),
            (vel.at[:, :, rows], vel_s.at[:, pl.ds(1, 16), rows]),
        )

    started = [begin(copies(g), sems.at[g]) for g in range(4)]
    clear_walls(adj_s, [(c, q) for c in range(3) for q in range(1, 20)])
    clear_walls(visc_s, [(q,) for q in range(1, 20)])
    zero = jnp.zeros((144, 128), F32)
    visc_s[1] = zero
    for c in range(3):
        adj_s[c, 1] = zero
    lane = lanes((32, 128))
    pair = lane >> 1
    pair_l = ((lane + 2) & 127) >> 1
    for g in range(4):
        for copy in started[g]:
            copy.wait()
        rows = pl.ds(g * 32, 32)
        padded = pl.ds(8 + g * 32, 32)
        half = g // 2
        left = jnp.zeros((32, 128), F32)
        right = jnp.zeros((32, 128), F32)
        for m in range(64):
            c, x = divmod(m, 16)
            plane = adj_s[c, x + 2, padded] if c < 3 else visc_s[x + 2, padded]
            turned = roll(plane, 2 * m, 1)
            right = jnp.where(pair == m, turned, right)
            left = jnp.where(pair_l == m, turned, left)
        zr[rows] = right
        zl[rows] = roll(left, 2, 1)
        left = jnp.zeros((32, 128), F32)
        right = jnp.zeros((32, 128), F32)
        for m in range(48):
            d, x = divmod(m, 16)
            at = 2 * m + half
            turned = roll(vel_s[d, x + 1, rows], at, 1)
            right = jnp.where(lane == at, turned, right)
            left = jnp.where(lane == (at - 1) % 128, turned, left)
        acc_r[rows] = right
        acc_l[rows] = roll(left, 1, 1)
    even = (lanes((64, 128)) & 1) == 0
    zr[pl.ds(128, 64)] = jnp.where(even, acc_r[pl.ds(0, 64)], acc_r[pl.ds(64, 64)])
    zl[pl.ds(128, 64)] = jnp.where(even, acc_l[pl.ds(0, 64)], acc_l[pl.ds(64, 64)])


def pack(adj, vel, visc):
    return pl.pallas_call(
        pack_kernel,
        in_specs=[ANY, ANY, ANY],
        out_specs=[VM] * 5,
        out_shape=[in_vmem(STATE[k]) for k in ("adj", "visc", "vel")] + [in_vmem((192, 128))] * 2,
        scratch_shapes=[
            pltpu.VMEM((128, 128), F32),
            pltpu.VMEM((128, 128), F32),
            pltpu.SemaphoreType.DMA((4, 3)),
        ],
        compiler_params=params(4),
        name="pack",
    )(hbm(adj), hbm(vel), hbm(visc))


def spread(a, group):
    kept = jnp.where((lanes(a.shape) >> 5) == group, a, 0.0)
    kept = kept + roll(kept, 32, 1)
    return kept + roll(kept, 64, 1)


def shift_rows(a, by):
    row = lax.broadcasted_iota(jnp.int32, a.shape, 0)
    moved = roll(a, by, 0)
    edge = 0 if by > 0 else a.shape[0] - 1
    return jnp.where(row == edge, 0.0, moved)


def edge_centre(hl, hr):
    odd = (lanes((128, 128)) & 1) == 1
    return jnp.where(odd, hl[pl.ds(0, 128)], hr[pl.ds(0, 128)])


def edge_velocity(message):
    both = message[pl.ds(128, 64)]
    odd = (lanes(both.shape) & 1) == 1
    upper = jnp.where(odd, roll(both, 1, 1), both)
    lower = jnp.where(odd, both, roll(both, -1, 1))
    return jnp.concatenate([upper, lower], axis=0)


def edge_middle(hl, hr, zl, zr, low=None, high=None):
    lane = lanes((128, 128))
    odd = (lane & 1) == 1
    x = (lane >> 1) & 15
    first = pl.ds(0, 128)
    left, right = hl[first], hr[first]
    centre = jnp.where(odd, left, right)
    minus = jnp.where(odd, roll(left, 1, 1), roll(zl[first], -1, 1))
    plus = jnp.where(odd, roll(zr[first], 1, 1), roll(right, -1, 1))
    velocity = jnp.where(odd, edge_velocity(hl), edge_velocity(hr))
    west = roll(centre, 2, 1)
    east = roll(centre, -2, 1)
    west = jnp.where(x == 0, 0.0 if low is None else roll(low, -30, 1), west)
    east = jnp.where(x == 15, 0.0 if high is None else roll(high, 30, 1), east)
    north = shift_rows(centre, -1)
    south = shift_rows(centre, 1)
    visc = spread(centre, 3)
    total = 0.0
    result = 0.0
    for d, (up, down) in enumerate(((east, west), (north, south), (plus, minus))):
        v = spread(velocity, d)
        a_up = 0.5 * ((visc + spread(up, 3)) + v)
        a_down = 0.5 * ((visc + spread(down, 3)) - v)
        total = total + (a_up + a_down)
        result = result + (a_up * up + a_down * down)
    return result + (1.0 - total) * centre


def ends(edge, r, m):
    return roll(edge[pl.ds(r, ROWS), :], (127 - 2 * m) % 128 if isinstance(m, int) else 127 - 2 * m, 1)


def first_step(adj_s, visc_s, vel_s, mid_s, coef_s, edge, x, ex):
    lane = lanes((ROWS, 128))
    q, t = x + 2, x + 1
    for r in range(0, 128, ROWS):
        rows, here = pl.ds(r, ROWS), pl.ds(8 + r, ROWS)
        above, below = pl.ds(9 + r, ROWS), pl.ds(7 + r, ROWS)

        def sides(plane, m):
            end = ends(edge, r, m)
            up = jnp.where(lane == 127, end, roll(plane, -1, 1))
            return up, jnp.where(lane == 0, end, roll(plane, 1, 1))

        centre = visc_s[q, here, :]
        pairs = (
            (visc_s[q + 1, here, :], visc_s[q - 1, here, :]),
            (visc_s[q, above, :], visc_s[q, below, :]),
            sides(centre, 48 + ex),
        )
        a = []
        for d, (plus, minus) in enumerate(pairs):
            v = vel_s[d, t, rows, :]
            a.append(0.5 * ((centre + plus) + v))
            a.append(0.5 * ((centre + minus) - v))
        a.append(1.0 - (((a[0] + a[1]) + (a[2] + a[3])) + (a[4] + a[5])))
        for k in range(7):
            coef_s[k, t, rows, :] = a[k]
        for c in range(3):
            centre = adj_s[c, q, here, :]
            up, down = sides(centre, c * 16 + ex)
            out = a[6] * centre
            out = out + a[0] * adj_s[c, q + 1, here, :]
            out = out + a[1] * adj_s[c, q - 1, here, :]
            out = out + a[2] * adj_s[c, q, above, :]
            out = out + a[3] * adj_s[c, q, below, :]
            out = out + a[4] * up
            mid_s[c, t, here, :] = out + a[5] * down
    for c in range(3):
        mid_s[c, t, pl.ds(0, 8), :] = jnp.zeros((8, 128), F32)
        mid_s[c, t, pl.ds(136, 8), :] = jnp.zeros((8, 128), F32)


def second_step(mid_s, coef_s, edge, x, store):
    lane = lanes((ROWS, 128))
    t = x + 1
    for r in range(0, 128, ROWS):
        rows, here = pl.ds(r, ROWS), pl.ds(8 + r, ROWS)
        above, below = pl.ds(9 + r, ROWS), pl.ds(7 + r, ROWS)
        a = [coef_s[k, t, rows, :] for k in range(7)]
        for c in range(3):
            centre = mid_s[c, t, here, :]
            end = ends(edge, r, c * 16 + x)
            out = a[6] * centre
            out = out + a[0] * mid_s[c, t + 1, here, :]
            out = out + a[1] * mid_s[c, t - 1, here, :]
            out = out + a[2] * mid_s[c, t, above, :]
            out = out + a[3] * mid_s[c, t, below, :]
            out = out + a[4] * jnp.where(lane == 127, end, roll(centre, -1, 1))
            store(c, rows, out + a[5] * jnp.where(lane == 0, end, roll(centre, 1, 1)))


def face_kernel(
    place, adj_s, visc_s, vel_s, hl, hr, zl, zr,
    face, mid_s, coef_s, centre, middle, msg_lo, msg_hi, sems,
):
    moved = []
    for msg, q, t in ((msg_lo, 2, 1), (msg_hi, 16, 16)):
        inside = pl.ds(8, 128)
        for c in range(3):
            moved.append((adj_s.at[c, pl.ds(q, 2), inside], msg.at[pl.ds(2 * c, 2)]))
            moved.append((vel_s.at[c, pl.ds(t, 1)], msg.at[pl.ds(6 + c, 1)]))
        moved.append((visc_s.at[pl.ds(q, 2), inside], msg.at[pl.ds(9, 2)]))
    centre[0] = edge_centre(hl, hr)
    moved += [(centre, msg_lo.at[pl.ds(11, 1)]), (centre, msg_hi.at[pl.ds(11, 1)])]
    moved = begin(moved, sems)
    middle[...] = edge_middle(hl, hr, zl, zr)
    for c in range(3):
        mid_s[c, 0] = jnp.zeros((144, 128), F32)
    for x in range(2):
        first_step(adj_s, visc_s, vel_s, mid_s, coef_s, centre.at[0], x, x)
    own = jnp.where(place[0] == 0, 1.0, 0.0)

    def store(c, rows, v):
        face[c, rows, :] = v * own

    second_step(mid_s, coef_s, middle, 0, store)
    for copy in moved:
        copy.wait()


def face_call(place, state, hl, hr, zl, zr):
    msg = pltpu.HBM((12, 128, 128), F32)
    return pl.pallas_call(
        face_kernel,
        in_specs=[SM] + [VM] * 7,
        out_specs=[VM] * 5 + [ANY, ANY],
        out_shape=[
            in_vmem((3, 128, 128)),
            in_vmem(STATE["mid"]),
            in_vmem(STATE["coef"]),
            in_vmem((1, 128, 128)),
            in_vmem((128, 128)),
            msg,
            msg,
        ],
        scratch_shapes=[pltpu.SemaphoreType.DMA((16,))],
        compiler_params=params(4),
        name="face",
    )(place, *[vmem(a) for a in (*state, hl, hr, zl, zr)])


def send(out_s, out, sems, i, x):
    return pltpu.make_async_copy(out_s.at[:, pl.ds(i, 1)], out.at[:, pl.ds(x, 1)], sems.at[i])


def inner_kernel(adj_s, visc_s, vel_s, centre, middle, _, __, mid_s, coef_s, out, out_s, sems):
    def first(x, carry):
        first_step(adj_s, visc_s, vel_s, mid_s, coef_s, centre.at[0], x, x)
        return carry

    lax.fori_loop(2, 9, first, 0)

    def second(x, carry):
        def store(c, rows, v):
            out_s[c, x - 2, rows, :] = v

        second_step(mid_s, coef_s, middle, x, store)
        send(out_s, out, sems, x - 2, x).start()
        return carry

    lax.fori_loop(2, 8, second, 0)
    for i in range(6):
        send(out_s, out, sems, i, i + 2).wait()


def inner(state, centre, middle, mid, coef):
    return pl.pallas_call(
        inner_kernel,
        in_specs=[VM] * 7,
        out_specs=[VM, VM, ANY],
        out_shape=[
            in_vmem(STATE["mid"]),
            in_vmem(STATE["coef"]),
            pltpu.HBM((3, 16, 128, 128), F32),
        ],
        scratch_shapes=[pltpu.VMEM((3, 6, 128, 128), F32), pltpu.SemaphoreType.DMA((6,))],
        input_output_aliases={5: 0, 6: 1},
        compiler_params=params(4),
        name="inner",
    )(*[vmem(a) for a in (*state, centre, middle, mid, coef)])


def outer_kernel(
    place, adj_i, visc_i, vel_i, mid_i, coef_i, centre, middle, hl, hr, zl, zr, low, high, _,
    adj_s, visc_s, vel_s, mid_s, coef_s, out, out_s, corner, edges, sems, sems_o,
):
    inside = pl.ds(8, 128)
    pairs = [(low.at[pl.ds(11, 1)], corner.at[pl.ds(0, 1)])]
    pairs += [(high.at[pl.ds(11, 1)], corner.at[pl.ds(1, 1)])]
    for msg, q, t in ((low, 0, 0), (high, 18, 17)):
        for c in range(3):
            pairs.append((msg.at[pl.ds(2 * c, 2)], adj_s.at[c, pl.ds(q, 2), inside]))
            pairs.append((msg.at[pl.ds(6 + c, 1)], vel_s.at[c, pl.ds(t, 1)]))
        pairs.append((msg.at[pl.ds(9, 2)], visc_s.at[pl.ds(q, 2), inside]))
    started = begin(pairs, sems)

    def first(x, carry):
        first_step(adj_s, visc_s, vel_s, mid_s, coef_s, centre.at[0], x, x)
        return carry

    lax.fori_loop(9, 15, first, 0)

    def second(x, carry):
        def store(c, rows, v):
            out_s[c, x - 8, rows, :] = v

        second_step(mid_s, coef_s, middle, x, store)
        send(out_s, out, sems_o, x - 8, x).start()
        return carry

    lax.fori_loop(8, 14, second, 0)
    for copy in started:
        copy.wait()
    edges[...] = edge_middle(hl, hr, zl, zr, corner[0], corner[1])
    first_step(adj_s, visc_s, vel_s, mid_s, coef_s, corner.at[0], -1, 15)
    first_step(adj_s, visc_s, vel_s, mid_s, coef_s, centre.at[0], 0, 0)
    first_step(adj_s, visc_s, vel_s, mid_s, coef_s, centre.at[0], 15, 15)
    first_step(adj_s, visc_s, vel_s, mid_s, coef_s, corner.at[1], 16, 0)

    @pl.when(place[0] == 0)
    def _():
        for c in range(3):
            mid_s[c, 0] = jnp.zeros((144, 128), F32)

    @pl.when(place[0] == place[1] - 1)
    def _():
        for c in range(3):
            mid_s[c, 17] = jnp.zeros((144, 128), F32)

    for i, x in ((6, 0), (7, 1), (8, 14), (9, 15)):

        def store(c, rows, v, i=i):
            out_s[c, i, rows, :] = v

        second_step(mid_s, coef_s, edges, x, store)
        send(out_s, out, sems_o, i, x).start()
    for i in range(10):
        send(out_s, out, sems_o, i, i + 8 if i < 6 else (0, 1, 14, 15)[i - 6]).wait()


def outer(place, state, mid, coef, centre, middle, hl, hr, zl, zr, low, high, out):
    held = [vmem(a) for a in (*state, mid, coef, centre, middle, hl, hr, zl, zr)]
    return pl.pallas_call(
        outer_kernel,
        in_specs=[SM] + [VM] * 11 + [ANY] * 3,
        out_specs=[VM] * 5 + [ANY],
        out_shape=[in_vmem(STATE[k]) for k in ("adj", "visc", "vel", "mid", "coef")]
        + [pltpu.HBM((3, 16, 128, 128), F32)],
        scratch_shapes=[
            pltpu.VMEM((3, 10, 128, 128), F32),
            pltpu.VMEM((2, 128, 128), F32),
            pltpu.VMEM((128, 128), F32),
            pltpu.SemaphoreType.DMA((16,)),
            pltpu.SemaphoreType.DMA((10,)),
        ],
        input_output_aliases={1: 0, 2: 1, 3: 2, 4: 3, 5: 4, 14: 5},
        compiler_params=params(6),
        name="outer",
    )(place, *held, hbm(low), hbm(high), hbm(out))[-1]


def pieces(a):
    high = a.astype(BF16)
    rest = a - high.astype(F32)
    mid = rest.astype(BF16)
    low = (rest - mid.astype(F32)).astype(BF16)
    return high, mid, low


def sums_kernel(place, places, face, more, out):
    row = lax.broadcasted_iota(jnp.int32, (128, 128), 0)
    column = lanes((128, 128))
    wanted = (row >> 2) + place[0] * 32
    count = jnp.zeros((128, 128), F32)
    for k in range(8):
        count = count + jnp.where(places[pl.ds(k, 1), :] == wanted, 1.0, 0.0)
    chosen = jnp.where((row & 3) == (column & 3), count, 0.0).astype(BF16)
    for c in range(3):
        total = 0.0
        for piece in pieces(face[c] + more[c]):
            total = total + jnp.dot(chosen, piece, preferred_element_type=F32)
        for g in range(8):
            out[g, c] = total[g * 16 : g * 16 + 16]


def partial_sums(place, places, face, more):
    return pl.pallas_call(
        sums_kernel,
        in_specs=[SM, VM, VM, VM],
        out_specs=VM,
        out_shape=jax.ShapeDtypeStruct((8, 3, 16, 128), F32),
        compiler_params=params(4),
        name="sums",
    )(place, places, face, more)


def product_kernel(parts, filters, out, sums):
    total = parts[0]
    for g in range(1, 8):
        total = total + parts[g]
    sums[...] = total
    for p in range(4):
        view = jnp.concatenate([sums[:, p * 4 + i, :] for i in range(4)], axis=1)
        stacked = jnp.concatenate(pieces(view), axis=0)
        wide = jnp.dot(stacked, filters[p], preferred_element_type=F32)
        out[p] = wide[0:3] + (wide[3:6] + wide[6:9])


def product(parts, filters):
    return pl.pallas_call(
        product_kernel,
        in_specs=[VM, VM],
        out_specs=VM,
        out_shape=jax.ShapeDtypeStruct((4, 3, 512), F32),
        scratch_shapes=[pltpu.VMEM((3, 16, 128), F32)],
        compiler_params=params(4),
        name="product",
    )(parts, filters)


def shards(adjoint, velocity, viscosity, filters, block_tiles, tile_place):
    gx = lax.axis_index("gx")
    gz = lax.axis_index("gz")
    nx = lax.axis_size("gx")
    nz = lax.axis_size("gz")
    ring = [(i, (i + 1) % nz) for i in range(nz)]
    back = [(b, a) for a, b in ring]
    along = [(i, i + 1) for i in range(nx - 1)]
    against = [(b, a) for a, b in along]
    place = jnp.stack([gx, jnp.int32(nx)]).astype(jnp.int32)

    *state, zl, zr = pack(adjoint, velocity, viscosity)
    hl = lax.ppermute(zl, "gz", ring)
    hr = lax.ppermute(zr, "gz", back)

    lists = lax.dynamic_slice_in_dim(block_tiles, gz * 32, 32, 0)
    tiles = jnp.arange(512, dtype=jnp.int32)
    places = jnp.sum(jnp.where(lists[:, :, None] == tiles, tile_place, 0), axis=2)
    places = jnp.repeat(places.T, 4, axis=1)

    face, mid, coef, centre, middle, msg_lo, msg_hi = face_call(place, state, hl, hr, zl, zr)
    got = [lax.ppermute(face, "gx", [(0, k)]) for k in (8, 2, 6)]
    low = lax.ppermute(msg_hi, "gx", along)
    high = lax.ppermute(msg_lo, "gx", against)
    face = (face + got[0]) + (got[1] + got[2])
    far = lax.ppermute(face, "gx", [(0, 4), (2, 10), (6, 14), (8, 12)])
    mid, coef, out = inner(state, centre, middle, mid, coef)
    face = face + far
    other = lax.ppermute(face, "gx", [(i, i + 1) for i in range(0, nx, 2)])
    parts = lax.all_to_all(partial_sums(place, places, face, other), "gz", 0, 0)
    out = outer(place, state, mid, coef, centre, middle, hl, hr, zl, zr, low, high, out)
    gradient = product(parts, filters)
    return out, gradient


def solution(mesh):
    placed = (
        P(None, "gx", None, "gz"),
        P(None, "gx", None, "gz"),
        P("gx", None, "gz"),
        P(("gx", "gz"), None, None),
        P(),
        P(),
    )
    return jax.shard_map(
        shards,
        mesh=mesh,
        in_specs=placed,
        out_specs=(P(None, "gx", None, "gz"), P(("gx", "gz"), None, None)),
        check_vma=False,
    )
```

```python
import functools

import jax
import jax.numpy as jnp
from jax import lax
from jax.experimental import pallas as pl
from jax.experimental.pallas import tpu as pltpu
from jax.sharding import PartitionSpec as P

F32 = jnp.float32
BF16 = jnp.bfloat16
ANY = pl.BlockSpec(memory_space=pl.ANY)
VM = pl.BlockSpec(memory_space=pltpu.VMEM)
MIB = 1024 * 1024
ROWS = 32


def lanes(shape):
    return lax.broadcasted_iota(jnp.int32, shape, len(shape) - 1)


def roll(x, shift, axis):
    if isinstance(shift, int):
        shift = shift % x.shape[axis]
    return pltpu.roll(x, shift, axis)


def in_vmem(shape):
    return pltpu.VMEM(shape, F32)


STATE = {
    "adj": (3, 20, 144, 128),
    "visc": (20, 144, 128),
    "vel": (3, 18, 128, 128),
    "mid": (3, 18, 144, 128),
    "coef": (7, 18, 128, 128),
}


def params(mib):
    return pltpu.CompilerParams(vmem_limit_bytes=mib * MIB)


def hbm(x):
    return pltpu.with_memory_space_constraint(x, pltpu.HBM)


def vmem(x):
    return pltpu.with_memory_space_constraint(x, pltpu.VMEM)


def clear_walls(ref, lead):
    for index in lead:
        ref[(*index, pl.ds(0, 8), slice(None))] = jnp.zeros((8, 128), F32)
        ref[(*index, pl.ds(136, 8), slice(None))] = jnp.zeros((8, 128), F32)


def begin(copies, sems):
    started = [pltpu.make_async_copy(s, t, sems.at[i]) for i, (s, t) in enumerate(copies)]
    for copy in started:
        copy.start()
    return started


def pack_kernel(adj, vel, visc, adj_s, visc_s, vel_s, zl, zr, acc_l, acc_r, sems):
    def copies(g):
        rows = pl.ds(g * 32, 32)
        padded = pl.ds(8 + g * 32, 32)
        return (
            (adj.at[:, :, rows], adj_s.at[:, pl.ds(2, 16), padded]),
            (visc.at[:, rows], visc_s.at[pl.ds(2, 16), padded]),
            (vel.at[:, :, rows], vel_s.at[:, pl.ds(1, 16), rows]),
        )

    started = [begin(copies(g), sems.at[g]) for g in range(4)]
    clear_walls(adj_s, [(c, q) for c in range(3) for q in range(1, 20)])
    clear_walls(visc_s, [(q,) for q in range(1, 20)])
    zero = jnp.zeros((144, 128), F32)
    visc_s[1] = zero
    for c in range(3):
        adj_s[c, 1] = zero
    lane = lanes((32, 128))
    pair = lane >> 1
    pair_l = ((lane + 2) & 127) >> 1
    for g in range(4):
        for copy in started[g]:
            copy.wait()
        rows = pl.ds(g * 32, 32)
        padded = pl.ds(8 + g * 32, 32)
        half = g // 2
        left = jnp.zeros((32, 128), F32)
        right = jnp.zeros((32, 128), F32)
        for m in range(64):
            c, x = divmod(m, 16)
            plane = adj_s[c, x + 2, padded] if c < 3 else visc_s[x + 2, padded]
            turned = roll(plane, 2 * m, 1)
            right = jnp.where(pair == m, turned, right)
            left = jnp.where(pair_l == m, turned, left)
        zr[rows] = right
        zl[rows] = roll(left, 2, 1)
        left = jnp.zeros((32, 128), F32)
        right = jnp.zeros((32, 128), F32)
        for m in range(48):
            d, x = divmod(m, 16)
            at = 2 * m + half
            turned = roll(vel_s[d, x + 1, rows], at, 1)
            right = jnp.where(lane == at, turned, right)
            left = jnp.where(lane == (at - 1) % 128, turned, left)
        acc_r[rows] = right
        acc_l[rows] = roll(left, 1, 1)
    even = (lanes((64, 128)) & 1) == 0
    zr[pl.ds(128, 64)] = jnp.where(even, acc_r[pl.ds(0, 64)], acc_r[pl.ds(64, 64)])
    zl[pl.ds(128, 64)] = jnp.where(even, acc_l[pl.ds(0, 64)], acc_l[pl.ds(64, 64)])


def pack(adj, vel, visc):
    return pl.pallas_call(
        pack_kernel,
        in_specs=[ANY, ANY, ANY],
        out_specs=[VM] * 5,
        out_shape=[in_vmem(STATE[k]) for k in ("adj", "visc", "vel")] + [in_vmem((192, 128))] * 2,
        scratch_shapes=[
            pltpu.VMEM((128, 128), F32),
            pltpu.VMEM((128, 128), F32),
            pltpu.SemaphoreType.DMA((4, 3)),
        ],
        compiler_params=params(4),
        name="pack",
    )(hbm(adj), hbm(vel), hbm(visc))


def spread(a, group):
    kept = jnp.where((lanes(a.shape) >> 5) == group, a, 0.0)
    kept = kept + roll(kept, 32, 1)
    return kept + roll(kept, 64, 1)


def shift_rows(a, by):
    row = lax.broadcasted_iota(jnp.int32, a.shape, 0)
    moved = roll(a, by, 0)
    edge = 0 if by > 0 else a.shape[0] - 1
    return jnp.where(row == edge, 0.0, moved)


def edge_centre(hl, hr):
    odd = (lanes((128, 128)) & 1) == 1
    return jnp.where(odd, hl[pl.ds(0, 128)], hr[pl.ds(0, 128)])


def edge_velocity(message):
    both = message[pl.ds(128, 64)]
    odd = (lanes(both.shape) & 1) == 1
    upper = jnp.where(odd, roll(both, 1, 1), both)
    lower = jnp.where(odd, both, roll(both, -1, 1))
    return jnp.concatenate([upper, lower], axis=0)


def edge_middle(hl, hr, zl, zr, low=None, high=None):
    lane = lanes((128, 128))
    odd = (lane & 1) == 1
    x = (lane >> 1) & 15
    first = pl.ds(0, 128)
    left, right = hl[first], hr[first]
    centre = jnp.where(odd, left, right)
    minus = jnp.where(odd, roll(left, 1, 1), roll(zl[first], -1, 1))
    plus = jnp.where(odd, roll(zr[first], 1, 1), roll(right, -1, 1))
    velocity = jnp.where(odd, edge_velocity(hl), edge_velocity(hr))
    west = roll(centre, 2, 1)
    east = roll(centre, -2, 1)
    west = jnp.where(x == 0, 0.0 if low is None else roll(low, -30, 1), west)
    east = jnp.where(x == 15, 0.0 if high is None else roll(high, 30, 1), east)
    north = shift_rows(centre, -1)
    south = shift_rows(centre, 1)
    visc = spread(centre, 3)
    total = 0.0
    result = 0.0
    for d, (up, down) in enumerate(((east, west), (north, south), (plus, minus))):
        v = spread(velocity, d)
        a_up = 0.5 * ((visc + spread(up, 3)) + v)
        a_down = 0.5 * ((visc + spread(down, 3)) - v)
        total = total + (a_up + a_down)
        result = result + (a_up * up + a_down * down)
    return result + (1.0 - total) * centre


def ends(edge, r, m):
    return roll(edge[pl.ds(r, ROWS), :], (127 - 2 * m) % 128 if isinstance(m, int) else 127 - 2 * m, 1)


def first_step(adj_s, visc_s, vel_s, mid_s, coef_s, edge, x, ex):
    lane = lanes((ROWS, 128))
    q, t = x + 2, x + 1
    for r in range(0, 128, ROWS):
        rows, here = pl.ds(r, ROWS), pl.ds(8 + r, ROWS)
        above, below = pl.ds(9 + r, ROWS), pl.ds(7 + r, ROWS)

        def sides(plane, m):
            end = ends(edge, r, m)
            up = jnp.where(lane == 127, end, roll(plane, -1, 1))
            return up, jnp.where(lane == 0, end, roll(plane, 1, 1))

        centre = visc_s[q, here, :]
        pairs = (
            (visc_s[q + 1, here, :], visc_s[q - 1, here, :]),
            (visc_s[q, above, :], visc_s[q, below, :]),
            sides(centre, 48 + ex),
        )
        a = []
        for d, (plus, minus) in enumerate(pairs):
            v = vel_s[d, t, rows, :]
            a.append(0.5 * ((centre + plus) + v))
            a.append(0.5 * ((centre + minus) - v))
        a.append(1.0 - (((a[0] + a[1]) + (a[2] + a[3])) + (a[4] + a[5])))
        for k in range(7):
            coef_s[k, t, rows, :] = a[k]
        for c in range(3):
            centre = adj_s[c, q, here, :]
            up, down = sides(centre, c * 16 + ex)
            out = a[6] * centre
            out = out + a[0] * adj_s[c, q + 1, here, :]
            out = out + a[1] * adj_s[c, q - 1, here, :]
            out = out + a[2] * adj_s[c, q, above, :]
            out = out + a[3] * adj_s[c, q, below, :]
            out = out + a[4] * up
            mid_s[c, t, here, :] = out + a[5] * down
    for c in range(3):
        mid_s[c, t, pl.ds(0, 8), :] = jnp.zeros((8, 128), F32)
        mid_s[c, t, pl.ds(136, 8), :] = jnp.zeros((8, 128), F32)


def second_step(mid_s, coef_s, edge, x, store):
    lane = lanes((ROWS, 128))
    t = x + 1
    for r in range(0, 128, ROWS):
        rows, here = pl.ds(r, ROWS), pl.ds(8 + r, ROWS)
        above, below = pl.ds(9 + r, ROWS), pl.ds(7 + r, ROWS)
        a = [coef_s[k, t, rows, :] for k in range(7)]
        for c in range(3):
            centre = mid_s[c, t, here, :]
            end = ends(edge, r, c * 16 + x)
            out = a[6] * centre
            out = out + a[0] * mid_s[c, t + 1, here, :]
            out = out + a[1] * mid_s[c, t - 1, here, :]
            out = out + a[2] * mid_s[c, t, above, :]
            out = out + a[3] * mid_s[c, t, below, :]
            out = out + a[4] * jnp.where(lane == 127, end, roll(centre, -1, 1))
            store(c, rows, out + a[5] * jnp.where(lane == 0, end, roll(centre, 1, 1)))


def face_kernel(
    adj_s, visc_s, vel_s, hl, hr, zl, zr, face, mid_s, coef_s, centre, middle
):
    centre[0] = edge_centre(hl, hr)
    middle[...] = edge_middle(hl, hr, zl, zr)
    for c in range(3):
        mid_s[c, 0] = jnp.zeros((144, 128), F32)
    for x in range(2):
        first_step(adj_s, visc_s, vel_s, mid_s, coef_s, centre.at[0], x, x)
    own = jnp.where(lax.axis_index("gx") == 0, 1.0, 0.0)

    def store(c, rows, v):
        face[c, rows, :] = v * own

    second_step(mid_s, coef_s, middle, 0, store)


def face_call(state, hl, hr, zl, zr):
    return pl.pallas_call(
        face_kernel,
        in_specs=[VM] * 7,
        out_specs=[VM] * 5,
        out_shape=[
            in_vmem((3, 128, 128)),
            in_vmem(STATE["mid"]),
            in_vmem(STATE["coef"]),
            in_vmem((1, 128, 128)),
            in_vmem((128, 128)),
        ],
        compiler_params=params(4),
        name="face",
    )(*[vmem(a) for a in (*state, hl, hr, zl, zr)])


def send(out_s, out, sems, i, x):
    return pltpu.make_async_copy(out_s.at[:, pl.ds(i, 1)], out.at[:, pl.ds(x, 1)], sems.at[i])


def choose(lists, place):
    gx, gz = lax.axis_index("gx"), lax.axis_index("gz")
    half = lists[:, pl.ds(pl.multiple_of((gz // 4) * 128, 128), 128)]
    tile = lax.broadcasted_iota(jnp.int32, (512, 128), 0)
    listed = jnp.zeros((512, 128), F32)
    for k in range(8):
        listed = listed + jnp.where(half[k : k + 1] == tile, 1.0, 0.0)
    row = lax.broadcasted_iota(jnp.int32, (128, 512), 0)
    wanted = gx * 32 + ((row >> 4) ^ gz) * 4 + ((row >> 2) & 3)
    sits = jnp.where(place[...] == wanted, 1.0, 0.0).astype(BF16)
    count = jnp.dot(sits, listed.astype(BF16), preferred_element_type=F32)
    row = lax.broadcasted_iota(jnp.int32, (128, 128), 0)
    column = lanes((128, 128))
    ours = jnp.where(row == (gz % 4) * 32 + (column >> 2), 1.0, 0.0).astype(BF16)
    wide = jnp.dot(count.astype(BF16), ours, preferred_element_type=F32)
    return jnp.where((row & 3) == (column & 3), wide, 0.0)


def inner_kernel(
    adj_s, visc_s, vel_s, centre, middle, lists, place, _, __,
    mid_s, coef_s, out, chosen, msg_lo, msg_hi, out_s, sems, sems_x,
):
    moved = []
    for msg, q, t in ((msg_lo, 2, 1), (msg_hi, 16, 16)):
        inside = pl.ds(8, 128)
        for c in range(3):
            moved.append((adj_s.at[c, pl.ds(q, 2), inside], msg.at[pl.ds(2 * c, 2)]))
            moved.append((vel_s.at[c, pl.ds(t, 1)], msg.at[pl.ds(6 + c, 1)]))
        moved.append((visc_s.at[pl.ds(q, 2), inside], msg.at[pl.ds(9, 2)]))
    moved += [(centre, msg_lo.at[pl.ds(11, 1)]), (centre, msg_hi.at[pl.ds(11, 1)])]
    moved = begin(moved, sems_x)

    def first(x, carry):
        first_step(adj_s, visc_s, vel_s, mid_s, coef_s, centre.at[0], x, x)
        return carry

    lax.fori_loop(2, 9, first, 0)

    def second(x, carry):
        def store(c, rows, v):
            out_s[c, x - 2, rows, :] = v

        second_step(mid_s, coef_s, middle, x, store)
        send(out_s, out, sems, x - 2, x).start()
        return carry

    lax.fori_loop(2, 8, second, 0)
    chosen[...] = choose(lists, place)
    for copy in moved:
        copy.wait()
    for i in range(6):
        send(out_s, out, sems, i, i + 2).wait()


FIELD = (3, 16, 128, 128)


def inner(state, centre, middle, lists, place, mid, coef):
    msg = pltpu.HBM((12, 128, 128), F32)
    return pl.pallas_call(
        inner_kernel,
        in_specs=[VM] * 9,
        out_specs=[VM, VM, ANY, VM, ANY, ANY],
        out_shape=[
            in_vmem(STATE["mid"]),
            in_vmem(STATE["coef"]),
            pltpu.HBM(FIELD, F32),
            in_vmem((128, 128)),
            msg,
            msg,
        ],
        scratch_shapes=[
            pltpu.VMEM((3, 6, 128, 128), F32),
            pltpu.SemaphoreType.DMA((6,)),
            pltpu.SemaphoreType.DMA((16,)),
        ],
        input_output_aliases={7: 0, 8: 1},
        compiler_params=params(5),
        name="inner",
    )(*[vmem(a) for a in (*state, centre, middle)], lists, place, vmem(mid), vmem(coef))


def middle_kernel(adj_s, visc_s, vel_s, centre, middle, _, __, ___, mid_s, coef_s, out, out_s, sems):
    def first(x, carry):
        first_step(adj_s, visc_s, vel_s, mid_s, coef_s, centre.at[0], x, x)
        return carry

    lax.fori_loop(9, 15, first, 0)

    def second(x, carry):
        def store(c, rows, v):
            out_s[c, x - 8, rows, :] = v

        second_step(mid_s, coef_s, middle, x, store)
        send(out_s, out, sems, x - 8, x).start()
        return carry

    lax.fori_loop(8, 14, second, 0)
    for i in range(6):
        send(out_s, out, sems, i, i + 8).wait()


def middle_call(state, centre, middle, mid, coef, out):
    return pl.pallas_call(
        middle_kernel,
        in_specs=[VM] * 7 + [ANY],
        out_specs=[VM, VM, ANY],
        out_shape=[in_vmem(STATE["mid"]), in_vmem(STATE["coef"]), pltpu.HBM(FIELD, F32)],
        scratch_shapes=[pltpu.VMEM((3, 6, 128, 128), F32), pltpu.SemaphoreType.DMA((6,))],
        input_output_aliases={5: 0, 6: 1, 7: 2},
        compiler_params=params(4),
        name="middle",
    )(*[vmem(a) for a in (*state, centre, middle, mid, coef)], hbm(out))


def outer_kernel(
    adj_i, visc_i, vel_i, mid_i, coef_i, centre, hl, hr, zl, zr, low, high, filters, _,
    adj_s, visc_s, vel_s, mid_s, coef_s, out, kept, out_s, corner, edges, sems, sems_o, sem_f,
):
    inside = pl.ds(8, 128)
    pairs = [(low.at[pl.ds(11, 1)], corner.at[pl.ds(0, 1)])]
    pairs += [(high.at[pl.ds(11, 1)], corner.at[pl.ds(1, 1)])]
    for msg, q, t in ((low, 0, 0), (high, 18, 17)):
        for c in range(3):
            pairs.append((msg.at[pl.ds(2 * c, 2)], adj_s.at[c, pl.ds(q, 2), inside]))
            pairs.append((msg.at[pl.ds(6 + c, 1)], vel_s.at[c, pl.ds(t, 1)]))
        pairs.append((msg.at[pl.ds(9, 2)], visc_s.at[pl.ds(q, 2), inside]))
    started = begin(pairs, sems)
    fetched = begin([(filters, kept)], sem_f)
    for copy in started:
        copy.wait()
    edges[...] = edge_middle(hl, hr, zl, zr, corner[0], corner[1])
    first_step(adj_s, visc_s, vel_s, mid_s, coef_s, corner.at[0], -1, 15)
    first_step(adj_s, visc_s, vel_s, mid_s, coef_s, centre.at[0], 0, 0)
    first_step(adj_s, visc_s, vel_s, mid_s, coef_s, centre.at[0], 15, 15)
    first_step(adj_s, visc_s, vel_s, mid_s, coef_s, corner.at[1], 16, 0)
    gx = lax.axis_index("gx")

    @pl.when(gx == 0)
    def _():
        for c in range(3):
            mid_s[c, 0] = jnp.zeros((144, 128), F32)

    @pl.when(gx == lax.axis_size("gx") - 1)
    def _():
        for c in range(3):
            mid_s[c, 17] = jnp.zeros((144, 128), F32)

    for i, x in enumerate((0, 1, 14, 15)):

        def store(c, rows, v, i=i):
            out_s[c, i, rows, :] = v

        second_step(mid_s, coef_s, edges, x, store)
        send(out_s, out, sems_o, i, x).start()
    for i, x in enumerate((0, 1, 14, 15)):
        send(out_s, out, sems_o, i, x).wait()
    for copy in fetched:
        copy.wait()


def outer(state, mid, coef, centre, hl, hr, zl, zr, low, high, filters, out):
    held = [vmem(a) for a in (*state, mid, coef, centre, hl, hr, zl, zr)]
    done = pl.pallas_call(
        outer_kernel,
        in_specs=[VM] * 10 + [ANY] * 4,
        out_specs=[VM] * 5 + [ANY, VM],
        out_shape=[in_vmem(STATE[k]) for k in ("adj", "visc", "vel", "mid", "coef")]
        + [pltpu.HBM(FIELD, F32), pltpu.VMEM(filters.shape, BF16)],
        scratch_shapes=[
            pltpu.VMEM((3, 4, 128, 128), F32),
            pltpu.VMEM((2, 128, 128), F32),
            pltpu.VMEM((128, 128), F32),
            pltpu.SemaphoreType.DMA((16,)),
            pltpu.SemaphoreType.DMA((4,)),
            pltpu.SemaphoreType.DMA((1,)),
        ],
        input_output_aliases={0: 0, 1: 1, 2: 2, 3: 3, 4: 4, 13: 5},
        compiler_params=params(4),
        name="outer",
    )(*held, low, high, hbm(filters), hbm(out))
    return done[5], done[6]


def join_kernel(*refs):
    total = refs[0][...]
    for ref in refs[1:-1]:
        total = total + ref[...]
    refs[-1][...] = total


def join(*parts):
    return pl.pallas_call(
        join_kernel,
        in_specs=[VM] * len(parts),
        out_specs=VM,
        out_shape=in_vmem(parts[0].shape),
        compiler_params=params(2),
        name="join",
    )(*[vmem(a) for a in parts])


def pieces(a):
    high = a.astype(BF16)
    rest = a - high.astype(F32)
    mid = rest.astype(BF16)
    low = (rest - mid.astype(F32)).astype(BF16)
    return high, mid, low


PART = (3, 16, 128)


def sums_kernel(chosen, face, more, kept, given):
    matrix = chosen[...].astype(BF16)
    for c in range(3):
        total = 0.0
        for piece in pieces(face[c] + more[c]):
            total = total + jnp.dot(matrix, piece, preferred_element_type=F32)
        for k in range(8):
            (given if k % 2 else kept)[k // 2, c] = total[k * 16 : k * 16 + 16]


def partial_sums(chosen, face, more):
    return pl.pallas_call(
        sums_kernel,
        in_specs=[VM] * 3,
        out_specs=[VM, VM],
        out_shape=[in_vmem((4, *PART))] * 2,
        compiler_params=params(2),
        name="sums",
    )(vmem(chosen), vmem(face), vmem(more))


def halve_kernel(kept, came, still, given):
    for k in range(kept.shape[0]):
        (given if k % 2 else still)[k // 2] = kept[k] + came[k]


def halve(kept, came):
    return pl.pallas_call(
        halve_kernel,
        in_specs=[VM] * 2,
        out_specs=[VM, VM],
        out_shape=[in_vmem((kept.shape[0] // 2, *PART))] * 2,
        compiler_params=params(2),
        name="halve",
    )(vmem(kept), vmem(came))


def product_kernel(kept, came, filters, out, sums):
    sums[...] = kept[0] + came[0]
    for p in range(4):
        view = jnp.concatenate([sums[:, p * 4 + i, :] for i in range(4)], axis=1)
        stacked = jnp.concatenate(pieces(view), axis=0)
        wide = jnp.dot(stacked, filters[p], preferred_element_type=F32)
        out[:, p, :] = wide[0:3] + (wide[3:6] + wide[6:9])


def product(kept, came, filters):
    return pl.pallas_call(
        product_kernel,
        in_specs=[VM] * 3,
        out_specs=VM,
        out_shape=jax.ShapeDtypeStruct((3, 4, 512), F32),
        scratch_shapes=[pltpu.VMEM(PART, F32)],
        compiler_params=params(4),
        name="product",
    )(vmem(kept), vmem(came), vmem(filters))


def shards(adjoint, velocity, viscosity, filters, block_tiles, tile_place):
    nx = lax.axis_size("gx")
    nz = lax.axis_size("gz")
    ring = [(i, (i + 1) % nz) for i in range(nz)]
    back = [(b, a) for a, b in ring]
    along = [(i, i + 1) for i in range(nx - 1)]
    against = [(b, a) for a, b in along]

    *state, zl, zr = pack(adjoint, velocity, viscosity)
    hl = lax.ppermute(zl, "gz", ring)
    hr = lax.ppermute(zr, "gz", back)
    face, mid, coef, centre, middle = face_call(state, hl, hr, zl, zr)

    got = [lax.ppermute(face, "gx", [(0, k)]) for k in (8, 2, 6)]
    mid, coef, out, chosen, msg_lo, msg_hi = inner(
        state, centre, middle, block_tiles.T, tile_place.reshape(1, -1), mid, coef
    )
    *got, mid, coef, out, chosen = lax.optimization_barrier((*got, mid, coef, out, chosen))
    face = join(face, *got)
    far = lax.ppermute(face, "gx", [(0, 4), (2, 10), (6, 14), (8, 12)])
    low = lax.ppermute(msg_hi, "gx", along)
    high = lax.ppermute(msg_lo, "gx", against)
    face = join(face, far)
    other = lax.ppermute(face, "gx", [(i, i + 1) for i in range(0, nx, 2)])
    kept, given = partial_sums(chosen, face, other)

    came = lax.ppermute(given, "gz", [(i, i ^ 1) for i in range(nz)])
    mid, coef, out = middle_call(state, centre, middle, mid, coef, out)
    came, mid, coef, out = lax.optimization_barrier((came, mid, coef, out))
    kept, given = halve(kept, came)
    came = lax.ppermute(given, "gz", [(i, i ^ 2) for i in range(nz)])
    out, near = outer(state, mid, coef, centre, hl, hr, zl, zr, low, high, filters, out)
    came, out = lax.optimization_barrier((came, out))
    kept, given = halve(kept, came)
    came = lax.ppermute(given, "gz", [(i, i ^ 4) for i in range(nz)])
    gradient = product(kept, came, near).transpose(1, 0, 2)
    return out, gradient


def solution(mesh):
    placed = (
        P(None, "gx", None, "gz"),
        P(None, "gx", None, "gz"),
        P("gx", None, "gz"),
        P(("gx", "gz"), None, None),
        P(),
        P(),
    )
    return jax.shard_map(
        shards,
        mesh=mesh,
        in_specs=placed,
        out_specs=(P(None, "gx", None, "gz"), P(("gx", "gz"), None, None)),
        check_vma=False,
    )
```

```python
import functools

import functools

import jax
import jax.numpy as jnp
from jax import lax
from jax.experimental import pallas as pl
from jax.experimental.pallas import tpu as pltpu
from jax.sharding import PartitionSpec as P

F32 = jnp.float32
BF16 = jnp.bfloat16
ANY = pl.BlockSpec(memory_space=pl.ANY)
VM = pl.BlockSpec(memory_space=pltpu.VMEM)
MIB = 1024 * 1024
ROWS = 32


def lanes(shape):
    return lax.broadcasted_iota(jnp.int32, shape, len(shape) - 1)


def roll(x, shift, axis):
    if isinstance(shift, int):
        shift = shift % x.shape[axis]
    return pltpu.roll(x, shift, axis)


def in_vmem(shape):
    return pltpu.VMEM(shape, F32)


STATE = {
    "adj": (3, 20, 144, 128),
    "visc": (20, 144, 128),
    "vel": (3, 18, 128, 128),
    "mid": (3, 18, 144, 128),
    "coef": (7, 18, 128, 128),
}


def cost(planes):
    return pl.CostEstimate(flops=planes * 3 * 16384 * 20, transcendentals=0, bytes_accessed=planes * 16384 * 4 * 22)


def params(mib):
    return pltpu.CompilerParams(vmem_limit_bytes=mib * MIB)


def hbm(x):
    return pltpu.with_memory_space_constraint(x, pltpu.HBM)


def vmem(x):
    return pltpu.with_memory_space_constraint(x, pltpu.VMEM)


def clear_walls(ref, lead):
    for index in lead:
        ref[(*index, pl.ds(0, 8), slice(None))] = jnp.zeros((8, 128), F32)
        ref[(*index, pl.ds(136, 8), slice(None))] = jnp.zeros((8, 128), F32)


def begin(copies, sems):
    started = [pltpu.make_async_copy(s, t, sems.at[i]) for i, (s, t) in enumerate(copies)]
    for copy in started:
        copy.start()
    return started


def pack_kernel(adj, vel, visc, adj_s, visc_s, vel_s, zl, zr, acc_l, acc_r, sems):
    def copies(g):
        rows = pl.ds(g * 32, 32)
        padded = pl.ds(8 + g * 32, 32)
        return (
            (adj.at[:, :, rows], adj_s.at[:, pl.ds(2, 16), padded]),
            (visc.at[:, rows], visc_s.at[pl.ds(2, 16), padded]),
            (vel.at[:, :, rows], vel_s.at[:, pl.ds(1, 16), rows]),
        )

    started = [begin(copies(g), sems.at[g]) for g in range(4)]
    clear_walls(adj_s, [(c, q) for c in range(3) for q in range(1, 20)])
    clear_walls(visc_s, [(q,) for q in range(1, 20)])
    zero = jnp.zeros((144, 128), F32)
    visc_s[1] = zero
    for c in range(3):
        adj_s[c, 1] = zero
    lane = lanes((32, 128))
    pair = lane >> 1
    pair_l = ((lane + 2) & 127) >> 1
    for g in range(4):
        for copy in started[g]:
            copy.wait()
        rows = pl.ds(g * 32, 32)
        padded = pl.ds(8 + g * 32, 32)
        half = g // 2
        left = jnp.zeros((32, 128), F32)
        right = jnp.zeros((32, 128), F32)
        for m in range(64):
            c, x = divmod(m, 16)
            plane = adj_s[c, x + 2, padded] if c < 3 else visc_s[x + 2, padded]
            turned = roll(plane, 2 * m, 1)
            right = jnp.where(pair == m, turned, right)
            left = jnp.where(pair_l == m, turned, left)
        zr[rows] = right
        zl[rows] = roll(left, 2, 1)
        left = jnp.zeros((32, 128), F32)
        right = jnp.zeros((32, 128), F32)
        for m in range(48):
            d, x = divmod(m, 16)
            at = 2 * m + half
            turned = roll(vel_s[d, x + 1, rows], at, 1)
            right = jnp.where(lane == at, turned, right)
            left = jnp.where(lane == (at - 1) % 128, turned, left)
        acc_r[rows] = right
        acc_l[rows] = roll(left, 1, 1)
    even = (lanes((64, 128)) & 1) == 0
    zr[pl.ds(128, 64)] = jnp.where(even, acc_r[pl.ds(0, 64)], acc_r[pl.ds(64, 64)])
    zl[pl.ds(128, 64)] = jnp.where(even, acc_l[pl.ds(0, 64)], acc_l[pl.ds(64, 64)])


def pack(adj, vel, visc):
    return pl.pallas_call(
        pack_kernel,
        in_specs=[ANY, ANY, ANY],
        out_specs=[VM] * 5,
        out_shape=[in_vmem(STATE[k]) for k in ("adj", "visc", "vel")] + [in_vmem((192, 128))] * 2,
        scratch_shapes=[
            pltpu.VMEM((128, 128), F32),
            pltpu.VMEM((128, 128), F32),
            pltpu.SemaphoreType.DMA((4, 3)),
        ],
        compiler_params=params(4),
        name="pack",
    )(hbm(adj), hbm(vel), hbm(visc))


def spread(a, group):
    kept = jnp.where((lanes(a.shape) >> 5) == group, a, 0.0)
    kept = kept + roll(kept, 32, 1)
    return kept + roll(kept, 64, 1)


def shift_rows(a, by):
    row = lax.broadcasted_iota(jnp.int32, a.shape, 0)
    moved = roll(a, by, 0)
    edge = 0 if by > 0 else a.shape[0] - 1
    return jnp.where(row == edge, 0.0, moved)


def edge_centre(hl, hr):
    odd = (lanes((128, 128)) & 1) == 1
    return jnp.where(odd, hl[pl.ds(0, 128)], hr[pl.ds(0, 128)])


def edge_velocity(message):
    both = message[pl.ds(128, 64)]
    odd = (lanes(both.shape) & 1) == 1
    upper = jnp.where(odd, roll(both, 1, 1), both)
    lower = jnp.where(odd, both, roll(both, -1, 1))
    return jnp.concatenate([upper, lower], axis=0)


def edge_middle(hl, hr, zl, zr, low=None, high=None):
    lane = lanes((128, 128))
    odd = (lane & 1) == 1
    x = (lane >> 1) & 15
    first = pl.ds(0, 128)
    left, right = hl[first], hr[first]
    centre = jnp.where(odd, left, right)
    minus = jnp.where(odd, roll(left, 1, 1), roll(zl[first], -1, 1))
    plus = jnp.where(odd, roll(zr[first], 1, 1), roll(right, -1, 1))
    velocity = jnp.where(odd, edge_velocity(hl), edge_velocity(hr))
    west = roll(centre, 2, 1)
    east = roll(centre, -2, 1)
    west = jnp.where(x == 0, 0.0 if low is None else roll(low, -30, 1), west)
    east = jnp.where(x == 15, 0.0 if high is None else roll(high, 30, 1), east)
    north = shift_rows(centre, -1)
    south = shift_rows(centre, 1)
    visc = spread(centre, 3)
    total = 0.0
    result = 0.0
    for d, (up, down) in enumerate(((east, west), (north, south), (plus, minus))):
        v = spread(velocity, d)
        a_up = 0.5 * ((visc + spread(up, 3)) + v)
        a_down = 0.5 * ((visc + spread(down, 3)) - v)
        total = total + (a_up + a_down)
        result = result + (a_up * up + a_down * down)
    return result + (1.0 - total) * centre


def ends(edge, r, m):
    return roll(edge[pl.ds(r, ROWS), :], (127 - 2 * m) % 128 if isinstance(m, int) else 127 - 2 * m, 1)


def first_step(adj_s, visc_s, vel_s, mid_s, coef_s, edge, x, ex):
    lane = lanes((ROWS, 128))
    q, t = x + 2, x + 1
    for r in range(0, 128, ROWS):
        rows, here = pl.ds(r, ROWS), pl.ds(8 + r, ROWS)
        above, below = pl.ds(9 + r, ROWS), pl.ds(7 + r, ROWS)

        def sides(plane, m):
            end = ends(edge, r, m)
            up = jnp.where(lane == 127, end, roll(plane, -1, 1))
            return up, jnp.where(lane == 0, end, roll(plane, 1, 1))

        centre = visc_s[q, here, :]
        pairs = (
            (visc_s[q + 1, here, :], visc_s[q - 1, here, :]),
            (visc_s[q, above, :], visc_s[q, below, :]),
            sides(centre, 48 + ex),
        )
        a = []
        for d, (plus, minus) in enumerate(pairs):
            v = vel_s[d, t, rows, :]
            a.append(0.5 * ((centre + plus) + v))
            a.append(0.5 * ((centre + minus) - v))
        a.append(1.0 - (((a[0] + a[1]) + (a[2] + a[3])) + (a[4] + a[5])))
        for k in range(7):
            coef_s[k, t, rows, :] = a[k]
        for c in range(3):
            centre = adj_s[c, q, here, :]
            up, down = sides(centre, c * 16 + ex)
            out = a[6] * centre
            out = out + a[0] * adj_s[c, q + 1, here, :]
            out = out + a[1] * adj_s[c, q - 1, here, :]
            out = out + a[2] * adj_s[c, q, above, :]
            out = out + a[3] * adj_s[c, q, below, :]
            out = out + a[4] * up
            mid_s[c, t, here, :] = out + a[5] * down
    for c in range(3):
        mid_s[c, t, pl.ds(0, 8), :] = jnp.zeros((8, 128), F32)
        mid_s[c, t, pl.ds(136, 8), :] = jnp.zeros((8, 128), F32)


def second_step(mid_s, coef_s, edge, x, store):
    lane = lanes((ROWS, 128))
    t = x + 1
    for r in range(0, 128, ROWS):
        rows, here = pl.ds(r, ROWS), pl.ds(8 + r, ROWS)
        above, below = pl.ds(9 + r, ROWS), pl.ds(7 + r, ROWS)
        a = [coef_s[k, t, rows, :] for k in range(7)]
        for c in range(3):
            centre = mid_s[c, t, here, :]
            end = ends(edge, r, c * 16 + x)
            out = a[6] * centre
            out = out + a[0] * mid_s[c, t + 1, here, :]
            out = out + a[1] * mid_s[c, t - 1, here, :]
            out = out + a[2] * mid_s[c, t, above, :]
            out = out + a[3] * mid_s[c, t, below, :]
            out = out + a[4] * jnp.where(lane == 127, end, roll(centre, -1, 1))
            store(c, rows, out + a[5] * jnp.where(lane == 0, end, roll(centre, 1, 1)))


def face_kernel(
    adj_s, visc_s, vel_s, hl, hr, zl, zr, face, mid_s, coef_s, centre, middle
):
    centre[0] = edge_centre(hl, hr)
    middle[...] = edge_middle(hl, hr, zl, zr)
    for c in range(3):
        mid_s[c, 0] = jnp.zeros((144, 128), F32)
    for x in range(2):
        first_step(adj_s, visc_s, vel_s, mid_s, coef_s, centre.at[0], x, x)
    own = jnp.where(lax.axis_index("gx") == 0, 1.0, 0.0)

    def store(c, rows, v):
        face[c, rows, :] = v * own

    second_step(mid_s, coef_s, middle, 0, store)


def face_call(state, hl, hr, zl, zr):
    return pl.pallas_call(
        face_kernel,
        in_specs=[VM] * 7,
        out_specs=[VM] * 5,
        out_shape=[
            in_vmem((3, 128, 128)),
            in_vmem(STATE["mid"]),
            in_vmem(STATE["coef"]),
            in_vmem((1, 128, 128)),
            in_vmem((128, 128)),
        ],
        compiler_params=params(4),
        cost_estimate=cost(3),
        name="face",
    )(*[vmem(a) for a in (*state, hl, hr, zl, zr)])


def send(out_s, out, sems, i, x):
    return pltpu.make_async_copy(out_s.at[:, pl.ds(i, 1)], out.at[:, pl.ds(x, 1)], sems.at[i])


def choose(lists, place):
    gx, gz = lax.axis_index("gx"), lax.axis_index("gz")
    half = lists[:, pl.ds(pl.multiple_of((gz // 4) * 128, 128), 128)]
    tile = lax.broadcasted_iota(jnp.int32, (512, 128), 0)
    listed = jnp.zeros((512, 128), F32)
    for k in range(8):
        listed = listed + jnp.where(half[k : k + 1] == tile, 1.0, 0.0)
    row = lax.broadcasted_iota(jnp.int32, (128, 512), 0)
    wanted = gx * 32 + ((row >> 4) ^ gz) * 4 + ((row >> 2) & 3)
    sits = jnp.where(place[...] == wanted, 1.0, 0.0).astype(BF16)
    count = jnp.dot(sits, listed.astype(BF16), preferred_element_type=F32)
    row = lax.broadcasted_iota(jnp.int32, (128, 128), 0)
    column = lanes((128, 128))
    ours = jnp.where(row == (gz % 4) * 32 + (column >> 2), 1.0, 0.0).astype(BF16)
    wide = jnp.dot(count.astype(BF16), ours, preferred_element_type=F32)
    return jnp.where((row & 3) == (column & 3), wide, 0.0)


def inner_kernel(
    adj_s, visc_s, vel_s, centre, middle, lists, place, _, __,
    mid_s, coef_s, out, chosen, msg_lo, msg_hi, out_s, sems, sems_x,
):
    moved = []
    for msg, q, t in ((msg_lo, 2, 1), (msg_hi, 16, 16)):
        inside = pl.ds(8, 128)
        for c in range(3):
            moved.append((adj_s.at[c, pl.ds(q, 2), inside], msg.at[pl.ds(2 * c, 2)]))
            moved.append((vel_s.at[c, pl.ds(t, 1)], msg.at[pl.ds(6 + c, 1)]))
        moved.append((visc_s.at[pl.ds(q, 2), inside], msg.at[pl.ds(9, 2)]))
    moved += [(centre, msg_lo.at[pl.ds(11, 1)]), (centre, msg_hi.at[pl.ds(11, 1)])]
    moved = begin(moved, sems_x)

    def first(x, carry):
        first_step(adj_s, visc_s, vel_s, mid_s, coef_s, centre.at[0], x, x)
        return carry

    lax.fori_loop(2, 9, first, 0)

    def second(x, carry):
        def store(c, rows, v):
            out_s[c, x - 2, rows, :] = v

        second_step(mid_s, coef_s, middle, x, store)
        send(out_s, out, sems, x - 2, x).start()
        return carry

    lax.fori_loop(2, 8, second, 0)
    chosen[...] = choose(lists, place)
    for copy in moved:
        copy.wait()
    for i in range(6):
        send(out_s, out, sems, i, i + 2).wait()


FIELD = (3, 16, 128, 128)


def inner(state, centre, middle, lists, place, mid, coef):
    msg = pltpu.HBM((12, 128, 128), F32)
    return pl.pallas_call(
        inner_kernel,
        in_specs=[VM] * 9,
        out_specs=[VM, VM, ANY, VM, ANY, ANY],
        out_shape=[
            in_vmem(STATE["mid"]),
            in_vmem(STATE["coef"]),
            pltpu.HBM(FIELD, F32),
            in_vmem((128, 128)),
            msg,
            msg,
        ],
        scratch_shapes=[
            pltpu.VMEM((3, 6, 128, 128), F32),
            pltpu.SemaphoreType.DMA((6,)),
            pltpu.SemaphoreType.DMA((16,)),
        ],
        input_output_aliases={7: 0, 8: 1},
        compiler_params=params(5),
        cost_estimate=cost(13),
        name="inner",
    )(*[vmem(a) for a in (*state, centre, middle)], lists, place, vmem(mid), vmem(coef))


def middle_kernel(adj_s, visc_s, vel_s, centre, middle, _, __, ___, mid_s, coef_s, out, out_s, sems):
    def first(x, carry):
        first_step(adj_s, visc_s, vel_s, mid_s, coef_s, centre.at[0], x, x)
        return carry

    lax.fori_loop(9, 15, first, 0)

    def second(x, carry):
        def store(c, rows, v):
            out_s[c, x - 8, rows, :] = v

        second_step(mid_s, coef_s, middle, x, store)
        send(out_s, out, sems, x - 8, x).start()
        return carry

    lax.fori_loop(8, 14, second, 0)
    for i in range(6):
        send(out_s, out, sems, i, i + 8).wait()


def middle_call(state, centre, middle, mid, coef, out):
    return pl.pallas_call(
        middle_kernel,
        in_specs=[VM] * 7 + [ANY],
        out_specs=[VM, VM, ANY],
        out_shape=[in_vmem(STATE["mid"]), in_vmem(STATE["coef"]), pltpu.HBM(FIELD, F32)],
        scratch_shapes=[pltpu.VMEM((3, 6, 128, 128), F32), pltpu.SemaphoreType.DMA((6,))],
        input_output_aliases={5: 0, 6: 1, 7: 2},
        compiler_params=params(4),
        cost_estimate=cost(12),
        name="middle",
    )(*[vmem(a) for a in (*state, centre, middle, mid, coef)], hbm(out))


def side_kernel(
    high, adj_i, visc_i, vel_i, mid_i, coef_i, centre, hl, hr, zl, zr, message, filters, _,
    adj_s, visc_s, vel_s, mid_s, coef_s, out, kept, out_s, corner, edges, sems, sems_o, sem_f,
):
    inside = pl.ds(8, 128)
    q, t = (18, 17) if high else (0, 0)
    pairs = [(message.at[pl.ds(11, 1)], corner)]
    for c in range(3):
        pairs.append((message.at[pl.ds(2 * c, 2)], adj_s.at[c, pl.ds(q, 2), inside]))
        pairs.append((message.at[pl.ds(6 + c, 1)], vel_s.at[c, pl.ds(t, 1)]))
    pairs.append((message.at[pl.ds(9, 2)], visc_s.at[pl.ds(q, 2), inside]))
    started = begin(pairs, sems)
    fetched = [] if high else begin([(filters, kept)], sem_f)
    started[0].wait()
    beside = (None, corner[0]) if high else (corner[0], None)
    edges[...] = edge_middle(hl, hr, zl, zr, *beside)
    for copy in started[1:]:
        copy.wait()
    if high:
        first_step(adj_s, visc_s, vel_s, mid_s, coef_s, centre.at[0], 15, 15)
        first_step(adj_s, visc_s, vel_s, mid_s, coef_s, corner.at[0], 16, 0)
    else:
        first_step(adj_s, visc_s, vel_s, mid_s, coef_s, centre.at[0], 0, 0)
        first_step(adj_s, visc_s, vel_s, mid_s, coef_s, corner.at[0], -1, 15)

    @pl.when(lax.axis_index("gx") == (lax.axis_size("gx") - 1 if high else 0))
    def _():
        for c in range(3):
            mid_s[c, t] = jnp.zeros((144, 128), F32)

    cells = (14, 15) if high else (1, 0)
    for i, x in enumerate(cells):

        def store(c, rows, v, i=i):
            out_s[c, i, rows, :] = v

        second_step(mid_s, coef_s, edges, x, store)
        send(out_s, out, sems_o, i, x).start()
    for i, x in enumerate(cells):
        send(out_s, out, sems_o, i, x).wait()
    for copy in fetched:
        copy.wait()


def side_call(high, state, mid, coef, centre, hl, hr, zl, zr, message, filters, out):
    held = [vmem(a) for a in (*state, mid, coef, centre, hl, hr, zl, zr)]
    done = pl.pallas_call(
        functools.partial(side_kernel, high),
        in_specs=[VM] * 10 + [ANY] * 3,
        out_specs=[VM] * 5 + [ANY, VM],
        out_shape=[in_vmem(STATE[k]) for k in ("adj", "visc", "vel", "mid", "coef")]
        + [pltpu.HBM(FIELD, F32), pltpu.VMEM((8, 128) if high else filters.shape, BF16)],
        scratch_shapes=[
            pltpu.VMEM((3, 2, 128, 128), F32),
            pltpu.VMEM((1, 128, 128), F32),
            pltpu.VMEM((128, 128), F32),
            pltpu.SemaphoreType.DMA((8,)),
            pltpu.SemaphoreType.DMA((2,)),
            pltpu.SemaphoreType.DMA((1,)),
        ],
        input_output_aliases={0: 0, 1: 1, 2: 2, 3: 3, 4: 4, 12: 5},
        compiler_params=params(4),
        cost_estimate=cost(4),
        name="side",
    )(*held, message, hbm(filters), hbm(out))
    return done[:3], done[3], done[4], done[5], done[6]


def join_kernel(*refs):
    total = refs[0][...]
    for ref in refs[1:-1]:
        total = total + ref[...]
    refs[-1][...] = total


def join(*parts):
    return pl.pallas_call(
        join_kernel,
        in_specs=[VM] * len(parts),
        out_specs=VM,
        out_shape=in_vmem(parts[0].shape),
        compiler_params=params(2),
        name="join",
    )(*[vmem(a) for a in parts])


def pieces(a):
    high = a.astype(BF16)
    rest = a - high.astype(F32)
    mid = rest.astype(BF16)
    low = (rest - mid.astype(F32)).astype(BF16)
    return high, mid, low


PART = (3, 16, 128)


def sums_kernel(chosen, face, more, kept, given):
    matrix = chosen[...].astype(BF16)
    for c in range(3):
        total = 0.0
        for piece in pieces(face[c] + more[c]):
            total = total + jnp.dot(matrix, piece, preferred_element_type=F32)
        for k in range(8):
            (given if k % 2 else kept)[k // 2, c] = total[k * 16 : k * 16 + 16]


def partial_sums(chosen, face, more):
    return pl.pallas_call(
        sums_kernel,
        in_specs=[VM] * 3,
        out_specs=[VM, VM],
        out_shape=[in_vmem((4, *PART))] * 2,
        compiler_params=params(2),
        name="sums",
    )(vmem(chosen), vmem(face), vmem(more))


def halve_kernel(kept, came, still, given):
    for k in range(kept.shape[0]):
        (given if k % 2 else still)[k // 2] = kept[k] + came[k]


def halve(kept, came):
    return pl.pallas_call(
        halve_kernel,
        in_specs=[VM] * 2,
        out_specs=[VM, VM],
        out_shape=[in_vmem((kept.shape[0] // 2, *PART))] * 2,
        compiler_params=params(2),
        name="halve",
    )(vmem(kept), vmem(came))


def product_kernel(kept, came, filters, out, sums):
    sums[...] = kept[0] + came[0]
    for p in range(4):
        view = jnp.concatenate([sums[:, p * 4 + i, :] for i in range(4)], axis=1)
        stacked = jnp.concatenate(pieces(view), axis=0)
        wide = jnp.dot(stacked, filters[p], preferred_element_type=F32)
        out[:, p, :] = wide[0:3] + (wide[3:6] + wide[6:9])


def product(kept, came, filters):
    return pl.pallas_call(
        product_kernel,
        in_specs=[VM] * 3,
        out_specs=VM,
        out_shape=jax.ShapeDtypeStruct((3, 4, 512), F32),
        scratch_shapes=[pltpu.VMEM(PART, F32)],
        compiler_params=params(4),
        name="product",
    )(vmem(kept), vmem(came), vmem(filters))


def shards(adjoint, velocity, viscosity, filters, block_tiles, tile_place):
    nx = lax.axis_size("gx")
    nz = lax.axis_size("gz")
    ring = [(i, (i + 1) % nz) for i in range(nz)]
    back = [(b, a) for a, b in ring]
    along = [(i, i + 1) for i in range(nx - 1)]
    against = [(b, a) for a, b in along]

    *state, zl, zr = pack(adjoint, velocity, viscosity)
    hl = lax.ppermute(zl, "gz", ring)
    hr = lax.ppermute(zr, "gz", back)
    face, mid, coef, centre, middle = face_call(state, hl, hr, zl, zr)

    got = [lax.ppermute(face, "gx", [(0, k)]) for k in (8, 2, 6)]
    mid, coef, out, chosen, msg_lo, msg_hi = inner(
        state, centre, middle, block_tiles.T, tile_place.reshape(1, -1), mid, coef
    )
    *got, mid, coef, out, msg_lo, msg_hi = lax.optimization_barrier(
        (*got, mid, coef, out, msg_lo, msg_hi)
    )
    face = join(face, *got)
    face, msg_lo, msg_hi = lax.optimization_barrier((face, msg_lo, msg_hi))
    far = lax.ppermute(face, "gx", [(0, 4), (2, 10), (6, 14), (8, 12)])
    low = lax.ppermute(msg_hi, "gx", along)
    high = lax.ppermute(msg_lo, "gx", against)
    face = join(face, far)
    other = lax.ppermute(face, "gx", [(i, i + 1) for i in range(0, nx, 2)])
    kept, given = partial_sums(chosen, face, other)

    came = lax.ppermute(given, "gz", [(i, i ^ 1) for i in range(nz)])
    mid, coef, out = middle_call(state, centre, middle, mid, coef, out)
    came, mid, coef, out = lax.optimization_barrier((came, mid, coef, out))
    kept, given = halve(kept, came)
    came = lax.ppermute(given, "gz", [(i, i ^ 2) for i in range(nz)])
    state, mid, coef, out, near = side_call(
        False, state, mid, coef, centre, hl, hr, zl, zr, low, filters, out
    )
    came, mid, out = lax.optimization_barrier((came, mid, out))
    kept, given = halve(kept, came)
    came = lax.ppermute(given, "gz", [(i, i ^ 4) for i in range(nz)])
    *_, out, _ = side_call(True, state, mid, coef, centre, hl, hr, zl, zr, high, filters, out)
    came, out = lax.optimization_barrier((came, out))
    gradient = product(kept, came, near).transpose(1, 0, 2)
    return out, gradient


def solution(mesh):
    placed = (
        P(None, "gx", None, "gz"),
        P(None, "gx", None, "gz"),
        P("gx", None, "gz"),
        P(("gx", "gz"), None, None),
        P(),
        P(),
    )
    return jax.shard_map(
        shards,
        mesh=mesh,
        in_specs=placed,
        out_specs=(P(None, "gx", None, "gz"), P(("gx", "gz"), None, None)),
        check_vma=False,
    )
```

```python
import jax
import jax.numpy as jnp
from jax import lax
from jax.experimental import pallas as pl
from jax.experimental.pallas import tpu as pltpu
from jax.sharding import PartitionSpec as P

F32 = jnp.float32
BF16 = jnp.bfloat16
ANY = pl.BlockSpec(memory_space=pl.ANY)
VM = pl.BlockSpec(memory_space=pltpu.VMEM)
MIB = 1024 * 1024
ROWS = 16
GROUPS = 4


def lanes(shape):
    return lax.broadcasted_iota(jnp.int32, shape, len(shape) - 1)


def roll(x, shift, axis):
    if isinstance(shift, int):
        shift = shift % x.shape[axis]
    return pltpu.roll(x, shift, axis)


def in_vmem(shape):
    return pltpu.VMEM(shape, F32)


STATE = {
    "adj": (3, 20, 144, 128),
    "visc": (20, 144, 128),
    "vel": (3, 18, 128, 128),
    "mid": (3, 18, 144, 128),
    "coef": (7, 18, 128, 128),
}


def cost(planes):
    return pl.CostEstimate(flops=planes * 3 * 16384 * 20, transcendentals=0, bytes_accessed=planes * 16384 * 4 * 22)


def params(mib):
    return pltpu.CompilerParams(vmem_limit_bytes=mib * MIB)


def hbm(x):
    return pltpu.with_memory_space_constraint(x, pltpu.HBM)


def vmem(x):
    return pltpu.with_memory_space_constraint(x, pltpu.VMEM)


def clear_walls(ref, lead):
    for index in lead:
        ref[(*index, pl.ds(0, 8), slice(None))] = jnp.zeros((8, 128), F32)
        ref[(*index, pl.ds(136, 8), slice(None))] = jnp.zeros((8, 128), F32)


def begin(copies, sems):
    started = [pltpu.make_async_copy(s, t, sems.at[i]) for i, (s, t) in enumerate(copies)]
    for copy in started:
        copy.start()
    return started


def pack_kernel(adj, vel, visc, adj_s, visc_s, vel_s, zl, zr, acc_l, acc_r, vel_l, vel_r, sems):
    inside = pl.ds(8, 128)
    n = 16 // GROUPS

    def copies(g):
        xs = pl.ds(g * n, n)
        return (
            (adj.at[:, xs], adj_s.at[:, pl.ds(2 + g * n, n), inside]),
            (visc.at[xs], visc_s.at[pl.ds(2 + g * n, n), inside]),
            (vel.at[:, xs], vel_s.at[:, pl.ds(1 + g * n, n)]),
        )

    started = [begin(copies(g), sems.at[g]) for g in range(GROUPS)]
    clear_walls(adj_s, [(c, q) for c in range(3) for q in range(1, 20)])
    clear_walls(visc_s, [(q,) for q in range(1, 20)])
    zero = jnp.zeros((144, 128), F32)
    visc_s[1] = zero
    for c in range(3):
        adj_s[c, 1] = zero
    lane = lanes((32, 128))
    pair = lane >> 1
    pair_l = ((lane + 2) & 127) >> 1
    for g in range(GROUPS):
        for copy in started[g]:
            copy.wait()
        for r in range(4):
            rows = pl.ds(r * 32, 32)
            padded = pl.ds(8 + r * 32, 32)
            half = r // 2
            if g == 0:
                left = right = vleft = vright = jnp.zeros((32, 128), F32)
            else:
                left, right, vleft, vright = (ref[rows] for ref in (acc_l, acc_r, vel_l, vel_r))
            for c in range(4):
                for x in range(g * n, g * n + n):
                    m = c * 16 + x
                    plane = adj_s[c, x + 2, padded] if c < 3 else visc_s[x + 2, padded]
                    turned = roll(plane, 2 * m, 1)
                    right = jnp.where(pair == m, turned, right)
                    left = jnp.where(pair_l == m, turned, left)
            for d in range(3):
                for x in range(g * n, g * n + n):
                    at = 2 * (d * 16 + x) + half
                    turned = roll(vel_s[d, x + 1, rows], at, 1)
                    vright = jnp.where(lane == at, turned, vright)
                    vleft = jnp.where(lane == (at - 1) % 128, turned, vleft)
            if g < GROUPS - 1:
                acc_l[rows] = left
                acc_r[rows] = right
            else:
                zr[rows] = right
                zl[rows] = roll(left, 2, 1)
                vleft = roll(vleft, 1, 1)
            vel_l[rows] = vleft
            vel_r[rows] = vright
    even = (lanes((64, 128)) & 1) == 0
    zr[pl.ds(128, 64)] = jnp.where(even, vel_r[pl.ds(0, 64)], vel_r[pl.ds(64, 64)])
    zl[pl.ds(128, 64)] = jnp.where(even, vel_l[pl.ds(0, 64)], vel_l[pl.ds(64, 64)])


def pack(adj, vel, visc):
    return pl.pallas_call(
        pack_kernel,
        in_specs=[ANY, ANY, ANY],
        out_specs=[VM] * 5,
        out_shape=[in_vmem(STATE[k]) for k in ("adj", "visc", "vel")] + [in_vmem((192, 128))] * 2,
        scratch_shapes=[
            *[pltpu.VMEM((128, 128), F32)] * 4,
            pltpu.SemaphoreType.DMA((GROUPS, 3)),
        ],
        compiler_params=params(4),
        name="pack",
    )(hbm(adj), hbm(vel), hbm(visc))


def spread(a, group):
    kept = jnp.where((lanes(a.shape) >> 5) == group, a, 0.0)
    kept = kept + roll(kept, 32, 1)
    return kept + roll(kept, 64, 1)


def shift_rows(a, by):
    row = lax.broadcasted_iota(jnp.int32, a.shape, 0)
    moved = roll(a, by, 0)
    edge = 0 if by > 0 else a.shape[0] - 1
    return jnp.where(row == edge, 0.0, moved)


def edge_centre(hl, hr):
    odd = (lanes((128, 128)) & 1) == 1
    return jnp.where(odd, hl[pl.ds(0, 128)], hr[pl.ds(0, 128)])


def edge_velocity(message):
    both = message[pl.ds(128, 64)]
    odd = (lanes(both.shape) & 1) == 1
    upper = jnp.where(odd, roll(both, 1, 1), both)
    lower = jnp.where(odd, both, roll(both, -1, 1))
    return jnp.concatenate([upper, lower], axis=0)


def edge_middle(hl, hr, zl, zr, low=None, high=None):
    lane = lanes((128, 128))
    odd = (lane & 1) == 1
    x = (lane >> 1) & 15
    first = pl.ds(0, 128)
    left, right = hl[first], hr[first]
    centre = jnp.where(odd, left, right)
    minus = jnp.where(odd, roll(left, 1, 1), roll(zl[first], -1, 1))
    plus = jnp.where(odd, roll(zr[first], 1, 1), roll(right, -1, 1))
    velocity = jnp.where(odd, edge_velocity(hl), edge_velocity(hr))
    west = roll(centre, 2, 1)
    east = roll(centre, -2, 1)
    west = jnp.where(x == 0, 0.0 if low is None else roll(low, -30, 1), west)
    east = jnp.where(x == 15, 0.0 if high is None else roll(high, 30, 1), east)
    north = shift_rows(centre, -1)
    south = shift_rows(centre, 1)
    visc = spread(centre, 3)
    total = 0.0
    result = 0.0
    for d, (up, down) in enumerate(((east, west), (north, south), (plus, minus))):
        v = spread(velocity, d)
        a_up = 0.5 * ((visc + spread(up, 3)) + v)
        a_down = 0.5 * ((visc + spread(down, 3)) - v)
        total = total + (a_up + a_down)
        result = result + (a_up * up + a_down * down)
    return result + (1.0 - total) * centre


def ends(edge, r, m):
    return roll(edge[pl.ds(r, ROWS), :], 127 - 2 * m, 1)


def first_step(adj_s, visc_s, vel_s, mid_s, coef_s, edge, x, ex):
    lane = lanes((ROWS, 128))
    q, t = x + 2, x + 1
    for r in range(0, 128, ROWS):
        rows, here = pl.ds(r, ROWS), pl.ds(8 + r, ROWS)
        above, below = pl.ds(9 + r, ROWS), pl.ds(7 + r, ROWS)

        def sides(plane, m):
            end = ends(edge, r, m)
            up = jnp.where(lane == 127, end, roll(plane, -1, 1))
            return up, jnp.where(lane == 0, end, roll(plane, 1, 1))

        centre = visc_s[q, here, :]
        pairs = (
            (visc_s[q + 1, here, :], visc_s[q - 1, here, :]),
            (visc_s[q, above, :], visc_s[q, below, :]),
            sides(centre, 48 + ex),
        )
        a = []
        for d, (plus, minus) in enumerate(pairs):
            v = vel_s[d, t, rows, :]
            a.append(0.5 * ((centre + plus) + v))
            a.append(0.5 * ((centre + minus) - v))
        a.append(1.0 - (((a[0] + a[1]) + (a[2] + a[3])) + (a[4] + a[5])))
        for k in range(7):
            coef_s[k, t, rows, :] = a[k]
        for c in range(3):
            centre = adj_s[c, q, here, :]
            up, down = sides(centre, c * 16 + ex)
            out = a[6] * centre
            out = out + a[0] * adj_s[c, q + 1, here, :]
            out = out + a[1] * adj_s[c, q - 1, here, :]
            out = out + a[2] * adj_s[c, q, above, :]
            out = out + a[3] * adj_s[c, q, below, :]
            out = out + a[4] * up
            mid_s[c, t, here, :] = out + a[5] * down
    for c in range(3):
        mid_s[c, t, pl.ds(0, 8), :] = jnp.zeros((8, 128), F32)
        mid_s[c, t, pl.ds(136, 8), :] = jnp.zeros((8, 128), F32)


def second_step(mid_s, coef_s, edge, x, store):
    lane = lanes((ROWS, 128))
    t = x + 1
    for r in range(0, 128, ROWS):
        rows, here = pl.ds(r, ROWS), pl.ds(8 + r, ROWS)
        above, below = pl.ds(9 + r, ROWS), pl.ds(7 + r, ROWS)
        a = [coef_s[k, t, rows, :] for k in range(7)]
        for c in range(3):
            centre = mid_s[c, t, here, :]
            end = ends(edge, r, c * 16 + x)
            out = a[6] * centre
            out = out + a[0] * mid_s[c, t + 1, here, :]
            out = out + a[1] * mid_s[c, t - 1, here, :]
            out = out + a[2] * mid_s[c, t, above, :]
            out = out + a[3] * mid_s[c, t, below, :]
            out = out + a[4] * jnp.where(lane == 127, end, roll(centre, -1, 1))
            store(c, rows, out + a[5] * jnp.where(lane == 0, end, roll(centre, 1, 1)))


def face_kernel(
    adj_s, visc_s, vel_s, hl, hr, zl, zr, face, mid_s, coef_s, centre, middle
):
    centre[...] = edge_centre(hl, hr)
    middle[...] = edge_middle(hl, hr, zl, zr)
    for c in range(3):
        mid_s[c, 0] = jnp.zeros((144, 128), F32)
    for x in range(2):
        first_step(adj_s, visc_s, vel_s, mid_s, coef_s, centre, x, x)
    own = jnp.where(lax.axis_index("gx") == 0, 1.0, 0.0)

    def store(c, rows, v):
        face[c, rows, :] = v * own

    second_step(mid_s, coef_s, middle, 0, store)


def face_call(state, hl, hr, zl, zr):
    return pl.pallas_call(
        face_kernel,
        in_specs=[VM] * 7,
        out_specs=[VM] * 5,
        out_shape=[
            in_vmem((3, 128, 128)),
            in_vmem(STATE["mid"]),
            in_vmem(STATE["coef"]),
            in_vmem((128, 128)),
            in_vmem((128, 128)),
        ],
        compiler_params=params(4),
        cost_estimate=cost(3),
        name="face",
    )(*[vmem(a) for a in (*state, hl, hr, zl, zr)])


def ship_kernel(adj_s, visc_s, vel_s, _, msg_lo, msg_hi, sems):
    moved = []
    inside = pl.ds(8, 128)
    for msg, q, t in ((msg_lo, 2, 1), (msg_hi, 16, 16)):
        for c in range(3):
            moved.append((adj_s.at[c, pl.ds(q, 2), inside], msg.at[pl.ds(2 * c, 2)]))
            moved.append((vel_s.at[c, pl.ds(t, 1)], msg.at[pl.ds(6 + c, 1)]))
        moved.append((visc_s.at[pl.ds(q, 2), inside], msg.at[pl.ds(9, 2)]))
    for copy in begin(moved, sems):
        copy.wait()


def ship(state, after):
    msg = pltpu.HBM((11, 128, 128), F32)
    return pl.pallas_call(
        ship_kernel,
        in_specs=[VM] * 4,
        out_specs=[ANY, ANY],
        out_shape=[msg, msg],
        scratch_shapes=[pltpu.SemaphoreType.DMA((14,))],
        compiler_params=params(1),
        cost_estimate=pl.CostEstimate(flops=0, transcendentals=0, bytes_accessed=2 * 2 * 11 * 65536),
        name="ship",
    )(*[vmem(a) for a in (*state, after)])


def choose(lists, place):
    gx, gz = lax.axis_index("gx"), lax.axis_index("gz")
    half = lists[:, pl.ds(pl.multiple_of((gz // 4) * 128, 128), 128)]
    tile = lax.broadcasted_iota(jnp.int32, (512, 128), 0)
    listed = jnp.zeros((512, 128), F32)
    for k in range(8):
        listed = listed + jnp.where(half[k : k + 1] == tile, 1.0, 0.0)
    row = lax.broadcasted_iota(jnp.int32, (128, 512), 0)
    wanted = gx * 32 + ((row >> 4) ^ gz) * 4 + ((row >> 2) & 3)
    sits = jnp.where(place[...] == wanted, 1.0, 0.0).astype(BF16)
    count = jnp.dot(sits, listed.astype(BF16), preferred_element_type=F32)
    row = lax.broadcasted_iota(jnp.int32, (128, 128), 0)
    column = lanes((128, 128))
    ours = jnp.where(row == (gz % 4) * 32 + (column >> 2), 1.0, 0.0).astype(BF16)
    wide = jnp.dot(count.astype(BF16), ours, preferred_element_type=F32)
    return jnp.where((row & 3) == (column & 3), wide, 0.0)


FIELD = (3, 16, 128, 128)


def run_first(cells, state, mid_s, coef_s, edge):
    for x in cells:
        first_step(*state, mid_s, coef_s, edge, x, x)


def run_second(cells, mid_s, coef_s, edge, done):
    for x in cells:

        def store(c, rows, v, x=x):
            done[c, x, rows, :] = v

        second_step(mid_s, coef_s, edge, x, store)


def inner_kernel(
    adj_s, visc_s, vel_s, centre, middle, lists, place, _, __, mid_s, coef_s, done, chosen, corner
):
    corner[...] = centre[...]
    chosen[...] = choose(lists, place)
    run_first(range(2, 9), (adj_s, visc_s, vel_s), mid_s, coef_s, centre)
    run_second(range(2, 8), mid_s, coef_s, middle, done)


def inner(state, centre, middle, lists, place, mid, coef):
    return pl.pallas_call(
        inner_kernel,
        in_specs=[VM] * 9,
        out_specs=[VM] * 5,
        out_shape=[
            in_vmem(STATE["mid"]),
            in_vmem(STATE["coef"]),
            in_vmem(FIELD),
            in_vmem((128, 128)),
            in_vmem((128, 128)),
        ],
        input_output_aliases={7: 0, 8: 1},
        compiler_params=params(4),
        cost_estimate=cost(13),
        name="inner",
    )(*[vmem(a) for a in (*state, centre, middle)], lists, place, vmem(mid), vmem(coef))


def middle_kernel(
    adj_i, visc_i, vel_i, centre, middle, _, __, ___, low, high, filters,
    adj_s, visc_s, vel_s, mid_s, coef_s, done, out, kept, sems, sem_o, sem_f,
):
    inside = pl.ds(8, 128)
    pairs = []
    for msg, q, t in ((low, 0, 0), (high, 18, 17)):
        for c in range(3):
            pairs.append((msg.at[pl.ds(2 * c, 2)], adj_s.at[c, pl.ds(q, 2), inside]))
            pairs.append((msg.at[pl.ds(6 + c, 1)], vel_s.at[c, pl.ds(t, 1)]))
        pairs.append((msg.at[pl.ds(9, 2)], visc_s.at[pl.ds(q, 2), inside]))
    started = begin([(done.at[:, pl.ds(2, 6)], out.at[:, pl.ds(2, 6)])], sem_o)
    started += begin(pairs, sems)
    started += begin([(filters, kept)], sem_f)
    run_first(range(9, 15), (adj_s, visc_s, vel_s), mid_s, coef_s, centre)
    run_second(range(8, 14), mid_s, coef_s, middle, done)
    for copy in started:
        copy.wait()


def middle_call(state, centre, middle, mid, coef, done, low, high, filters):
    held = [vmem(a) for a in (*state, centre, middle, mid, coef, done)]
    return pl.pallas_call(
        middle_kernel,
        in_specs=[VM] * 8 + [ANY] * 3,
        out_specs=[VM] * 6 + [ANY, VM],
        out_shape=[in_vmem(STATE[k]) for k in ("adj", "visc", "vel", "mid", "coef")]
        + [in_vmem(FIELD), pltpu.HBM(FIELD, F32), pltpu.VMEM(filters.shape, BF16)],
        scratch_shapes=[
            pltpu.SemaphoreType.DMA((14,)),
            pltpu.SemaphoreType.DMA((1,)),
            pltpu.SemaphoreType.DMA((1,)),
        ],
        input_output_aliases={0: 0, 1: 1, 2: 2, 5: 3, 6: 4, 7: 5},
        compiler_params=params(4),
        cost_estimate=cost(12),
        name="middle",
    )(*held, low, high, hbm(filters))


def sides_kernel(
    adj_s, visc_s, vel_s, centre, hl, hr, zl, zr, low, high, _, __, ___, ____,
    mid_s, coef_s, done, out, edges, sems,
):
    started = begin([(done.at[:, pl.ds(8, 6)], out.at[:, pl.ds(8, 6)])], sems)
    edges[...] = edge_middle(hl, hr, zl, zr, low[...], high[...])
    state = (adj_s, visc_s, vel_s)
    first_step(*state, mid_s, coef_s, low, -1, 15)
    first_step(*state, mid_s, coef_s, high, 16, 0)
    run_first((0, 15), state, mid_s, coef_s, centre)
    gx = lax.axis_index("gx")
    for t, end in ((0, 0), (17, lax.axis_size("gx") - 1)):

        @pl.when(gx == end)
        def _(t=t):
            for c in range(3):
                mid_s[c, t] = jnp.zeros((144, 128), F32)

    for i, x in enumerate((0, 14)):
        run_second((x, x + 1), mid_s, coef_s, edges, done)
        copy = pltpu.make_async_copy(
            done.at[:, pl.ds(x, 2)], out.at[:, pl.ds(x, 2)], sems.at[i + 1]
        )
        copy.start()
        started.append(copy)
    for copy in started:
        copy.wait()


def sides_call(state, centre, hl, hr, zl, zr, low, high, mid, coef, done, out):
    held = [vmem(a) for a in (*state, centre, hl, hr, zl, zr, low, high, mid, coef, done)]
    return pl.pallas_call(
        sides_kernel,
        in_specs=[VM] * 13 + [ANY],
        out_specs=[VM] * 3 + [ANY],
        out_shape=[in_vmem(STATE["mid"]), in_vmem(STATE["coef"]), in_vmem(FIELD)]
        + [pltpu.HBM(FIELD, F32)],
        scratch_shapes=[pltpu.VMEM((128, 128), F32), pltpu.SemaphoreType.DMA((3,))],
        input_output_aliases={10: 0, 11: 1, 12: 2, 13: 3},
        compiler_params=params(4),
        cost_estimate=cost(8),
        name="sides",
    )(*held, hbm(out))[-1]


def join_kernel(*refs):
    total = refs[0][...]
    for ref in refs[1:-1]:
        total = total + ref[...]
    refs[-1][...] = total


def join(*parts):
    return pl.pallas_call(
        join_kernel,
        in_specs=[VM] * len(parts),
        out_specs=VM,
        out_shape=in_vmem(parts[0].shape),
        compiler_params=params(2),
        name="join",
    )(*[vmem(a) for a in parts])


def pieces(a):
    high = a.astype(BF16)
    rest = a - high.astype(F32)
    mid = rest.astype(BF16)
    low = (rest - mid.astype(F32)).astype(BF16)
    return high, mid, low


PART = (3, 16, 128)


def sums_kernel(chosen, face, more, kept, given):
    matrix = chosen[...].astype(BF16)
    for c in range(3):
        total = 0.0
        for piece in pieces(face[c] + more[c]):
            total = total + jnp.dot(matrix, piece, preferred_element_type=F32)
        for k in range(8):
            (given if k % 2 else kept)[k // 2, c] = total[k * 16 : k * 16 + 16]


def partial_sums(chosen, face, more):
    return pl.pallas_call(
        sums_kernel,
        in_specs=[VM] * 3,
        out_specs=[VM, VM],
        out_shape=[in_vmem((4, *PART))] * 2,
        compiler_params=params(2),
        name="sums",
    )(vmem(chosen), vmem(face), vmem(more))


def halve_kernel(kept, came, *parts):
    for k, part in enumerate(parts):
        part[...] = kept[k] + came[k]


def halve(kept, came):
    return pl.pallas_call(
        halve_kernel,
        in_specs=[VM] * 2,
        out_specs=[VM] * 4,
        out_shape=[in_vmem(PART)] * 4,
        compiler_params=params(2),
        name="halve",
    )(vmem(kept), vmem(came))


def product_kernel(a, b, c, d, filters, out, sums):
    sums[...] = (a[...] + b[...]) + (c[...] + d[...])
    for p in range(4):
        view = jnp.concatenate([sums[:, p * 4 + i, :] for i in range(4)], axis=1)
        stacked = jnp.concatenate(pieces(view), axis=0)
        wide = jnp.dot(stacked, filters[p], preferred_element_type=F32)
        out[:, p, :] = wide[0:3] + (wide[3:6] + wide[6:9])


def product(parts, filters):
    return pl.pallas_call(
        product_kernel,
        in_specs=[VM] * 5,
        out_specs=VM,
        out_shape=jax.ShapeDtypeStruct((3, 4, 512), F32),
        scratch_shapes=[pltpu.VMEM(PART, F32)],
        compiler_params=params(4),
        name="product",
    )(*[vmem(a) for a in (*parts, filters)])


def shards(adjoint, velocity, viscosity, filters, block_tiles, tile_place):
    nx = lax.axis_size("gx")
    nz = lax.axis_size("gz")
    ring = [(i, (i + 1) % nz) for i in range(nz)]
    back = [(b, a) for a, b in ring]
    along = [(i, i + 1) for i in range(nx - 1)]
    against = [(b, a) for a, b in along]

    *state, zl, zr = pack(adjoint, velocity, viscosity)
    hl = lax.ppermute(zl, "gz", ring)
    hr = lax.ppermute(zr, "gz", back)
    msg_lo, msg_hi = ship(state, zl)
    low = lax.ppermute(msg_hi, "gx", along)
    high = lax.ppermute(msg_lo, "gx", against)
    hl, hr, *_ = lax.optimization_barrier((hl, hr, msg_lo, msg_hi))
    face, mid, coef, centre, middle = face_call(state, hl, hr, zl, zr)

    got = [lax.ppermute(face, "gx", [(0, k)]) for k in (8, 2, 6)]
    mid, coef, done, chosen, corner = inner(
        state, centre, middle, block_tiles.T, tile_place.reshape(1, -1), mid, coef
    )
    beside = lax.ppermute(corner, "gx", along), lax.ppermute(corner, "gx", against)
    *got, mid, coef, done = lax.optimization_barrier((*got, mid, coef, done))
    face = join(face, *got)
    far = lax.ppermute(face, "gx", [(0, 4), (2, 10), (6, 14), (8, 12)])
    *state, mid, coef, done, out, near = middle_call(
        state, centre, middle, mid, coef, done, low, high, filters
    )
    far, mid, coef, done, *beside = lax.optimization_barrier((far, mid, coef, done, *beside))
    face = join(face, far)
    other = lax.ppermute(face, "gx", [(i, i + 1) for i in range(0, nx, 2)])
    kept, given = partial_sums(chosen, face, other)

    came = lax.ppermute(given, "gz", [(i, i ^ 1) for i in range(nz)])
    out = sides_call(state, centre, hl, hr, zl, zr, *beside, mid, coef, done, out)
    came, out = lax.optimization_barrier((came, out))
    parts = halve(kept, came)
    parts = [parts[0]] + [
        lax.ppermute(parts[k], "gz", [(i, i ^ (2 * k)) for i in range(nz)]) for k in (2, 1, 3)
    ]
    gradient = product(parts, near).transpose(1, 0, 2)
    return out, gradient


def solution(mesh):
    placed = (
        P(None, "gx", None, "gz"),
        P(None, "gx", None, "gz"),
        P("gx", None, "gz"),
        P(("gx", "gz"), None, None),
        P(),
        P(),
    )
    return jax.shard_map(
        shards,
        mesh=mesh,
        in_specs=placed,
        out_specs=(P(None, "gx", None, "gz"), P(("gx", "gz"), None, None)),
        check_vma=False,
    )
```

```python
import jax
import jax.numpy as jnp
from jax import lax
from jax.experimental import pallas as pl
from jax.experimental.pallas import tpu as pltpu
from jax.sharding import PartitionSpec as P

F32 = jnp.float32
BF16 = jnp.bfloat16
ANY = pl.BlockSpec(memory_space=pl.ANY)
VM = pl.BlockSpec(memory_space=pltpu.VMEM)
MIB = 1024 * 1024
ROWS = 16
GROUPS = 4


def lanes(shape):
    return lax.broadcasted_iota(jnp.int32, shape, len(shape) - 1)


def roll(x, shift, axis):
    if isinstance(shift, int):
        shift = shift % x.shape[axis]
    return pltpu.roll(x, shift, axis)


def in_vmem(shape):
    return pltpu.VMEM(shape, F32)


STATE = {
    "adj": (3, 20, 144, 128),
    "visc": (20, 144, 128),
    "vel": (3, 18, 128, 128),
    "mid": (3, 18, 144, 128),
    "coef": (7, 18, 128, 128),
}


def cost(planes):
    return pl.CostEstimate(flops=planes * 3 * 16384 * 20, transcendentals=0, bytes_accessed=planes * 16384 * 4 * 22)


def params(mib):
    return pltpu.CompilerParams(vmem_limit_bytes=mib * MIB)


def hbm(x):
    return pltpu.with_memory_space_constraint(x, pltpu.HBM)


def vmem(x):
    return pltpu.with_memory_space_constraint(x, pltpu.VMEM)


def clear_walls(ref, lead):
    for index in lead:
        ref[(*index, pl.ds(0, 8), slice(None))] = jnp.zeros((8, 128), F32)
        ref[(*index, pl.ds(136, 8), slice(None))] = jnp.zeros((8, 128), F32)


def begin(copies, sems):
    started = [pltpu.make_async_copy(s, t, sems.at[i]) for i, (s, t) in enumerate(copies)]
    for copy in started:
        copy.start()
    return started


def pack_kernel(adj, vel, visc, adj_s, visc_s, vel_s, zl, zr, acc_l, acc_r, vel_l, vel_r, sems):
    inside = pl.ds(8, 128)
    n = 16 // GROUPS

    def copies(g):
        xs = pl.ds(g * n, n)
        return (
            (adj.at[:, xs], adj_s.at[:, pl.ds(2 + g * n, n), inside]),
            (visc.at[xs], visc_s.at[pl.ds(2 + g * n, n), inside]),
            (vel.at[:, xs], vel_s.at[:, pl.ds(1 + g * n, n)]),
        )

    started = [begin(copies(g), sems.at[g]) for g in range(GROUPS)]
    clear_walls(adj_s, [(c, q) for c in range(3) for q in range(1, 20)])
    clear_walls(visc_s, [(q,) for q in range(1, 20)])
    zero = jnp.zeros((144, 128), F32)
    visc_s[1] = zero
    for c in range(3):
        adj_s[c, 1] = zero
    lane = lanes((32, 128))
    pair = lane >> 1
    pair_l = ((lane + 2) & 127) >> 1
    for g in range(GROUPS):
        for copy in started[g]:
            copy.wait()
        for r in range(4):
            rows = pl.ds(r * 32, 32)
            padded = pl.ds(8 + r * 32, 32)
            half = r // 2
            if g == 0:
                left = right = vleft = vright = jnp.zeros((32, 128), F32)
            else:
                left, right, vleft, vright = (ref[rows] for ref in (acc_l, acc_r, vel_l, vel_r))
            for c in range(4):
                for x in range(g * n, g * n + n):
                    m = c * 16 + x
                    plane = adj_s[c, x + 2, padded] if c < 3 else visc_s[x + 2, padded]
                    turned = roll(plane, 2 * m, 1)
                    right = jnp.where(pair == m, turned, right)
                    left = jnp.where(pair_l == m, turned, left)
            for d in range(3):
                for x in range(g * n, g * n + n):
                    at = 2 * (d * 16 + x) + half
                    turned = roll(vel_s[d, x + 1, rows], at, 1)
                    vright = jnp.where(lane == at, turned, vright)
                    vleft = jnp.where(lane == (at - 1) % 128, turned, vleft)
            if g < GROUPS - 1:
                acc_l[rows] = left
                acc_r[rows] = right
            else:
                zr[rows] = right
                zl[rows] = roll(left, 2, 1)
                vleft = roll(vleft, 1, 1)
            vel_l[rows] = vleft
            vel_r[rows] = vright
    even = (lanes((64, 128)) & 1) == 0
    zr[pl.ds(128, 64)] = jnp.where(even, vel_r[pl.ds(0, 64)], vel_r[pl.ds(64, 64)])
    zl[pl.ds(128, 64)] = jnp.where(even, vel_l[pl.ds(0, 64)], vel_l[pl.ds(64, 64)])


def pack(adj, vel, visc):
    return pl.pallas_call(
        pack_kernel,
        in_specs=[ANY, ANY, ANY],
        out_specs=[VM] * 5,
        out_shape=[in_vmem(STATE[k]) for k in ("adj", "visc", "vel")] + [in_vmem((192, 128))] * 2,
        scratch_shapes=[
            *[pltpu.VMEM((128, 128), F32)] * 4,
            pltpu.SemaphoreType.DMA((GROUPS, 3)),
        ],
        compiler_params=params(4),
        name="pack",
    )(hbm(adj), hbm(vel), hbm(visc))


def spread(a, group):
    kept = jnp.where((lanes(a.shape) >> 5) == group, a, 0.0)
    kept = kept + roll(kept, 32, 1)
    return kept + roll(kept, 64, 1)


def shift_rows(a, by):
    row = lax.broadcasted_iota(jnp.int32, a.shape, 0)
    moved = roll(a, by, 0)
    edge = 0 if by > 0 else a.shape[0] - 1
    return jnp.where(row == edge, 0.0, moved)


def edge_centre(hl, hr):
    odd = (lanes((128, 128)) & 1) == 1
    return jnp.where(odd, hl[pl.ds(0, 128)], hr[pl.ds(0, 128)])


def edge_velocity(message):
    both = message[pl.ds(128, 64)]
    odd = (lanes(both.shape) & 1) == 1
    upper = jnp.where(odd, roll(both, 1, 1), both)
    lower = jnp.where(odd, both, roll(both, -1, 1))
    return jnp.concatenate([upper, lower], axis=0)


def edge_middle(hl, hr, zl, zr, low=None, high=None):
    lane = lanes((128, 128))
    odd = (lane & 1) == 1
    x = (lane >> 1) & 15
    first = pl.ds(0, 128)
    left, right = hl[first], hr[first]
    centre = jnp.where(odd, left, right)
    minus = jnp.where(odd, roll(left, 1, 1), roll(zl[first], -1, 1))
    plus = jnp.where(odd, roll(zr[first], 1, 1), roll(right, -1, 1))
    velocity = jnp.where(odd, edge_velocity(hl), edge_velocity(hr))
    west = roll(centre, 2, 1)
    east = roll(centre, -2, 1)
    west = jnp.where(x == 0, 0.0 if low is None else roll(low, -30, 1), west)
    east = jnp.where(x == 15, 0.0 if high is None else roll(high, 30, 1), east)
    north = shift_rows(centre, -1)
    south = shift_rows(centre, 1)
    visc = spread(centre, 3)
    total = 0.0
    result = 0.0
    for d, (up, down) in enumerate(((east, west), (north, south), (plus, minus))):
        v = spread(velocity, d)
        a_up = 0.5 * ((visc + spread(up, 3)) + v)
        a_down = 0.5 * ((visc + spread(down, 3)) - v)
        total = total + (a_up + a_down)
        result = result + (a_up * up + a_down * down)
    return result + (1.0 - total) * centre


def ends(edge, r, m):
    return roll(edge[pl.ds(r, ROWS), :], 127 - 2 * m, 1)


def first_step(adj_s, visc_s, vel_s, mid_s, coef_s, edge, x, ex):
    lane = lanes((ROWS, 128))
    q, t = x + 2, x + 1
    for r in range(0, 128, ROWS):
        rows, here = pl.ds(r, ROWS), pl.ds(8 + r, ROWS)
        above, below = pl.ds(9 + r, ROWS), pl.ds(7 + r, ROWS)

        def sides(plane, m):
            end = ends(edge, r, m)
            up = jnp.where(lane == 127, end, roll(plane, -1, 1))
            return up, jnp.where(lane == 0, end, roll(plane, 1, 1))

        centre = visc_s[q, here, :]
        pairs = (
            (visc_s[q + 1, here, :], visc_s[q - 1, here, :]),
            (visc_s[q, above, :], visc_s[q, below, :]),
            sides(centre, 48 + ex),
        )
        a = []
        for d, (plus, minus) in enumerate(pairs):
            v = vel_s[d, t, rows, :]
            a.append(0.5 * ((centre + plus) + v))
            a.append(0.5 * ((centre + minus) - v))
        a.append(1.0 - (((a[0] + a[1]) + (a[2] + a[3])) + (a[4] + a[5])))
        for k in range(7):
            coef_s[k, t, rows, :] = a[k]
        for c in range(3):
            centre = adj_s[c, q, here, :]
            up, down = sides(centre, c * 16 + ex)
            out = a[6] * centre
            out = out + a[0] * adj_s[c, q + 1, here, :]
            out = out + a[1] * adj_s[c, q - 1, here, :]
            out = out + a[2] * adj_s[c, q, above, :]
            out = out + a[3] * adj_s[c, q, below, :]
            out = out + a[4] * up
            mid_s[c, t, here, :] = out + a[5] * down
    for c in range(3):
        mid_s[c, t, pl.ds(0, 8), :] = jnp.zeros((8, 128), F32)
        mid_s[c, t, pl.ds(136, 8), :] = jnp.zeros((8, 128), F32)


def second_step(mid_s, coef_s, edge, x, store):
    lane = lanes((ROWS, 128))
    t = x + 1
    for r in range(0, 128, ROWS):
        rows, here = pl.ds(r, ROWS), pl.ds(8 + r, ROWS)
        above, below = pl.ds(9 + r, ROWS), pl.ds(7 + r, ROWS)
        a = [coef_s[k, t, rows, :] for k in range(7)]
        for c in range(3):
            centre = mid_s[c, t, here, :]
            end = ends(edge, r, c * 16 + x)
            out = a[6] * centre
            out = out + a[0] * mid_s[c, t + 1, here, :]
            out = out + a[1] * mid_s[c, t - 1, here, :]
            out = out + a[2] * mid_s[c, t, above, :]
            out = out + a[3] * mid_s[c, t, below, :]
            out = out + a[4] * jnp.where(lane == 127, end, roll(centre, -1, 1))
            store(c, rows, out + a[5] * jnp.where(lane == 0, end, roll(centre, 1, 1)))


def face_kernel(
    adj_s, visc_s, vel_s, hl, hr, zl, zr, face, mid_s, coef_s, centre, middle
):
    centre[...] = edge_centre(hl, hr)
    middle[...] = edge_middle(hl, hr, zl, zr)
    for c in range(3):
        mid_s[c, 0] = jnp.zeros((144, 128), F32)
    for x in range(2):
        first_step(adj_s, visc_s, vel_s, mid_s, coef_s, centre, x, x)
    own = jnp.where(lax.axis_index("gx") == 0, 1.0, 0.0)

    def store(c, rows, v):
        face[c, rows, :] = v * own

    second_step(mid_s, coef_s, middle, 0, store)


def face_call(state, hl, hr, zl, zr):
    return pl.pallas_call(
        face_kernel,
        in_specs=[VM] * 7,
        out_specs=[VM] * 5,
        out_shape=[
            in_vmem((3, 128, 128)),
            in_vmem(STATE["mid"]),
            in_vmem(STATE["coef"]),
            in_vmem((128, 128)),
            in_vmem((128, 128)),
        ],
        compiler_params=params(4),
        cost_estimate=cost(3),
        name="face",
    )(*[vmem(a) for a in (*state, hl, hr, zl, zr)])


def ship_kernel(adj_s, visc_s, vel_s, centre, msg_lo, msg_hi, sems):
    moved = []
    inside = pl.ds(8, 128)
    for msg, q, t in ((msg_lo, 2, 1), (msg_hi, 16, 16)):
        for c in range(3):
            moved.append((adj_s.at[c, pl.ds(q, 2), inside], msg.at[pl.ds(2 * c, 2)]))
            moved.append((vel_s.at[c, pl.ds(t, 1)], msg.at[pl.ds(6 + c, 1)]))
        moved.append((visc_s.at[pl.ds(q, 2), inside], msg.at[pl.ds(9, 2)]))
        moved.append((centre, msg.at[11]))
    for copy in begin(moved, sems):
        copy.wait()


def ship(state, centre):
    msg = pltpu.HBM((12, 128, 128), F32)
    return pl.pallas_call(
        ship_kernel,
        in_specs=[VM] * 4,
        out_specs=[ANY, ANY],
        out_shape=[msg, msg],
        scratch_shapes=[pltpu.SemaphoreType.DMA((16,))],
        compiler_params=params(1),
        cost_estimate=pl.CostEstimate(flops=0, transcendentals=0, bytes_accessed=2 * 2 * 11 * 65536),
        name="ship",
    )(*[vmem(a) for a in (*state, centre)])


def choose(lists, place):
    gx, gz = lax.axis_index("gx"), lax.axis_index("gz")
    half = lists[:, pl.ds(pl.multiple_of((gz // 4) * 128, 128), 128)]
    tile = lax.broadcasted_iota(jnp.int32, (512, 128), 0)
    listed = jnp.zeros((512, 128), F32)
    for k in range(8):
        listed = listed + jnp.where(half[k : k + 1] == tile, 1.0, 0.0)
    row = lax.broadcasted_iota(jnp.int32, (128, 512), 0)
    wanted = gx * 32 + ((row >> 4) ^ gz) * 4 + ((row >> 2) & 3)
    sits = jnp.where(place[...] == wanted, 1.0, 0.0).astype(BF16)
    count = jnp.dot(sits, listed.astype(BF16), preferred_element_type=F32)
    row = lax.broadcasted_iota(jnp.int32, (128, 128), 0)
    column = lanes((128, 128))
    ours = jnp.where(row == (gz % 4) * 32 + (column >> 2), 1.0, 0.0).astype(BF16)
    wide = jnp.dot(count.astype(BF16), ours, preferred_element_type=F32)
    return jnp.where((row & 3) == (column & 3), wide, 0.0)


FIELD = (3, 16, 128, 128)


def run_first(cells, state, mid_s, coef_s, edge):
    for x in cells:
        first_step(*state, mid_s, coef_s, edge, x, x)


def run_second(cells, mid_s, coef_s, edge, done):
    for x in cells:

        def store(c, rows, v, x=x):
            done[c, x, rows, :] = v

        second_step(mid_s, coef_s, edge, x, store)


def inner_kernel(
    adj_s, visc_s, vel_s, centre, middle, lists, place, _, __, mid_s, coef_s, done, chosen
):
    chosen[...] = choose(lists, place)
    run_first(range(2, 9), (adj_s, visc_s, vel_s), mid_s, coef_s, centre)
    run_second(range(2, 8), mid_s, coef_s, middle, done)


def inner(state, centre, middle, lists, place, mid, coef):
    return pl.pallas_call(
        inner_kernel,
        in_specs=[VM] * 9,
        out_specs=[VM] * 4,
        out_shape=[
            in_vmem(STATE["mid"]),
            in_vmem(STATE["coef"]),
            in_vmem(FIELD),
            in_vmem((128, 128)),
        ],
        input_output_aliases={7: 0, 8: 1},
        compiler_params=params(4),
        cost_estimate=cost(13),
        name="inner",
    )(*[vmem(a) for a in (*state, centre, middle)], lists, place, vmem(mid), vmem(coef))


def middle_kernel(
    adj_s, visc_s, vel_s, centre, middle, _, __, ___, filters, mid_s, coef_s, done, out, kept, sems
):
    started = begin([(done.at[:, pl.ds(2, 6)], out.at[:, pl.ds(2, 6)]), (filters, kept)], sems)
    run_first(range(9, 15), (adj_s, visc_s, vel_s), mid_s, coef_s, centre)
    run_second(range(8, 14), mid_s, coef_s, middle, done)
    for copy in started:
        copy.wait()


def middle_call(state, centre, middle, mid, coef, done, filters):
    held = [vmem(a) for a in (*state, centre, middle, mid, coef, done)]
    return pl.pallas_call(
        middle_kernel,
        in_specs=[VM] * 8 + [ANY],
        out_specs=[VM] * 3 + [ANY, VM],
        out_shape=[in_vmem(STATE["mid"]), in_vmem(STATE["coef"]), in_vmem(FIELD)]
        + [pltpu.HBM(FIELD, F32), pltpu.VMEM(filters.shape, BF16)],
        scratch_shapes=[pltpu.SemaphoreType.DMA((2,))],
        input_output_aliases={5: 0, 6: 1, 7: 2},
        compiler_params=params(4),
        cost_estimate=cost(12),
        name="middle",
    )(*held, hbm(filters))


def sides_kernel(
    adj_i, visc_i, vel_i, centre, hl, hr, zl, zr, low, high, _, __, ___, ____,
    adj_s, visc_s, vel_s, mid_s, coef_s, done, out, edges, sems,
):
    started = begin([(done.at[:, pl.ds(8, 6)], out.at[:, pl.ds(8, 6)])], sems)
    for msg, q, t in ((low, 0, 0), (high, 18, 17)):
        for i in range(2):
            for c in range(3):
                adj_s[c, q + i, pl.ds(8, 128)] = msg[2 * c + i]
            visc_s[q + i, pl.ds(8, 128)] = msg[9 + i]
        for d in range(3):
            vel_s[d, t] = msg[6 + d]
    edges[...] = edge_middle(hl, hr, zl, zr, low[11], high[11])
    state = (adj_s, visc_s, vel_s)
    first_step(*state, mid_s, coef_s, low.at[11], -1, 15)
    first_step(*state, mid_s, coef_s, high.at[11], 16, 0)
    run_first((0, 15), state, mid_s, coef_s, centre)
    gx = lax.axis_index("gx")
    for t, end in ((0, 0), (17, lax.axis_size("gx") - 1)):

        @pl.when(gx == end)
        def _(t=t):
            for c in range(3):
                mid_s[c, t] = jnp.zeros((144, 128), F32)

    for i, x in enumerate((0, 14)):
        run_second((x, x + 1), mid_s, coef_s, edges, done)
        copy = pltpu.make_async_copy(
            done.at[:, pl.ds(x, 2)], out.at[:, pl.ds(x, 2)], sems.at[i + 1]
        )
        copy.start()
        started.append(copy)
    for copy in started:
        copy.wait()


def sides_call(state, centre, hl, hr, zl, zr, low, high, mid, coef, done, out):
    held = [vmem(a) for a in (*state, centre, hl, hr, zl, zr, low, high, mid, coef, done)]
    return pl.pallas_call(
        sides_kernel,
        in_specs=[VM] * 13 + [ANY],
        out_specs=[VM] * 6 + [ANY],
        out_shape=[in_vmem(STATE[k]) for k in ("adj", "visc", "vel", "mid", "coef")]
        + [in_vmem(FIELD), pltpu.HBM(FIELD, F32)],
        scratch_shapes=[pltpu.VMEM((128, 128), F32), pltpu.SemaphoreType.DMA((3,))],
        input_output_aliases={0: 0, 1: 1, 2: 2, 10: 3, 11: 4, 12: 5, 13: 6},
        compiler_params=params(4),
        cost_estimate=cost(8),
        name="sides",
    )(*held, hbm(out))[-1]


def join_kernel(*refs):
    total = refs[0][...]
    for ref in refs[1:-1]:
        total = total + ref[...]
    refs[-1][...] = total


def join(*parts):
    return pl.pallas_call(
        join_kernel,
        in_specs=[VM] * len(parts),
        out_specs=VM,
        out_shape=in_vmem(parts[0].shape),
        compiler_params=params(2),
        name="join",
    )(*[vmem(a) for a in parts])


def pieces(a):
    high = a.astype(BF16)
    rest = a - high.astype(F32)
    mid = rest.astype(BF16)
    low = (rest - mid.astype(F32)).astype(BF16)
    return high, mid, low


PART = (3, 16, 128)


def sums_kernel(chosen, face, more, *pairs):
    matrix = chosen[...].astype(BF16)
    for c in range(3):
        total = 0.0
        for piece in pieces(face[c] + more[c]):
            total = total + jnp.dot(matrix, piece, preferred_element_type=F32)
        for k in range(8):
            pairs[k // 2][k % 2, c] = total[k * 16 : k * 16 + 16]


def partial_sums(chosen, face, more):
    return pl.pallas_call(
        sums_kernel,
        in_specs=[VM] * 3,
        out_specs=[VM] * 4,
        out_shape=[in_vmem((2, *PART))] * 4,
        compiler_params=params(2),
        name="sums",
    )(vmem(chosen), vmem(face), vmem(more))


def gather_kernel(a, b, c, d, kept, given):
    kept[...] = (a[0] + b[0]) + (c[0] + d[0])
    given[...] = (a[1] + b[1]) + (c[1] + d[1])


def gather(pairs):
    return pl.pallas_call(
        gather_kernel,
        in_specs=[VM] * 4,
        out_specs=[VM] * 2,
        out_shape=[in_vmem(PART)] * 2,
        compiler_params=params(2),
        name="gather",
    )(*[vmem(a) for a in pairs])


def product_kernel(kept, came, filters, out, sums):
    sums[...] = kept[...] + came[...]
    for p in range(4):
        view = jnp.concatenate([sums[:, p * 4 + i, :] for i in range(4)], axis=1)
        stacked = jnp.concatenate(pieces(view), axis=0)
        wide = jnp.dot(stacked, filters[p], preferred_element_type=F32)
        out[:, p, :] = wide[0:3] + (wide[3:6] + wide[6:9])


def product(parts, filters):
    return pl.pallas_call(
        product_kernel,
        in_specs=[VM] * 3,
        out_specs=VM,
        out_shape=jax.ShapeDtypeStruct((3, 4, 512), F32),
        scratch_shapes=[pltpu.VMEM(PART, F32)],
        compiler_params=params(4),
        name="product",
    )(*[vmem(a) for a in (*parts, filters)])


def shards(adjoint, velocity, viscosity, filters, block_tiles, tile_place):
    nx = lax.axis_size("gx")
    nz = lax.axis_size("gz")
    ring = [(i, (i + 1) % nz) for i in range(nz)]
    back = [(b, a) for a, b in ring]
    along = [(i, i + 1) for i in range(nx - 1)]
    against = [(b, a) for a, b in along]

    *state, zl, zr = pack(adjoint, velocity, viscosity)
    hl = lax.ppermute(zl, "gz", ring)
    hr = lax.ppermute(zr, "gz", back)
    face, mid, coef, centre, middle = face_call(state, hl, hr, zl, zr)

    got = [lax.ppermute(face, "gx", [(0, k)]) for k in (8, 2, 6)]
    mid, coef, done, chosen = inner(
        state, centre, middle, block_tiles.T, tile_place.reshape(1, -1), mid, coef
    )
    msg_lo, msg_hi = ship(state, centre)
    *got, mid, coef, done, msg_lo, msg_hi = lax.optimization_barrier(
        (*got, mid, coef, done, msg_lo, msg_hi)
    )
    face = join(face, *got)
    far = lax.ppermute(face, "gx", [(0, 4), (2, 10), (6, 14), (8, 12)])
    mid, coef, done, out, near = middle_call(state, centre, middle, mid, coef, done, filters)
    far, mid, coef, done = lax.optimization_barrier((far, mid, coef, done))
    face = join(face, far)
    other = lax.ppermute(face, "gx", [(i, i + 1) for i in range(0, nx, 2)])
    other, msg_lo, msg_hi = lax.optimization_barrier((other, msg_lo, msg_hi))
    low = lax.ppermute(msg_hi, "gx", along)
    high = lax.ppermute(msg_lo, "gx", against)
    own, *pairs = partial_sums(chosen, face, other)
    pairs = [own] + [
        lax.ppermute(pairs[k // 2 - 1], "gz", [(i, i ^ k) for i in range(nz)]) for k in (4, 2, 6)
    ]
    kept, given = gather(pairs)
    came = lax.ppermute(given, "gz", [(i, i ^ 1) for i in range(nz)])
    out = sides_call(state, centre, hl, hr, zl, zr, low, high, mid, coef, done, out)
    came, out = lax.optimization_barrier((came, out))
    gradient = product((kept, came), near).transpose(1, 0, 2)
    return out, gradient


def solution(mesh):
    placed = (
        P(None, "gx", None, "gz"),
        P(None, "gx", None, "gz"),
        P("gx", None, "gz"),
        P(("gx", "gz"), None, None),
        P(),
        P(),
    )
    return jax.shard_map(
        shards,
        mesh=mesh,
        in_specs=placed,
        out_specs=(P(None, "gx", None, "gz"), P(("gx", "gz"), None, None)),
        check_vma=False,
    )
```

```python
import jax
import jax.numpy as jnp
from jax import lax
from jax.experimental import pallas as pl
from jax.experimental.pallas import tpu as pltpu
from jax.sharding import PartitionSpec as P

F32 = jnp.float32
BF16 = jnp.bfloat16
ANY = pl.BlockSpec(memory_space=pl.ANY)
VM = pl.BlockSpec(memory_space=pltpu.VMEM)
MIB = 1024 * 1024
ROWS = 16
GROUPS = 4


def lanes(shape):
    return lax.broadcasted_iota(jnp.int32, shape, len(shape) - 1)


def roll(x, shift, axis):
    if isinstance(shift, int):
        shift = shift % x.shape[axis]
    return pltpu.roll(x, shift, axis)


def in_vmem(shape):
    return pltpu.VMEM(shape, F32)


STATE = {
    "adj": (3, 20, 144, 128),
    "visc": (20, 144, 128),
    "vel": (3, 18, 128, 128),
    "mid": (3, 18, 144, 128),
    "coef": (7, 18, 128, 128),
}


def cost(planes):
    return pl.CostEstimate(flops=planes * 3 * 16384 * 20, transcendentals=0, bytes_accessed=planes * 16384 * 4 * 22)


def params(mib):
    return pltpu.CompilerParams(vmem_limit_bytes=mib * MIB)


def hbm(x):
    return pltpu.with_memory_space_constraint(x, pltpu.HBM)


def vmem(x):
    return pltpu.with_memory_space_constraint(x, pltpu.VMEM)


def clear_walls(ref, lead):
    for index in lead:
        ref[(*index, pl.ds(0, 8), slice(None))] = jnp.zeros((8, 128), F32)
        ref[(*index, pl.ds(136, 8), slice(None))] = jnp.zeros((8, 128), F32)


def begin(copies, sems):
    started = [pltpu.make_async_copy(s, t, sems.at[i]) for i, (s, t) in enumerate(copies)]
    for copy in started:
        copy.start()
    return started


def even(axis):
    return lax.axis_index(axis) % 2 == 0


def in_order(axis, a, b):
    return jnp.where(even(axis), b, a), jnp.where(even(axis), a, b)


def pack_kernel(adj, vel, visc, adj_s, visc_s, vel_s, za, zb, msg_a, msg_b, *rest):
    acc_l, acc_r, vel_l, vel_r, sems = rest
    inside = pl.ds(8, 128)
    n = 16 // GROUPS

    def copies(g):
        xs = pl.ds(g * n, n)
        return (
            (adj.at[:, xs], adj_s.at[:, pl.ds(2 + g * n, n), inside]),
            (visc.at[xs], visc_s.at[pl.ds(2 + g * n, n), inside]),
            (vel.at[:, xs], vel_s.at[:, pl.ds(1 + g * n, n)]),
        )

    started = [begin(copies(g), sems.at[g]) for g in range(GROUPS)]
    clear_walls(adj_s, [(c, q) for c in range(3) for q in range(1, 20)])
    clear_walls(visc_s, [(q,) for q in range(1, 20)])
    zero = jnp.zeros((144, 128), F32)
    visc_s[1] = zero
    for c in range(3):
        adj_s[c, 1] = zero
    lane = lanes((32, 128))
    pair = lane >> 1
    pair_l = ((lane + 2) & 127) >> 1
    for g in range(GROUPS):
        for copy in started[g]:
            copy.wait()
        for r in range(4):
            rows = pl.ds(r * 32, 32)
            padded = pl.ds(8 + r * 32, 32)
            half = r // 2
            if g == 0:
                left = right = vleft = vright = jnp.zeros((32, 128), F32)
            else:
                left, right, vleft, vright = (ref[rows] for ref in (acc_l, acc_r, vel_l, vel_r))
            for c in range(4):
                for x in range(g * n, g * n + n):
                    m = c * 16 + x
                    plane = adj_s[c, x + 2, padded] if c < 3 else visc_s[x + 2, padded]
                    turned = roll(plane, 2 * m, 1)
                    right = jnp.where(pair == m, turned, right)
                    left = jnp.where(pair_l == m, turned, left)
            for d in range(3):
                for x in range(g * n, g * n + n):
                    at = 2 * (d * 16 + x) + half
                    turned = roll(vel_s[d, x + 1, rows], at, 1)
                    vright = jnp.where(lane == at, turned, vright)
                    vleft = jnp.where(lane == (at - 1) % 128, turned, vleft)
            if g < GROUPS - 1:
                acc_l[rows] = left
                acc_r[rows] = right
            else:
                zb[rows], za[rows] = in_order("gz", roll(left, 2, 1), right)
                vleft = roll(vleft, 1, 1)
            vel_l[rows] = vleft
            vel_r[rows] = vright
    near = jnp.where(even("gx"), 17, 2)
    for msg, q in ((msg_a, near), (msg_b, 19 - near)):
        for c in range(3):
            msg[c] = adj_s[c, q, inside]
        msg[3] = visc_s[q, inside]
    first = (lanes((64, 128)) & 1) == 0
    right = jnp.where(first, vel_r[pl.ds(0, 64)], vel_r[pl.ds(64, 64)])
    left = jnp.where(first, vel_l[pl.ds(0, 64)], vel_l[pl.ds(64, 64)])
    zb[pl.ds(128, 64)], za[pl.ds(128, 64)] = in_order("gz", left, right)


def pack(adj, vel, visc):
    return pl.pallas_call(
        pack_kernel,
        in_specs=[ANY, ANY, ANY],
        out_specs=[VM] * 7,
        out_shape=[in_vmem(STATE[k]) for k in ("adj", "visc", "vel")]
        + [in_vmem((192, 128))] * 2
        + [in_vmem((4, 128, 128))] * 2,
        scratch_shapes=[
            *[pltpu.VMEM((128, 128), F32)] * 4,
            pltpu.SemaphoreType.DMA((GROUPS, 3)),
        ],
        compiler_params=params(4),
        name="pack",
    )(hbm(adj), hbm(vel), hbm(visc))


def spread(a, group):
    kept = jnp.where((lanes(a.shape) >> 5) == group, a, 0.0)
    kept = kept + roll(kept, 32, 1)
    return kept + roll(kept, 64, 1)


def shift_rows(a, by):
    row = lax.broadcasted_iota(jnp.int32, a.shape, 0)
    moved = roll(a, by, 0)
    edge = 0 if by > 0 else a.shape[0] - 1
    return jnp.where(row == edge, 0.0, moved)


def edge_centre(hl, hr):
    odd = (lanes((128, 128)) & 1) == 1
    return jnp.where(odd, hl[:128], hr[:128])


def edge_velocity(message):
    both = message[128:]
    odd = (lanes(both.shape) & 1) == 1
    upper = jnp.where(odd, roll(both, 1, 1), both)
    lower = jnp.where(odd, both, roll(both, -1, 1))
    return jnp.concatenate([upper, lower], axis=0)


def edge_middle(hl, hr, zl, zr, low=None, high=None):
    lane = lanes((128, 128))
    odd = (lane & 1) == 1
    x = (lane >> 1) & 15
    left, right = hl[:128], hr[:128]
    centre = jnp.where(odd, left, right)
    minus = jnp.where(odd, roll(left, 1, 1), roll(zl[:128], -1, 1))
    plus = jnp.where(odd, roll(zr[:128], 1, 1), roll(right, -1, 1))
    velocity = jnp.where(odd, edge_velocity(hl), edge_velocity(hr))
    west = roll(centre, 2, 1)
    east = roll(centre, -2, 1)
    west = jnp.where(x == 0, 0.0 if low is None else roll(low, -30, 1), west)
    east = jnp.where(x == 15, 0.0 if high is None else roll(high, 30, 1), east)
    north = shift_rows(centre, -1)
    south = shift_rows(centre, 1)
    visc = spread(centre, 3)
    total = 0.0
    result = 0.0
    for d, (up, down) in enumerate(((east, west), (north, south), (plus, minus))):
        v = spread(velocity, d)
        a_up = 0.5 * ((visc + spread(up, 3)) + v)
        a_down = 0.5 * ((visc + spread(down, 3)) - v)
        total = total + (a_up + a_down)
        result = result + (a_up * up + a_down * down)
    return result + (1.0 - total) * centre


def ends(edge, r, m):
    return roll(edge[pl.ds(r, ROWS), :], 127 - 2 * m, 1)


def first_step(adj_s, visc_s, vel_s, mid_s, coef_s, edge, x, ex):
    lane = lanes((ROWS, 128))
    q, t = x + 2, x + 1
    for r in range(0, 128, ROWS):
        rows, here = pl.ds(r, ROWS), pl.ds(8 + r, ROWS)
        above, below = pl.ds(9 + r, ROWS), pl.ds(7 + r, ROWS)

        def sides(plane, m):
            end = ends(edge, r, m)
            up = jnp.where(lane == 127, end, roll(plane, -1, 1))
            return up, jnp.where(lane == 0, end, roll(plane, 1, 1))

        centre = visc_s[q, here, :]
        pairs = (
            (visc_s[q + 1, here, :], visc_s[q - 1, here, :]),
            (visc_s[q, above, :], visc_s[q, below, :]),
            sides(centre, 48 + ex),
        )
        a = []
        for d, (plus, minus) in enumerate(pairs):
            v = vel_s[d, t, rows, :]
            a.append(0.5 * ((centre + plus) + v))
            a.append(0.5 * ((centre + minus) - v))
        a.append(1.0 - (((a[0] + a[1]) + (a[2] + a[3])) + (a[4] + a[5])))
        for k in range(7):
            coef_s[k, t, rows, :] = a[k]
        for c in range(3):
            centre = adj_s[c, q, here, :]
            up, down = sides(centre, c * 16 + ex)
            out = a[6] * centre
            out = out + a[0] * adj_s[c, q + 1, here, :]
            out = out + a[1] * adj_s[c, q - 1, here, :]
            out = out + a[2] * adj_s[c, q, above, :]
            out = out + a[3] * adj_s[c, q, below, :]
            out = out + a[4] * up
            mid_s[c, t, here, :] = out + a[5] * down
    for c in range(3):
        mid_s[c, t, pl.ds(0, 8), :] = jnp.zeros((8, 128), F32)
        mid_s[c, t, pl.ds(136, 8), :] = jnp.zeros((8, 128), F32)


def second_step(mid_s, coef_s, edge, x, store):
    lane = lanes((ROWS, 128))
    t = x + 1
    for r in range(0, 128, ROWS):
        rows, here = pl.ds(r, ROWS), pl.ds(8 + r, ROWS)
        above, below = pl.ds(9 + r, ROWS), pl.ds(7 + r, ROWS)
        a = [coef_s[k, t, rows, :] for k in range(7)]
        for c in range(3):
            centre = mid_s[c, t, here, :]
            end = ends(edge, r, c * 16 + x)
            out = a[6] * centre
            out = out + a[0] * mid_s[c, t + 1, here, :]
            out = out + a[1] * mid_s[c, t - 1, here, :]
            out = out + a[2] * mid_s[c, t, above, :]
            out = out + a[3] * mid_s[c, t, below, :]
            out = out + a[4] * jnp.where(lane == 127, end, roll(centre, -1, 1))
            store(c, rows, out + a[5] * jnp.where(lane == 0, end, roll(centre, 1, 1)))


def face_kernel(
    adj_s, visc_s, vel_s, ra, rb, za, zb, face, mid_s, coef_s, centre, middle
):
    hl, hr = in_order("gz", ra[...], rb[...])
    zr, zl = in_order("gz", za[...], zb[...])
    centre[...] = edge_centre(hl, hr)
    middle[...] = edge_middle(hl, hr, zl, zr)
    for c in range(3):
        mid_s[c, 0] = jnp.zeros((144, 128), F32)
    for x in range(2):
        first_step(adj_s, visc_s, vel_s, mid_s, coef_s, centre, x, x)
    own = jnp.where(lax.axis_index("gx") == 0, 1.0, 0.0)

    def store(c, rows, v):
        face[c, rows, :] = v * own

    second_step(mid_s, coef_s, middle, 0, store)


def face_call(state, ha, hb, za, zb):
    return pl.pallas_call(
        face_kernel,
        in_specs=[VM] * 7,
        out_specs=[VM] * 5,
        out_shape=[
            in_vmem((3, 128, 128)),
            in_vmem(STATE["mid"]),
            in_vmem(STATE["coef"]),
            in_vmem((128, 128)),
            in_vmem((128, 128)),
        ],
        compiler_params=params(4),
        cost_estimate=cost(3),
        name="face",
    )(*[vmem(a) for a in (*state, ha, hb, za, zb)])


def choose(lists, place):
    gx, gz = lax.axis_index("gx"), lax.axis_index("gz")
    half = lists[:, pl.ds(pl.multiple_of((gz // 4) * 128, 128), 128)]
    tile = lax.broadcasted_iota(jnp.int32, (512, 128), 0)
    listed = jnp.zeros((512, 128), F32)
    for k in range(8):
        listed = listed + jnp.where(half[k : k + 1] == tile, 1.0, 0.0)
    row = lax.broadcasted_iota(jnp.int32, (128, 512), 0)
    wanted = gx * 32 + ((row >> 4) ^ gz) * 4 + ((row >> 2) & 3)
    sits = jnp.where(place[...] == wanted, 1.0, 0.0).astype(BF16)
    count = jnp.dot(sits, listed.astype(BF16), preferred_element_type=F32)
    row = lax.broadcasted_iota(jnp.int32, (128, 128), 0)
    column = lanes((128, 128))
    ours = jnp.where(row == (gz % 4) * 32 + (column >> 2), 1.0, 0.0).astype(BF16)
    wide = jnp.dot(count.astype(BF16), ours, preferred_element_type=F32)
    return jnp.where((row & 3) == (column & 3), wide, 0.0)


FIELD = (3, 16, 128, 128)


def run_first(cells, state, mid_s, coef_s, edge):
    for x in cells:
        first_step(*state, mid_s, coef_s, edge, x, x)


def run_second(cells, mid_s, coef_s, edge, done):
    for x in cells:

        def store(c, rows, v, x=x):
            done[c, x, rows, :] = v

        second_step(mid_s, coef_s, edge, x, store)


def inner_kernel(
    adj_i, visc_i, vel_s, centre, middle, lists, place, ra, rb, _, __,
    adj_s, visc_s, mid_s, coef_s, done, chosen, msg_a, msg_b,
):
    beyond = jnp.where(even("gx"), 18, 1)
    for msg, q in ((ra, beyond), (rb, 19 - beyond)):
        for c in range(3):
            adj_s[c, q, pl.ds(8, 128)] = msg[c]
        visc_s[q, pl.ds(8, 128)] = msg[3]
    state = (adj_s, visc_s, vel_s)
    run_first((0, 15), state, mid_s, coef_s, centre)
    near = jnp.where(even("gx"), 16, 1)
    for msg, t in ((msg_a, near), (msg_b, 17 - near)):
        for c in range(3):
            msg[c] = mid_s[c, t, pl.ds(8, 128)]
        msg[3] = centre[...]
    chosen[...] = choose(lists, place)
    run_first(range(2, 9), state, mid_s, coef_s, centre)
    run_second(range(1, 8), mid_s, coef_s, middle, done)


def inner(state, centre, middle, lists, place, ra, rb, mid, coef):
    return pl.pallas_call(
        inner_kernel,
        in_specs=[VM] * 11,
        out_specs=[VM] * 8,
        out_shape=[in_vmem(STATE[k]) for k in ("adj", "visc", "mid", "coef")]
        + [in_vmem(FIELD), in_vmem((128, 128))]
        + [in_vmem((4, 128, 128))] * 2,
        input_output_aliases={0: 0, 1: 1, 9: 2, 10: 3},
        compiler_params=params(4),
        cost_estimate=cost(16),
        name="inner",
    )(*[vmem(a) for a in (*state, centre, middle)], lists, place, *[vmem(a) for a in (ra, rb, mid, coef)])


def middle_kernel(
    adj_s, visc_s, vel_s, centre, middle, _, __, ___, filters, mid_s, coef_s, done, out, kept, sems
):
    started = begin([(done.at[:, pl.ds(1, 7)], out.at[:, pl.ds(1, 7)]), (filters, kept)], sems)
    run_first(range(9, 15), (adj_s, visc_s, vel_s), mid_s, coef_s, centre)
    run_second(range(8, 15), mid_s, coef_s, middle, done)
    for copy in started:
        copy.wait()


def middle_call(state, centre, middle, mid, coef, done, filters):
    held = [vmem(a) for a in (*state, centre, middle, mid, coef, done)]
    return pl.pallas_call(
        middle_kernel,
        in_specs=[VM] * 8 + [ANY],
        out_specs=[VM] * 3 + [ANY, VM],
        out_shape=[in_vmem(STATE["mid"]), in_vmem(STATE["coef"]), in_vmem(FIELD)]
        + [pltpu.HBM(FIELD, F32), pltpu.VMEM(filters.shape, BF16)],
        scratch_shapes=[pltpu.SemaphoreType.DMA((2,))],
        input_output_aliases={5: 0, 6: 1, 7: 2},
        compiler_params=params(4),
        cost_estimate=cost(12),
        name="middle",
    )(*held, hbm(filters))


def last_kernel(
    ha, hb, za, zb, ra, rb, _, coef_s, __, ___, mid_s, done, out, edges, sems
):
    copies = [
        pltpu.make_async_copy(done.at[:, pl.ds(x, n)], out.at[:, pl.ds(x, n)], sems.at[i])
        for i, (x, n) in enumerate(((8, 7), (0, 1), (15, 1)))
    ]
    copies[0].start()
    hl, hr = in_order("gz", ha[...], hb[...])
    zr, zl = in_order("gz", za[...], zb[...])
    low, high = in_order("gx", ra[3], rb[3])
    edges[...] = edge_middle(hl, hr, zl, zr, low, high)
    beyond = jnp.where(even("gx"), 17, 0)
    for msg, t in ((ra, beyond), (rb, 17 - beyond)):
        for c in range(3):
            mid_s[c, t, pl.ds(8, 128)] = msg[c]
    for i, x in ((1, 0), (2, 15)):
        run_second((x,), mid_s, coef_s, edges, done)
        copies[i].start()
    for copy in copies:
        copy.wait()


def last_call(ha, hb, za, zb, ra, rb, mid, coef, done, out):
    held = [vmem(a) for a in (ha, hb, za, zb, ra, rb, mid, coef, done)]
    return pl.pallas_call(
        last_kernel,
        in_specs=[VM] * 9 + [ANY],
        out_specs=[VM] * 2 + [ANY],
        out_shape=[in_vmem(STATE["mid"]), in_vmem(FIELD), pltpu.HBM(FIELD, F32)],
        scratch_shapes=[pltpu.VMEM((128, 128), F32), pltpu.SemaphoreType.DMA((3,))],
        input_output_aliases={6: 0, 8: 1, 9: 2},
        compiler_params=params(4),
        cost_estimate=cost(4),
        name="last",
    )(*held, hbm(out))[-1]


def join_kernel(*refs):
    total = refs[0][...]
    for ref in refs[1:-1]:
        total = total + ref[...]
    refs[-1][...] = total


def join(*parts):
    return pl.pallas_call(
        join_kernel,
        in_specs=[VM] * len(parts),
        out_specs=VM,
        out_shape=in_vmem(parts[0].shape),
        compiler_params=params(2),
        name="join",
    )(*[vmem(a) for a in parts])


def pieces(a):
    high = a.astype(BF16)
    rest = a - high.astype(F32)
    mid = rest.astype(BF16)
    low = (rest - mid.astype(F32)).astype(BF16)
    return high, mid, low


PART = (3, 16, 128)


def sums_kernel(chosen, face, more, *pairs):
    matrix = chosen[...].astype(BF16)
    for c in range(3):
        total = 0.0
        for piece in pieces(face[c] + more[c]):
            total = total + jnp.dot(matrix, piece, preferred_element_type=F32)
        for k in range(8):
            pairs[k // 2][k % 2, c] = total[k * 16 : k * 16 + 16]


def partial_sums(chosen, face, more):
    return pl.pallas_call(
        sums_kernel,
        in_specs=[VM] * 3,
        out_specs=[VM] * 4,
        out_shape=[in_vmem((2, *PART))] * 4,
        compiler_params=params(2),
        name="sums",
    )(vmem(chosen), vmem(face), vmem(more))


def gather_kernel(a, b, c, d, kept, given):
    kept[...] = (a[0] + b[0]) + (c[0] + d[0])
    given[...] = (a[1] + b[1]) + (c[1] + d[1])


def gather(pairs):
    return pl.pallas_call(
        gather_kernel,
        in_specs=[VM] * 4,
        out_specs=[VM] * 2,
        out_shape=[in_vmem(PART)] * 2,
        compiler_params=params(2),
        name="gather",
    )(*[vmem(a) for a in pairs])


def product_kernel(kept, came, filters, out, sums):
    sums[...] = kept[...] + came[...]
    for p in range(4):
        view = jnp.concatenate([sums[:, p * 4 + i, :] for i in range(4)], axis=1)
        stacked = jnp.concatenate(pieces(view), axis=0)
        wide = jnp.dot(stacked, filters[p], preferred_element_type=F32)
        out[:, p, :] = wide[0:3] + (wide[3:6] + wide[6:9])


def product(parts, filters):
    return pl.pallas_call(
        product_kernel,
        in_specs=[VM] * 3,
        out_specs=VM,
        out_shape=jax.ShapeDtypeStruct((3, 4, 512), F32),
        scratch_shapes=[pltpu.VMEM(PART, F32)],
        compiler_params=params(4),
        name="product",
    )(*[vmem(a) for a in (*parts, filters)])


def shards(adjoint, velocity, viscosity, filters, block_tiles, tile_place):
    nx = lax.axis_size("gx")
    nz = lax.axis_size("gz")
    inside_z = [(i, i ^ 1) for i in range(nz)]
    across_z = [(i, (i + 1 if i % 2 else i - 1) % nz) for i in range(nz)]
    inside_x = [(i, i ^ 1) for i in range(nx)]
    across_x = [(i, i + 1 if i % 2 else i - 1) for i in range(1, nx - 1)]

    *state, za, zb, msg_a, msg_b = pack(adjoint, velocity, viscosity)
    ha = lax.ppermute(za, "gz", inside_z)
    hb = lax.ppermute(zb, "gz", across_z)
    ha, hb, msg_a, msg_b = lax.optimization_barrier((ha, hb, msg_a, msg_b))
    ra = lax.ppermute(msg_a, "gx", inside_x)
    rb = lax.ppermute(msg_b, "gx", across_x)
    face, mid, coef, centre, middle = face_call(state, ha, hb, za, zb)

    got = [lax.ppermute(face, "gx", [(0, k)]) for k in (8, 2, 6)]
    adj, visc, mid, coef, done, chosen, msg_a, msg_b = inner(
        state, centre, middle, block_tiles.T, tile_place.reshape(1, -1), ra, rb, mid, coef
    )
    *got, mid, coef, done = lax.optimization_barrier((*got, mid, coef, done))
    face = join(face, *got)
    far = lax.ppermute(face, "gx", [(0, 4), (2, 10), (6, 14), (8, 12)])
    mid, coef, done, out, near = middle_call(
        (adj, visc, state[2]), centre, middle, mid, coef, done, filters
    )
    far, mid, coef, done = lax.optimization_barrier((far, mid, coef, done))
    face = join(face, far)
    other = lax.ppermute(face, "gx", [(i, i + 1) for i in range(0, nx, 2)])
    other, msg_a, msg_b = lax.optimization_barrier((other, msg_a, msg_b))
    ra = lax.ppermute(msg_a, "gx", inside_x)
    rb = lax.ppermute(msg_b, "gx", across_x)
    own, *pairs = partial_sums(chosen, face, other)
    pairs = [
        lax.ppermute(pairs[k // 2 - 1], "gz", [(i, i ^ k) for i in range(nz)]) for k in (4, 2, 6)
    ]
    kept, given = gather((own, *pairs))
    came = lax.ppermute(given, "gz", inside_z)
    out = last_call(ha, hb, za, zb, ra, rb, mid, coef, done, out)
    came, out = lax.optimization_barrier((came, out))
    gradient = product((kept, came), near).transpose(1, 0, 2)
    return out, gradient


def solution(mesh):
    placed = (
        P(None, "gx", None, "gz"),
        P(None, "gx", None, "gz"),
        P("gx", None, "gz"),
        P(("gx", "gz"), None, None),
        P(),
        P(),
    )
    return jax.shard_map(
        shards,
        mesh=mesh,
        in_specs=placed,
        out_specs=(P(None, "gx", None, "gz"), P(("gx", "gz"), None, None)),
        check_vma=False,
    )
```

```python
import jax
import jax.numpy as jnp
from jax import lax
from jax.experimental import pallas as pl
from jax.experimental.pallas import tpu as pltpu
from jax.sharding import PartitionSpec as P

F32 = jnp.float32
BF16 = jnp.bfloat16
ANY = pl.BlockSpec(memory_space=pl.ANY)
VM = pl.BlockSpec(memory_space=pltpu.VMEM)
MIB = 1024 * 1024
ROWS = 16
GROUPS = 4


def lanes(shape):
    return lax.broadcasted_iota(jnp.int32, shape, len(shape) - 1)


def roll(x, shift, axis):
    if isinstance(shift, int):
        shift = shift % x.shape[axis]
    return pltpu.roll(x, shift, axis)


def in_vmem(shape):
    return pltpu.VMEM(shape, F32)


STATE = {
    "adj": (3, 20, 144, 128),
    "visc": (20, 144, 128),
    "vel": (3, 18, 128, 128),
    "mid": (3, 18, 144, 128),
    "coef": (7, 18, 128, 128),
}


def cost(planes):
    return pl.CostEstimate(flops=planes * 3 * 16384 * 20, transcendentals=0, bytes_accessed=planes * 16384 * 4 * 22)


def params(mib):
    return pltpu.CompilerParams(vmem_limit_bytes=mib * MIB)


def hbm(x):
    return pltpu.with_memory_space_constraint(x, pltpu.HBM)


def vmem(x):
    return pltpu.with_memory_space_constraint(x, pltpu.VMEM)


def clear_walls(ref, lead):
    for index in lead:
        ref[(*index, pl.ds(0, 8), slice(None))] = jnp.zeros((8, 128), F32)
        ref[(*index, pl.ds(136, 8), slice(None))] = jnp.zeros((8, 128), F32)


def begin(copies, sems):
    started = [pltpu.make_async_copy(s, t, sems.at[i]) for i, (s, t) in enumerate(copies)]
    for copy in started:
        copy.start()
    return started


def even(axis):
    return lax.axis_index(axis) % 2 == 0


def in_order(axis, a, b):
    return jnp.where(even(axis), b, a), jnp.where(even(axis), a, b)


def pack_kernel(adj, vel, visc, adj_s, visc_s, vel_s, za, zb, msg_a, msg_b, *rest):
    acc_l, acc_r, vel_l, vel_r, sems = rest
    inside = pl.ds(8, 128)
    n = 16 // GROUPS

    def copies(g):
        xs = pl.ds(g * n, n)
        return (
            (adj.at[:, xs], adj_s.at[:, pl.ds(2 + g * n, n), inside]),
            (visc.at[xs], visc_s.at[pl.ds(2 + g * n, n), inside]),
            (vel.at[:, xs], vel_s.at[:, pl.ds(1 + g * n, n)]),
        )

    started = [begin(copies(g), sems.at[g]) for g in range(GROUPS)]
    clear_walls(adj_s, [(c, q) for c in range(3) for q in range(1, 20)])
    clear_walls(visc_s, [(q,) for q in range(1, 20)])
    zero = jnp.zeros((144, 128), F32)
    visc_s[1] = zero
    for c in range(3):
        adj_s[c, 1] = zero
    lane = lanes((32, 128))
    pair = lane >> 1
    pair_l = ((lane + 2) & 127) >> 1
    for g in range(GROUPS):
        for copy in started[g]:
            copy.wait()
        for r in range(4):
            rows = pl.ds(r * 32, 32)
            padded = pl.ds(8 + r * 32, 32)
            half = r // 2
            if g == 0:
                left = right = vleft = vright = jnp.zeros((32, 128), F32)
            else:
                left, right, vleft, vright = (ref[rows] for ref in (acc_l, acc_r, vel_l, vel_r))
            for c in range(4):
                for x in range(g * n, g * n + n):
                    m = c * 16 + x
                    plane = adj_s[c, x + 2, padded] if c < 3 else visc_s[x + 2, padded]
                    turned = roll(plane, 2 * m, 1)
                    right = jnp.where(pair == m, turned, right)
                    left = jnp.where(pair_l == m, turned, left)
            for d in range(3):
                for x in range(g * n, g * n + n):
                    at = 2 * (d * 16 + x) + half
                    turned = roll(vel_s[d, x + 1, rows], at, 1)
                    vright = jnp.where(lane == at, turned, vright)
                    vleft = jnp.where(lane == (at - 1) % 128, turned, vleft)
            if g < GROUPS - 1:
                acc_l[rows] = left
                acc_r[rows] = right
            else:
                zb[rows], za[rows] = in_order("gz", roll(left, 2, 1), right)
                vleft = roll(vleft, 1, 1)
            vel_l[rows] = vleft
            vel_r[rows] = vright
    near = jnp.where(even("gx"), 17, 2)
    for msg, q in ((msg_a, near), (msg_b, 19 - near)):
        for c in range(3):
            msg[c] = adj_s[c, q, inside]
        msg[3] = visc_s[q, inside]
    first = (lanes((64, 128)) & 1) == 0
    right = jnp.where(first, vel_r[pl.ds(0, 64)], vel_r[pl.ds(64, 64)])
    left = jnp.where(first, vel_l[pl.ds(0, 64)], vel_l[pl.ds(64, 64)])
    zb[pl.ds(128, 64)], za[pl.ds(128, 64)] = in_order("gz", left, right)


def pack(adj, vel, visc):
    return pl.pallas_call(
        pack_kernel,
        in_specs=[ANY, ANY, ANY],
        out_specs=[VM] * 7,
        out_shape=[in_vmem(STATE[k]) for k in ("adj", "visc", "vel")]
        + [in_vmem((192, 128))] * 2
        + [in_vmem((4, 128, 128))] * 2,
        scratch_shapes=[
            *[pltpu.VMEM((128, 128), F32)] * 4,
            pltpu.SemaphoreType.DMA((GROUPS, 3)),
        ],
        compiler_params=params(4),
        name="pack",
    )(hbm(adj), hbm(vel), hbm(visc))


def spread(a, group):
    kept = jnp.where((lanes(a.shape) >> 5) == group, a, 0.0)
    kept = kept + roll(kept, 32, 1)
    return kept + roll(kept, 64, 1)


def shift_rows(a, by):
    row = lax.broadcasted_iota(jnp.int32, a.shape, 0)
    moved = roll(a, by, 0)
    edge = 0 if by > 0 else a.shape[0] - 1
    return jnp.where(row == edge, 0.0, moved)


def edge_centre(hl, hr):
    odd = (lanes((128, 128)) & 1) == 1
    return jnp.where(odd, hl[:128], hr[:128])


def edge_velocity(message):
    both = message[128:]
    odd = (lanes(both.shape) & 1) == 1
    upper = jnp.where(odd, roll(both, 1, 1), both)
    lower = jnp.where(odd, both, roll(both, -1, 1))
    return jnp.concatenate([upper, lower], axis=0)


def edge_middle(hl, hr, zl, zr, low=None, high=None):
    lane = lanes((128, 128))
    odd = (lane & 1) == 1
    x = (lane >> 1) & 15
    left, right = hl[:128], hr[:128]
    centre = jnp.where(odd, left, right)
    minus = jnp.where(odd, roll(left, 1, 1), roll(zl[:128], -1, 1))
    plus = jnp.where(odd, roll(zr[:128], 1, 1), roll(right, -1, 1))
    velocity = jnp.where(odd, edge_velocity(hl), edge_velocity(hr))
    west = roll(centre, 2, 1)
    east = roll(centre, -2, 1)
    west = jnp.where(x == 0, 0.0 if low is None else roll(low, -30, 1), west)
    east = jnp.where(x == 15, 0.0 if high is None else roll(high, 30, 1), east)
    north = shift_rows(centre, -1)
    south = shift_rows(centre, 1)
    visc = spread(centre, 3)
    total = 0.0
    result = 0.0
    for d, (up, down) in enumerate(((east, west), (north, south), (plus, minus))):
        v = spread(velocity, d)
        a_up = 0.5 * ((visc + spread(up, 3)) + v)
        a_down = 0.5 * ((visc + spread(down, 3)) - v)
        total = total + (a_up + a_down)
        result = result + (a_up * up + a_down * down)
    return result + (1.0 - total) * centre


def ends(edge, r, m):
    return roll(edge[pl.ds(r, ROWS), :], 127 - 2 * m, 1)


def first_step(adj_s, visc_s, vel_s, mid_s, coef_s, edge, x, ex):
    lane = lanes((ROWS, 128))
    q, t = x + 2, x + 1
    for r in range(0, 128, ROWS):
        rows, here = pl.ds(r, ROWS), pl.ds(8 + r, ROWS)
        above, below = pl.ds(9 + r, ROWS), pl.ds(7 + r, ROWS)

        def sides(plane, m):
            end = ends(edge, r, m)
            up = jnp.where(lane == 127, end, roll(plane, -1, 1))
            return up, jnp.where(lane == 0, end, roll(plane, 1, 1))

        centre = visc_s[q, here, :]
        pairs = (
            (visc_s[q + 1, here, :], visc_s[q - 1, here, :]),
            (visc_s[q, above, :], visc_s[q, below, :]),
            sides(centre, 48 + ex),
        )
        a = []
        for d, (plus, minus) in enumerate(pairs):
            v = vel_s[d, t, rows, :]
            a.append(0.5 * ((centre + plus) + v))
            a.append(0.5 * ((centre + minus) - v))
        a.append(1.0 - (((a[0] + a[1]) + (a[2] + a[3])) + (a[4] + a[5])))
        for k in range(7):
            coef_s[k, t, rows, :] = a[k]
        for c in range(3):
            centre = adj_s[c, q, here, :]
            up, down = sides(centre, c * 16 + ex)
            out = a[6] * centre
            out = out + a[0] * adj_s[c, q + 1, here, :]
            out = out + a[1] * adj_s[c, q - 1, here, :]
            out = out + a[2] * adj_s[c, q, above, :]
            out = out + a[3] * adj_s[c, q, below, :]
            out = out + a[4] * up
            mid_s[c, t, here, :] = out + a[5] * down
    for c in range(3):
        mid_s[c, t, pl.ds(0, 8), :] = jnp.zeros((8, 128), F32)
        mid_s[c, t, pl.ds(136, 8), :] = jnp.zeros((8, 128), F32)


def second_step(mid_s, coef_s, edge, x, store):
    lane = lanes((ROWS, 128))
    t = x + 1
    for r in range(0, 128, ROWS):
        rows, here = pl.ds(r, ROWS), pl.ds(8 + r, ROWS)
        above, below = pl.ds(9 + r, ROWS), pl.ds(7 + r, ROWS)
        a = [coef_s[k, t, rows, :] for k in range(7)]
        for c in range(3):
            centre = mid_s[c, t, here, :]
            end = ends(edge, r, c * 16 + x)
            out = a[6] * centre
            out = out + a[0] * mid_s[c, t + 1, here, :]
            out = out + a[1] * mid_s[c, t - 1, here, :]
            out = out + a[2] * mid_s[c, t, above, :]
            out = out + a[3] * mid_s[c, t, below, :]
            out = out + a[4] * jnp.where(lane == 127, end, roll(centre, -1, 1))
            store(c, rows, out + a[5] * jnp.where(lane == 0, end, roll(centre, 1, 1)))


def face_kernel(
    adj_s, visc_s, vel_s, ra, rb, za, zb, face, mid_s, coef_s, centre, middle
):
    hl, hr = in_order("gz", ra[...], rb[...])
    zr, zl = in_order("gz", za[...], zb[...])
    centre[...] = edge_centre(hl, hr)
    middle[...] = edge_middle(hl, hr, zl, zr)
    for c in range(3):
        mid_s[c, 0] = jnp.zeros((144, 128), F32)
    for x in range(2):
        first_step(adj_s, visc_s, vel_s, mid_s, coef_s, centre, x, x)
    own = jnp.where(lax.axis_index("gx") == 0, 1.0, 0.0)

    def store(c, rows, v):
        face[c, rows, :] = v * own

    second_step(mid_s, coef_s, middle, 0, store)


def face_call(state, ha, hb, za, zb):
    return pl.pallas_call(
        face_kernel,
        in_specs=[VM] * 7,
        out_specs=[VM] * 5,
        out_shape=[
            in_vmem((3, 128, 128)),
            in_vmem(STATE["mid"]),
            in_vmem(STATE["coef"]),
            in_vmem((128, 128)),
            in_vmem((128, 128)),
        ],
        compiler_params=params(4),
        cost_estimate=cost(3),
        name="face",
    )(*[vmem(a) for a in (*state, ha, hb, za, zb)])


def choose(lists, place):
    gx, gz = lax.axis_index("gx"), lax.axis_index("gz")
    half = lists[:, pl.ds(pl.multiple_of((gz // 4) * 128, 128), 128)]
    tile = lax.broadcasted_iota(jnp.int32, (512, 128), 0)
    listed = jnp.zeros((512, 128), F32)
    for k in range(8):
        listed = listed + jnp.where(half[k : k + 1] == tile, 1.0, 0.0)
    row = lax.broadcasted_iota(jnp.int32, (128, 512), 0)
    wanted = gx * 32 + ((row >> 4) ^ gz) * 4 + ((row >> 2) & 3)
    sits = jnp.where(place[...] == wanted, 1.0, 0.0).astype(BF16)
    count = jnp.dot(sits, listed.astype(BF16), preferred_element_type=F32)
    row = lax.broadcasted_iota(jnp.int32, (128, 128), 0)
    column = lanes((128, 128))
    ours = jnp.where(row == (gz % 4) * 32 + (column >> 2), 1.0, 0.0).astype(BF16)
    wide = jnp.dot(count.astype(BF16), ours, preferred_element_type=F32)
    return jnp.where((row & 3) == (column & 3), wide, 0.0)


FIELD = (3, 16, 128, 128)


def run_first(cells, state, mid_s, coef_s, edge):
    for x in cells:
        first_step(*state, mid_s, coef_s, edge, x, x)


def run_second(cells, mid_s, coef_s, edge, done):
    for x in cells:

        def store(c, rows, v, x=x):
            done[c, x, rows, :] = v

        second_step(mid_s, coef_s, edge, x, store)


def inner_kernel(
    adj_s, visc_s, vel_s, centre, middle, lists, place, _, __, mid_s, coef_s, done, chosen
):
    chosen[...] = choose(lists, place)
    run_first(range(2, 9), (adj_s, visc_s, vel_s), mid_s, coef_s, centre)
    run_second(range(2, 8), mid_s, coef_s, middle, done)


def inner(state, centre, middle, lists, place, mid, coef):
    return pl.pallas_call(
        inner_kernel,
        in_specs=[VM] * 9,
        out_specs=[VM] * 4,
        out_shape=[in_vmem(STATE["mid"]), in_vmem(STATE["coef"]), in_vmem(FIELD), in_vmem((128, 128))],
        input_output_aliases={7: 0, 8: 1},
        compiler_params=params(4),
        cost_estimate=cost(13),
        name="inner",
    )(*[vmem(a) for a in (*state, centre, middle)], lists, place, *[vmem(a) for a in (mid, coef)])


def ends_kernel(
    adj_i, visc_i, vel_s, centre, middle, ra, rb, _, __, ___, ____,
    adj_s, visc_s, mid_s, coef_s, done, out, msg_a, msg_b, sems,
):
    started = begin([(done.at[:, pl.ds(8, 6)], out.at[:, pl.ds(8, 6)])], sems)
    beyond = jnp.where(even("gx"), 18, 1)
    for msg, q in ((ra, beyond), (rb, 19 - beyond)):
        for c in range(3):
            adj_s[c, q, pl.ds(8, 128)] = msg[c]
        visc_s[q, pl.ds(8, 128)] = msg[3]
    run_first((0, 15), (adj_s, visc_s, vel_s), mid_s, coef_s, centre)
    near = jnp.where(even("gx"), 16, 1)
    for msg, t in ((msg_a, near), (msg_b, 17 - near)):
        for c in range(3):
            msg[c] = mid_s[c, t, pl.ds(8, 128)]
        msg[3] = centre[...]
    run_second((1, 14), mid_s, coef_s, middle, done)
    for copy in started:
        copy.wait()


def ends_call(state, centre, middle, ra, rb, mid, coef, done, out):
    held = [vmem(a) for a in (*state, centre, middle, ra, rb, mid, coef, done)]
    return pl.pallas_call(
        ends_kernel,
        in_specs=[VM] * 10 + [ANY],
        out_specs=[VM] * 5 + [ANY, VM, VM],
        out_shape=[in_vmem(STATE[k]) for k in ("adj", "visc", "mid", "coef")]
        + [in_vmem(FIELD), pltpu.HBM(FIELD, F32)]
        + [in_vmem((4, 128, 128))] * 2,
        scratch_shapes=[pltpu.SemaphoreType.DMA((1,))],
        input_output_aliases={0: 0, 1: 1, 7: 2, 8: 3, 9: 4, 10: 5},
        compiler_params=params(4),
        cost_estimate=cost(4),
        name="ends",
    )(*held, hbm(out))[2:]


def middle_kernel(
    adj_s, visc_s, vel_s, centre, middle, _, __, ___, filters, mid_s, coef_s, done, out, kept, sems
):
    started = begin([(done.at[:, pl.ds(2, 6)], out.at[:, pl.ds(2, 6)]), (filters, kept)], sems)
    run_first(range(9, 15), (adj_s, visc_s, vel_s), mid_s, coef_s, centre)
    run_second(range(8, 14), mid_s, coef_s, middle, done)
    for copy in started:
        copy.wait()


def middle_call(state, centre, middle, mid, coef, done, filters):
    held = [vmem(a) for a in (*state, centre, middle, mid, coef, done)]
    return pl.pallas_call(
        middle_kernel,
        in_specs=[VM] * 8 + [ANY],
        out_specs=[VM] * 3 + [ANY, VM],
        out_shape=[in_vmem(STATE["mid"]), in_vmem(STATE["coef"]), in_vmem(FIELD)]
        + [pltpu.HBM(FIELD, F32), pltpu.VMEM(filters.shape, BF16)],
        scratch_shapes=[pltpu.SemaphoreType.DMA((2,))],
        input_output_aliases={5: 0, 6: 1, 7: 2},
        compiler_params=params(4),
        cost_estimate=cost(12),
        name="middle",
    )(*held, hbm(filters))


def last_kernel(
    ha, hb, za, zb, ra, rb, _, coef_s, __, ___, mid_s, done, out, edges, sems
):
    copies = [
        pltpu.make_async_copy(done.at[:, pl.ds(x, n)], out.at[:, pl.ds(x, n)], sems.at[i])
        for i, (x, n) in enumerate(((1, 1), (14, 1), (0, 1), (15, 1)))
    ]
    copies[0].start()
    copies[1].start()
    hl, hr = in_order("gz", ha[...], hb[...])
    zr, zl = in_order("gz", za[...], zb[...])
    low, high = in_order("gx", ra[3], rb[3])
    edges[...] = edge_middle(hl, hr, zl, zr, low, high)
    beyond = jnp.where(even("gx"), 17, 0)
    for msg, t in ((ra, beyond), (rb, 17 - beyond)):
        for c in range(3):
            mid_s[c, t, pl.ds(8, 128)] = msg[c]
    for i, x in ((2, 0), (3, 15)):
        run_second((x,), mid_s, coef_s, edges, done)
        copies[i].start()
    for copy in copies:
        copy.wait()


def last_call(ha, hb, za, zb, ra, rb, mid, coef, done, out):
    held = [vmem(a) for a in (ha, hb, za, zb, ra, rb, mid, coef, done)]
    return pl.pallas_call(
        last_kernel,
        in_specs=[VM] * 9 + [ANY],
        out_specs=[VM] * 2 + [ANY],
        out_shape=[in_vmem(STATE["mid"]), in_vmem(FIELD), pltpu.HBM(FIELD, F32)],
        scratch_shapes=[pltpu.VMEM((128, 128), F32), pltpu.SemaphoreType.DMA((4,))],
        input_output_aliases={6: 0, 8: 1, 9: 2},
        compiler_params=params(4),
        cost_estimate=cost(4),
        name="last",
    )(*held, hbm(out))[-1]


def join_kernel(*refs):
    total = refs[0][...]
    for ref in refs[1:-1]:
        total = total + ref[...]
    refs[-1][...] = total


def join(*parts):
    return pl.pallas_call(
        join_kernel,
        in_specs=[VM] * len(parts),
        out_specs=VM,
        out_shape=in_vmem(parts[0].shape),
        compiler_params=params(2),
        name="join",
    )(*[vmem(a) for a in parts])


def pieces(a):
    high = a.astype(BF16)
    rest = a - high.astype(F32)
    mid = rest.astype(BF16)
    low = (rest - mid.astype(F32)).astype(BF16)
    return high, mid, low


PART = (3, 16, 128)


def sums_kernel(chosen, face, more, *pairs):
    matrix = chosen[...].astype(BF16)
    for c in range(3):
        total = 0.0
        for piece in pieces(face[c] + more[c]):
            total = total + jnp.dot(matrix, piece, preferred_element_type=F32)
        for k in range(8):
            pairs[k // 2][k % 2, c] = total[k * 16 : k * 16 + 16]


def partial_sums(chosen, face, more):
    return pl.pallas_call(
        sums_kernel,
        in_specs=[VM] * 3,
        out_specs=[VM] * 4,
        out_shape=[in_vmem((2, *PART))] * 4,
        compiler_params=params(2),
        name="sums",
    )(vmem(chosen), vmem(face), vmem(more))


def gather_kernel(a, b, c, d, kept, given):
    kept[...] = (a[0] + b[0]) + (c[0] + d[0])
    given[...] = (a[1] + b[1]) + (c[1] + d[1])


def gather(pairs):
    return pl.pallas_call(
        gather_kernel,
        in_specs=[VM] * 4,
        out_specs=[VM] * 2,
        out_shape=[in_vmem(PART)] * 2,
        compiler_params=params(2),
        name="gather",
    )(*[vmem(a) for a in pairs])


def product_kernel(kept, came, filters, out, sums):
    sums[...] = kept[...] + came[...]
    for p in range(4):
        view = jnp.concatenate([sums[:, p * 4 + i, :] for i in range(4)], axis=1)
        stacked = jnp.concatenate(pieces(view), axis=0)
        wide = jnp.dot(stacked, filters[p], preferred_element_type=F32)
        out[:, p, :] = wide[0:3] + (wide[3:6] + wide[6:9])


def product(parts, filters):
    return pl.pallas_call(
        product_kernel,
        in_specs=[VM] * 3,
        out_specs=VM,
        out_shape=jax.ShapeDtypeStruct((3, 4, 512), F32),
        scratch_shapes=[pltpu.VMEM(PART, F32)],
        compiler_params=params(4),
        name="product",
    )(*[vmem(a) for a in (*parts, filters)])


def shards(adjoint, velocity, viscosity, filters, block_tiles, tile_place):
    nx = lax.axis_size("gx")
    nz = lax.axis_size("gz")
    inside_z = [(i, i ^ 1) for i in range(nz)]
    across_z = [(i, (i + 1 if i % 2 else i - 1) % nz) for i in range(nz)]
    inside_x = [(i, i ^ 1) for i in range(nx)]
    across_x = [(i, i + 1 if i % 2 else i - 1) for i in range(1, nx - 1)]

    *state, za, zb, msg_a, msg_b = pack(adjoint, velocity, viscosity)
    ha = lax.ppermute(za, "gz", inside_z)
    hb = lax.ppermute(zb, "gz", across_z)
    face, mid, coef, centre, middle = face_call(state, ha, hb, za, zb)

    face, msg_a, msg_b = lax.optimization_barrier((face, msg_a, msg_b))
    ra = lax.ppermute(msg_a, "gx", inside_x)
    rb = lax.ppermute(msg_b, "gx", across_x)
    got = [lax.ppermute(face, "gx", [(0, k)]) for k in (8, 2, 6)]
    mid, coef, done, chosen = inner(
        state, centre, middle, block_tiles.T, tile_place.reshape(1, -1), mid, coef
    )
    *got, mid, coef, done = lax.optimization_barrier((*got, mid, coef, done))
    face = join(face, *got)
    far = lax.ppermute(face, "gx", [(0, 4), (2, 10), (6, 14), (8, 12)])
    mid, coef, done, out, near = middle_call(state, centre, middle, mid, coef, done, filters)
    far, mid, coef, done, ra, rb = lax.optimization_barrier((far, mid, coef, done, ra, rb))
    face = join(face, far)
    other = lax.ppermute(face, "gx", [(i, i + 1) for i in range(0, nx, 2)])
    mid, coef, done, out, msg_a, msg_b = ends_call(
        state, centre, middle, ra, rb, mid, coef, done, out
    )
    other, mid, coef, done, msg_a, msg_b = lax.optimization_barrier(
        (other, mid, coef, done, msg_a, msg_b)
    )
    ra = lax.ppermute(msg_a, "gx", inside_x)
    rb = lax.ppermute(msg_b, "gx", across_x)
    own, *pairs = partial_sums(chosen, face, other)
    pairs = [
        lax.ppermute(pairs[k // 2 - 1], "gz", [(i, i ^ k) for i in range(nz)]) for k in (4, 2, 6)
    ]
    kept, given = gather((own, *pairs))
    came = lax.ppermute(given, "gz", inside_z)
    out = last_call(ha, hb, za, zb, ra, rb, mid, coef, done, out)
    came, out = lax.optimization_barrier((came, out))
    gradient = product((kept, came), near).transpose(1, 0, 2)
    return out, gradient


def solution(mesh):
    placed = (
        P(None, "gx", None, "gz"),
        P(None, "gx", None, "gz"),
        P("gx", None, "gz"),
        P(("gx", "gz"), None, None),
        P(),
        P(),
    )
    return jax.shard_map(
        shards,
        mesh=mesh,
        in_specs=placed,
        out_specs=(P(None, "gx", None, "gz"), P(("gx", "gz"), None, None)),
        check_vma=False,
    )
```

```python
import jax
import jax.numpy as jnp
from jax import lax
from jax.experimental import pallas as pl
from jax.experimental.pallas import tpu as pltpu
from jax.sharding import PartitionSpec as P

F32 = jnp.float32
BF16 = jnp.bfloat16
ANY = pl.BlockSpec(memory_space=pl.ANY)
VM = pl.BlockSpec(memory_space=pltpu.VMEM)
MIB = 1024 * 1024
ROWS = 16
GROUPS = 4


def lanes(shape):
    return lax.broadcasted_iota(jnp.int32, shape, len(shape) - 1)


def roll(x, shift, axis):
    if isinstance(shift, int):
        shift = shift % x.shape[axis]
    return pltpu.roll(x, shift, axis)


def in_vmem(shape):
    return pltpu.VMEM(shape, F32)


STATE = {
    "adj": (3, 20, 144, 128),
    "visc": (20, 144, 128),
    "vel": (3, 18, 128, 128),
    "mid": (3, 18, 144, 128),
    "coef": (7, 18, 128, 128),
}


def cost(planes):
    return pl.CostEstimate(flops=planes * 3 * 16384 * 20, transcendentals=0, bytes_accessed=planes * 16384 * 4 * 22)


def params(mib):
    return pltpu.CompilerParams(vmem_limit_bytes=mib * MIB)


def hbm(x):
    return pltpu.with_memory_space_constraint(x, pltpu.HBM)


def vmem(x):
    return pltpu.with_memory_space_constraint(x, pltpu.VMEM)


def clear_walls(ref, lead):
    for index in lead:
        ref[(*index, pl.ds(0, 8), slice(None))] = jnp.zeros((8, 128), F32)
        ref[(*index, pl.ds(136, 8), slice(None))] = jnp.zeros((8, 128), F32)


def begin(copies, sems):
    started = [pltpu.make_async_copy(s, t, sems.at[i]) for i, (s, t) in enumerate(copies)]
    for copy in started:
        copy.start()
    return started


def even(axis):
    return lax.axis_index(axis) % 2 == 0


def in_order(axis, a, b):
    return jnp.where(even(axis), b, a), jnp.where(even(axis), a, b)


def pack_kernel(adj, vel, visc, adj_s, visc_s, vel_s, za, zb, msg_a, msg_b, *rest):
    acc_l, acc_r, vel_l, vel_r, sems = rest
    inside = pl.ds(8, 128)
    n = 16 // GROUPS

    def copies(g):
        xs = pl.ds(g * n, n)
        return (
            (adj.at[:, xs], adj_s.at[:, pl.ds(2 + g * n, n), inside]),
            (visc.at[xs], visc_s.at[pl.ds(2 + g * n, n), inside]),
            (vel.at[:, xs], vel_s.at[:, pl.ds(1 + g * n, n)]),
        )

    started = [begin(copies(g), sems.at[g]) for g in range(GROUPS)]
    clear_walls(adj_s, [(c, q) for c in range(3) for q in range(1, 20)])
    clear_walls(visc_s, [(q,) for q in range(1, 20)])
    zero = jnp.zeros((144, 128), F32)
    visc_s[1] = zero
    for c in range(3):
        adj_s[c, 1] = zero
    lane = lanes((32, 128))
    pair = lane >> 1
    pair_l = ((lane + 2) & 127) >> 1
    for g in range(GROUPS):
        for copy in started[g]:
            copy.wait()
        for r in range(4):
            rows = pl.ds(r * 32, 32)
            padded = pl.ds(8 + r * 32, 32)
            half = r // 2
            if g == 0:
                left = right = vleft = vright = jnp.zeros((32, 128), F32)
            else:
                left, right, vleft, vright = (ref[rows] for ref in (acc_l, acc_r, vel_l, vel_r))
            for c in range(4):
                for x in range(g * n, g * n + n):
                    m = c * 16 + x
                    plane = adj_s[c, x + 2, padded] if c < 3 else visc_s[x + 2, padded]
                    turned = roll(plane, 2 * m, 1)
                    right = jnp.where(pair == m, turned, right)
                    left = jnp.where(pair_l == m, turned, left)
            for d in range(3):
                for x in range(g * n, g * n + n):
                    at = 2 * (d * 16 + x) + half
                    turned = roll(vel_s[d, x + 1, rows], at, 1)
                    vright = jnp.where(lane == at, turned, vright)
                    vleft = jnp.where(lane == (at - 1) % 128, turned, vleft)
            if g < GROUPS - 1:
                acc_l[rows] = left
                acc_r[rows] = right
            else:
                zb[rows], za[rows] = in_order("gz", roll(left, 2, 1), right)
                vleft = roll(vleft, 1, 1)
            vel_l[rows] = vleft
            vel_r[rows] = vright
    near = jnp.where(even("gx"), 17, 2)
    for msg, q in ((msg_a, near), (msg_b, 19 - near)):
        for c in range(3):
            msg[c] = adj_s[c, q, inside]
        msg[3] = visc_s[q, inside]
    first = (lanes((64, 128)) & 1) == 0
    right = jnp.where(first, vel_r[pl.ds(0, 64)], vel_r[pl.ds(64, 64)])
    left = jnp.where(first, vel_l[pl.ds(0, 64)], vel_l[pl.ds(64, 64)])
    zb[pl.ds(128, 64)], za[pl.ds(128, 64)] = in_order("gz", left, right)


def pack(adj, vel, visc):
    return pl.pallas_call(
        pack_kernel,
        in_specs=[ANY, ANY, ANY],
        out_specs=[VM] * 7,
        out_shape=[in_vmem(STATE[k]) for k in ("adj", "visc", "vel")]
        + [in_vmem((192, 128))] * 2
        + [in_vmem((4, 128, 128))] * 2,
        scratch_shapes=[
            *[pltpu.VMEM((128, 128), F32)] * 4,
            pltpu.SemaphoreType.DMA((GROUPS, 3)),
        ],
        compiler_params=params(4),
        name="pack",
    )(hbm(adj), hbm(vel), hbm(visc))


def spread(a, group):
    kept = jnp.where((lanes(a.shape) >> 5) == group, a, 0.0)
    kept = kept + roll(kept, 32, 1)
    return kept + roll(kept, 64, 1)


def shift_rows(a, by):
    row = lax.broadcasted_iota(jnp.int32, a.shape, 0)
    moved = roll(a, by, 0)
    edge = 0 if by > 0 else a.shape[0] - 1
    return jnp.where(row == edge, 0.0, moved)


def edge_centre(hl, hr):
    odd = (lanes((128, 128)) & 1) == 1
    return jnp.where(odd, hl[:128], hr[:128])


def edge_velocity(message):
    both = message[128:]
    odd = (lanes(both.shape) & 1) == 1
    upper = jnp.where(odd, roll(both, 1, 1), both)
    lower = jnp.where(odd, both, roll(both, -1, 1))
    return jnp.concatenate([upper, lower], axis=0)


def edge_middle(hl, hr, zl, zr, low=None, high=None):
    lane = lanes((128, 128))
    odd = (lane & 1) == 1
    x = (lane >> 1) & 15
    left, right = hl[:128], hr[:128]
    centre = jnp.where(odd, left, right)
    minus = jnp.where(odd, roll(left, 1, 1), roll(zl[:128], -1, 1))
    plus = jnp.where(odd, roll(zr[:128], 1, 1), roll(right, -1, 1))
    velocity = jnp.where(odd, edge_velocity(hl), edge_velocity(hr))
    west = roll(centre, 2, 1)
    east = roll(centre, -2, 1)
    west = jnp.where(x == 0, 0.0 if low is None else roll(low, -30, 1), west)
    east = jnp.where(x == 15, 0.0 if high is None else roll(high, 30, 1), east)
    north = shift_rows(centre, -1)
    south = shift_rows(centre, 1)
    visc = spread(centre, 3)
    total = 0.0
    result = 0.0
    for d, (up, down) in enumerate(((east, west), (north, south), (plus, minus))):
        v = spread(velocity, d)
        a_up = 0.5 * ((visc + spread(up, 3)) + v)
        a_down = 0.5 * ((visc + spread(down, 3)) - v)
        total = total + (a_up + a_down)
        result = result + (a_up * up + a_down * down)
    return result + (1.0 - total) * centre


def ends(edge, r, m):
    return roll(edge[pl.ds(r, ROWS), :], 127 - 2 * m, 1)


def first_step(adj_s, visc_s, vel_s, mid_s, coef_s, edge, x, ex):
    lane = lanes((ROWS, 128))
    q, t = x + 2, x + 1
    for r in range(0, 128, ROWS):
        rows, here = pl.ds(r, ROWS), pl.ds(8 + r, ROWS)
        above, below = pl.ds(9 + r, ROWS), pl.ds(7 + r, ROWS)

        def sides(plane, m):
            end = ends(edge, r, m)
            up = jnp.where(lane == 127, end, roll(plane, -1, 1))
            return up, jnp.where(lane == 0, end, roll(plane, 1, 1))

        centre = visc_s[q, here, :]
        pairs = (
            (visc_s[q + 1, here, :], visc_s[q - 1, here, :]),
            (visc_s[q, above, :], visc_s[q, below, :]),
            sides(centre, 48 + ex),
        )
        a = []
        for d, (plus, minus) in enumerate(pairs):
            v = vel_s[d, t, rows, :]
            a.append(0.5 * ((centre + plus) + v))
            a.append(0.5 * ((centre + minus) - v))
        a.append(1.0 - (((a[0] + a[1]) + (a[2] + a[3])) + (a[4] + a[5])))
        for k in range(7):
            coef_s[k, t, rows, :] = a[k]
        for c in range(3):
            centre = adj_s[c, q, here, :]
            up, down = sides(centre, c * 16 + ex)
            out = a[6] * centre
            out = out + a[0] * adj_s[c, q + 1, here, :]
            out = out + a[1] * adj_s[c, q - 1, here, :]
            out = out + a[2] * adj_s[c, q, above, :]
            out = out + a[3] * adj_s[c, q, below, :]
            out = out + a[4] * up
            mid_s[c, t, here, :] = out + a[5] * down
    for c in range(3):
        mid_s[c, t, pl.ds(0, 8), :] = jnp.zeros((8, 128), F32)
        mid_s[c, t, pl.ds(136, 8), :] = jnp.zeros((8, 128), F32)


def second_step(mid_s, coef_s, edge, x, store):
    lane = lanes((ROWS, 128))
    t = x + 1
    for r in range(0, 128, ROWS):
        rows, here = pl.ds(r, ROWS), pl.ds(8 + r, ROWS)
        above, below = pl.ds(9 + r, ROWS), pl.ds(7 + r, ROWS)
        a = [coef_s[k, t, rows, :] for k in range(7)]
        for c in range(3):
            centre = mid_s[c, t, here, :]
            end = ends(edge, r, c * 16 + x)
            out = a[6] * centre
            out = out + a[0] * mid_s[c, t + 1, here, :]
            out = out + a[1] * mid_s[c, t - 1, here, :]
            out = out + a[2] * mid_s[c, t, above, :]
            out = out + a[3] * mid_s[c, t, below, :]
            out = out + a[4] * jnp.where(lane == 127, end, roll(centre, -1, 1))
            store(c, rows, out + a[5] * jnp.where(lane == 0, end, roll(centre, 1, 1)))


def face_kernel(
    adj_s, visc_s, vel_s, ra, rb, za, zb, face, mid_s, coef_s, centre, middle
):
    hl, hr = in_order("gz", ra[...], rb[...])
    zr, zl = in_order("gz", za[...], zb[...])
    centre[...] = edge_centre(hl, hr)
    middle[...] = edge_middle(hl, hr, zl, zr)
    for c in range(3):
        mid_s[c, 0] = jnp.zeros((144, 128), F32)
    for x in range(2):
        first_step(adj_s, visc_s, vel_s, mid_s, coef_s, centre, x, x)
    own = jnp.where(lax.axis_index("gx") == 0, 1.0, 0.0)

    def store(c, rows, v):
        face[c, rows, :] = v * own

    second_step(mid_s, coef_s, middle, 0, store)


def face_call(state, ha, hb, za, zb):
    return pl.pallas_call(
        face_kernel,
        in_specs=[VM] * 7,
        out_specs=[VM] * 5,
        out_shape=[
            in_vmem((3, 128, 128)),
            in_vmem(STATE["mid"]),
            in_vmem(STATE["coef"]),
            in_vmem((128, 128)),
            in_vmem((128, 128)),
        ],
        compiler_params=params(4),
        cost_estimate=cost(3),
        name="face",
    )(*[vmem(a) for a in (*state, ha, hb, za, zb)])


def choose(lists, place):
    gx, gz = lax.axis_index("gx"), lax.axis_index("gz")
    half = lists[:, pl.ds(pl.multiple_of((gz // 4) * 128, 128), 128)]
    tile = lax.broadcasted_iota(jnp.int32, (512, 128), 0)
    listed = jnp.zeros((512, 128), F32)
    for k in range(8):
        listed = listed + jnp.where(half[k : k + 1] == tile, 1.0, 0.0)
    row = lax.broadcasted_iota(jnp.int32, (128, 512), 0)
    wanted = gx * 32 + ((row >> 4) ^ gz) * 4 + ((row >> 2) & 3)
    sits = jnp.where(place[...] == wanted, 1.0, 0.0).astype(BF16)
    count = jnp.dot(sits, listed.astype(BF16), preferred_element_type=F32)
    row = lax.broadcasted_iota(jnp.int32, (128, 128), 0)
    column = lanes((128, 128))
    ours = jnp.where(row == (gz % 4) * 32 + (column >> 2), 1.0, 0.0).astype(BF16)
    wide = jnp.dot(count.astype(BF16), ours, preferred_element_type=F32)
    return jnp.where((row & 3) == (column & 3), wide, 0.0)


FIELD = (3, 16, 128, 128)


def run_first(cells, state, mid_s, coef_s, edge):
    for x in cells:
        first_step(*state, mid_s, coef_s, edge, x, x)


def run_second(cells, mid_s, coef_s, edge, done):
    for x in cells:

        def store(c, rows, v, x=x):
            done[c, x, rows, :] = v

        second_step(mid_s, coef_s, edge, x, store)


def inner_kernel(
    adj_s, visc_s, vel_s, centre, middle, lists, place, _, __, mid_s, coef_s, done, chosen
):
    chosen[...] = choose(lists, place)
    run_first(range(2, 9), (adj_s, visc_s, vel_s), mid_s, coef_s, centre)
    run_second(range(2, 8), mid_s, coef_s, middle, done)


def inner(state, centre, middle, lists, place, mid, coef):
    return pl.pallas_call(
        inner_kernel,
        in_specs=[VM] * 9,
        out_specs=[VM] * 4,
        out_shape=[in_vmem(STATE["mid"]), in_vmem(STATE["coef"]), in_vmem(FIELD), in_vmem((128, 128))],
        input_output_aliases={7: 0, 8: 1},
        compiler_params=params(4),
        cost_estimate=cost(13),
        name="inner",
    )(*[vmem(a) for a in (*state, centre, middle)], lists, place, *[vmem(a) for a in (mid, coef)])


def ends_kernel(
    adj_i, visc_i, vel_s, centre, middle, ra, rb, _, __, ___, ____,
    adj_s, visc_s, mid_s, coef_s, done, out, msg_a, msg_b, sems,
):
    started = begin([(done.at[:, pl.ds(8, 6)], out.at[:, pl.ds(8, 6)])], sems)
    beyond = jnp.where(even("gx"), 18, 1)
    for msg, q in ((ra, beyond), (rb, 19 - beyond)):
        for c in range(3):
            adj_s[c, q, pl.ds(8, 128)] = msg[c]
        visc_s[q, pl.ds(8, 128)] = msg[3]
    run_first((0, 15), (adj_s, visc_s, vel_s), mid_s, coef_s, centre)
    near = jnp.where(even("gx"), 16, 1)
    for msg, t in ((msg_a, near), (msg_b, 17 - near)):
        for c in range(3):
            msg[c] = mid_s[c, t, pl.ds(8, 128)]
        msg[3] = centre[...]
    run_second((1, 14), mid_s, coef_s, middle, done)
    for copy in started:
        copy.wait()


def ends_call(state, centre, middle, ra, rb, mid, coef, done, out):
    held = [vmem(a) for a in (*state, centre, middle, ra, rb, mid, coef, done)]
    return pl.pallas_call(
        ends_kernel,
        in_specs=[VM] * 10 + [ANY],
        out_specs=[VM] * 5 + [ANY, VM, VM],
        out_shape=[in_vmem(STATE[k]) for k in ("adj", "visc", "mid", "coef")]
        + [in_vmem(FIELD), pltpu.HBM(FIELD, F32)]
        + [in_vmem((4, 128, 128))] * 2,
        scratch_shapes=[pltpu.SemaphoreType.DMA((1,))],
        input_output_aliases={0: 0, 1: 1, 7: 2, 8: 3, 9: 4, 10: 5},
        compiler_params=params(4),
        cost_estimate=cost(4),
        name="ends",
    )(*held, hbm(out))[2:]


def middle_kernel(
    adj_s, visc_s, vel_s, centre, middle, _, __, ___, filters, mid_s, coef_s, done, out, kept, sems
):
    started = begin([(done.at[:, pl.ds(2, 6)], out.at[:, pl.ds(2, 6)]), (filters, kept)], sems)
    run_first(range(9, 15), (adj_s, visc_s, vel_s), mid_s, coef_s, centre)
    run_second(range(8, 14), mid_s, coef_s, middle, done)
    for copy in started:
        copy.wait()


def middle_call(state, centre, middle, mid, coef, done, filters):
    held = [vmem(a) for a in (*state, centre, middle, mid, coef, done)]
    return pl.pallas_call(
        middle_kernel,
        in_specs=[VM] * 8 + [ANY],
        out_specs=[VM] * 3 + [ANY, VM],
        out_shape=[in_vmem(STATE["mid"]), in_vmem(STATE["coef"]), in_vmem(FIELD)]
        + [pltpu.HBM(FIELD, F32), pltpu.VMEM(filters.shape, BF16)],
        scratch_shapes=[pltpu.SemaphoreType.DMA((2,))],
        input_output_aliases={5: 0, 6: 1, 7: 2},
        compiler_params=params(4),
        cost_estimate=cost(12),
        name="middle",
    )(*held, hbm(filters))


def last_kernel(
    ha, hb, za, zb, ra, rb, _, coef_s, __, ___, mid_s, done, out, edges, sems
):
    copies = [
        pltpu.make_async_copy(done.at[:, pl.ds(x, n)], out.at[:, pl.ds(x, n)], sems.at[i])
        for i, (x, n) in enumerate(((1, 1), (14, 1), (0, 1), (15, 1)))
    ]
    copies[0].start()
    copies[1].start()
    hl, hr = in_order("gz", ha[...], hb[...])
    zr, zl = in_order("gz", za[...], zb[...])
    low, high = in_order("gx", ra[3], rb[3])
    edges[...] = edge_middle(hl, hr, zl, zr, low, high)
    beyond = jnp.where(even("gx"), 17, 0)
    for msg, t in ((ra, beyond), (rb, 17 - beyond)):
        for c in range(3):
            mid_s[c, t, pl.ds(8, 128)] = msg[c]
    for i, x in ((2, 0), (3, 15)):
        run_second((x,), mid_s, coef_s, edges, done)
        copies[i].start()
    for copy in copies:
        copy.wait()


def last_call(ha, hb, za, zb, ra, rb, mid, coef, done, out):
    held = [vmem(a) for a in (ha, hb, za, zb, ra, rb, mid, coef, done)]
    return pl.pallas_call(
        last_kernel,
        in_specs=[VM] * 9 + [ANY],
        out_specs=[VM] * 2 + [ANY],
        out_shape=[in_vmem(STATE["mid"]), in_vmem(FIELD), pltpu.HBM(FIELD, F32)],
        scratch_shapes=[pltpu.VMEM((128, 128), F32), pltpu.SemaphoreType.DMA((4,))],
        input_output_aliases={6: 0, 8: 1, 9: 2},
        compiler_params=params(4),
        cost_estimate=cost(4),
        name="last",
    )(*held, hbm(out))[-1]


def join_kernel(*refs):
    total = refs[0][...]
    for ref in refs[1:-1]:
        total = total + ref[...]
    refs[-1][...] = total


def join(*parts):
    return pl.pallas_call(
        join_kernel,
        in_specs=[VM] * len(parts),
        out_specs=VM,
        out_shape=in_vmem(parts[0].shape),
        compiler_params=params(2),
        name="join",
    )(*[vmem(a) for a in parts])


def pieces(a):
    high = a.astype(BF16)
    rest = a - high.astype(F32)
    mid = rest.astype(BF16)
    low = (rest - mid.astype(F32)).astype(BF16)
    return high, mid, low


PART = (3, 16, 128)


def sums_kernel(chosen, face, more, *pairs):
    matrix = chosen[...].astype(BF16)
    for c in range(3):
        total = 0.0
        for piece in pieces(face[c] + more[c]):
            total = total + jnp.dot(matrix, piece, preferred_element_type=F32)
        for k in range(8):
            pairs[k // 2][k % 2, c] = total[k * 16 : k * 16 + 16]


def partial_sums(chosen, face, more):
    return pl.pallas_call(
        sums_kernel,
        in_specs=[VM] * 3,
        out_specs=[VM] * 4,
        out_shape=[in_vmem((2, *PART))] * 4,
        compiler_params=params(2),
        name="sums",
    )(vmem(chosen), vmem(face), vmem(more))


def gather_kernel(a, b, c, d, kept, given):
    kept[...] = (a[0] + b[0]) + (c[0] + d[0])
    given[...] = (a[1] + b[1]) + (c[1] + d[1])


def gather(pairs):
    return pl.pallas_call(
        gather_kernel,
        in_specs=[VM] * 4,
        out_specs=[VM] * 2,
        out_shape=[in_vmem(PART)] * 2,
        compiler_params=params(2),
        name="gather",
    )(*[vmem(a) for a in pairs])


def product_kernel(kept, came, filters, out, sums):
    sums[...] = kept[...] + came[...]
    for p in range(4):
        view = jnp.concatenate([sums[:, p * 4 + i, :] for i in range(4)], axis=1)
        stacked = jnp.concatenate(pieces(view), axis=0)
        wide = jnp.dot(stacked, filters[p], preferred_element_type=F32)
        out[:, p, :] = wide[0:3] + (wide[3:6] + wide[6:9])


def product(parts, filters):
    return pl.pallas_call(
        product_kernel,
        in_specs=[VM] * 3,
        out_specs=VM,
        out_shape=jax.ShapeDtypeStruct((3, 4, 512), F32),
        scratch_shapes=[pltpu.VMEM(PART, F32)],
        compiler_params=params(4),
        name="product",
    )(*[vmem(a) for a in (*parts, filters)])


def shards(adjoint, velocity, viscosity, filters, block_tiles, tile_place):
    nx = lax.axis_size("gx")
    nz = lax.axis_size("gz")
    inside_z = [(i, i ^ 1) for i in range(nz)]
    across_z = [(i, (i + 1 if i % 2 else i - 1) % nz) for i in range(nz)]
    inside_x = [(i, i ^ 1) for i in range(nx)]
    across_x = [(i, i + 1 if i % 2 else i - 1) for i in range(1, nx - 1)]

    *state, za, zb, msg_a, msg_b = pack(adjoint, velocity, viscosity)
    ha = lax.ppermute(za, "gz", inside_z)
    hb = lax.ppermute(zb, "gz", across_z)
    face, mid, coef, centre, middle = face_call(state, ha, hb, za, zb)

    face, msg_a, msg_b = lax.optimization_barrier((face, msg_a, msg_b))
    ra = lax.ppermute(msg_a, "gx", inside_x)
    rb = lax.ppermute(msg_b, "gx", across_x)
    got = [lax.ppermute(face, "gx", [(0, k)]) for k in (8, 2, 6)]
    mid, coef, done, chosen = inner(
        state, centre, middle, block_tiles.T, tile_place.reshape(1, -1), mid, coef
    )
    *got, mid, coef, done = lax.optimization_barrier((*got, mid, coef, done))
    face = join(face, *got)
    far = lax.ppermute(face, "gx", [(0, 4), (2, 10), (6, 14), (8, 12)])
    mid, coef, done, out, near = middle_call(state, centre, middle, mid, coef, done, filters)
    mid, coef, done, out, msg_a, msg_b = ends_call(
        state, centre, middle, ra, rb, mid, coef, done, out
    )
    ra = lax.ppermute(msg_a, "gx", inside_x)
    rb = lax.ppermute(msg_b, "gx", across_x)
    far, mid, coef, done = lax.optimization_barrier((far, mid, coef, done))
    face = join(face, far)
    other = lax.ppermute(face, "gx", [(i, i + 1) for i in range(0, nx, 2)])
    own, *pairs = partial_sums(chosen, face, other)
    pairs = [
        lax.ppermute(pairs[k // 2 - 1], "gz", [(i, i ^ k) for i in range(nz)]) for k in (4, 2, 6)
    ]
    kept, given = gather((own, *pairs))
    came = lax.ppermute(given, "gz", inside_z)
    out = last_call(ha, hb, za, zb, ra, rb, mid, coef, done, out)
    came, out = lax.optimization_barrier((came, out))
    gradient = product((kept, came), near).transpose(1, 0, 2)
    return out, gradient


def solution(mesh):
    placed = (
        P(None, "gx", None, "gz"),
        P(None, "gx", None, "gz"),
        P("gx", None, "gz"),
        P(("gx", "gz"), None, None),
        P(),
        P(),
    )
    return jax.shard_map(
        shards,
        mesh=mesh,
        in_specs=placed,
        out_specs=(P(None, "gx", None, "gz"), P(("gx", "gz"), None, None)),
        check_vma=False,
    )
```

```python
import jax
import jax.numpy as jnp
from jax import lax
from jax.experimental import pallas as pl
from jax.experimental.pallas import tpu as pltpu
from jax.sharding import PartitionSpec as P

F32 = jnp.float32
BF16 = jnp.bfloat16
ANY = pl.BlockSpec(memory_space=pl.ANY)
VM = pl.BlockSpec(memory_space=pltpu.VMEM)
MIB = 1024 * 1024
ROWS = 16
GROUPS = 4


def lanes(shape):
    return lax.broadcasted_iota(jnp.int32, shape, len(shape) - 1)


def roll(x, shift, axis):
    if isinstance(shift, int):
        shift = shift % x.shape[axis]
    return pltpu.roll(x, shift, axis)


def in_vmem(shape):
    return pltpu.VMEM(shape, F32)


STATE = {
    "adj": (3, 20, 144, 128),
    "visc": (20, 144, 128),
    "vel": (3, 18, 128, 128),
    "mid": (3, 18, 144, 128),
    "coef": (7, 18, 128, 128),
}


def cost(planes):
    return pl.CostEstimate(flops=planes * 3 * 16384 * 20, transcendentals=0, bytes_accessed=planes * 16384 * 4 * 22)


def params(mib):
    return pltpu.CompilerParams(vmem_limit_bytes=mib * MIB)


def hbm(x):
    return pltpu.with_memory_space_constraint(x, pltpu.HBM)


def vmem(x):
    return pltpu.with_memory_space_constraint(x, pltpu.VMEM)


def clear_walls(ref, lead):
    for index in lead:
        ref[(*index, pl.ds(0, 8), slice(None))] = jnp.zeros((8, 128), F32)
        ref[(*index, pl.ds(136, 8), slice(None))] = jnp.zeros((8, 128), F32)


def begin(copies, sems):
    started = [pltpu.make_async_copy(s, t, sems.at[i]) for i, (s, t) in enumerate(copies)]
    for copy in started:
        copy.start()
    return started


def even(axis):
    return lax.axis_index(axis) % 2 == 0


def in_order(axis, a, b):
    return jnp.where(even(axis), b, a), jnp.where(even(axis), a, b)


def pack_kernel(adj, vel, visc, adj_s, visc_s, vel_s, za, zb, msg_a, msg_b, *rest):
    acc_l, acc_r, vel_l, vel_r, sems = rest
    inside = pl.ds(8, 128)
    n = 16 // GROUPS

    def copies(g):
        xs = pl.ds(g * n, n)
        return (
            (adj.at[:, xs], adj_s.at[:, pl.ds(2 + g * n, n), inside]),
            (visc.at[xs], visc_s.at[pl.ds(2 + g * n, n), inside]),
            (vel.at[:, xs], vel_s.at[:, pl.ds(1 + g * n, n)]),
        )

    started = [begin(copies(g), sems.at[g]) for g in range(GROUPS)]
    clear_walls(adj_s, [(c, q) for c in range(3) for q in range(1, 20)])
    clear_walls(visc_s, [(q,) for q in range(1, 20)])
    zero = jnp.zeros((144, 128), F32)
    visc_s[1] = zero
    for c in range(3):
        adj_s[c, 1] = zero
    lane = lanes((32, 128))
    pair = lane >> 1
    pair_l = ((lane + 2) & 127) >> 1
    for g in range(GROUPS):
        for copy in started[g]:
            copy.wait()
        for r in range(4):
            rows = pl.ds(r * 32, 32)
            padded = pl.ds(8 + r * 32, 32)
            half = r // 2
            if g == 0:
                left = right = vleft = vright = jnp.zeros((32, 128), F32)
            else:
                left, right, vleft, vright = (ref[rows] for ref in (acc_l, acc_r, vel_l, vel_r))
            for c in range(4):
                for x in range(g * n, g * n + n):
                    m = c * 16 + x
                    plane = adj_s[c, x + 2, padded] if c < 3 else visc_s[x + 2, padded]
                    turned = roll(plane, 2 * m, 1)
                    right = jnp.where(pair == m, turned, right)
                    left = jnp.where(pair_l == m, turned, left)
            for d in range(3):
                for x in range(g * n, g * n + n):
                    at = 2 * (d * 16 + x) + half
                    turned = roll(vel_s[d, x + 1, rows], at, 1)
                    vright = jnp.where(lane == at, turned, vright)
                    vleft = jnp.where(lane == (at - 1) % 128, turned, vleft)
            if g < GROUPS - 1:
                acc_l[rows] = left
                acc_r[rows] = right
            else:
                zb[rows], za[rows] = in_order("gz", roll(left, 2, 1), right)
                vleft = roll(vleft, 1, 1)
            vel_l[rows] = vleft
            vel_r[rows] = vright
    near = jnp.where(even("gx"), 17, 2)
    for msg, q in ((msg_a, near), (msg_b, 19 - near)):
        for c in range(3):
            msg[c] = adj_s[c, q, inside]
        msg[3] = visc_s[q, inside]
    first = (lanes((64, 128)) & 1) == 0
    right = jnp.where(first, vel_r[pl.ds(0, 64)], vel_r[pl.ds(64, 64)])
    left = jnp.where(first, vel_l[pl.ds(0, 64)], vel_l[pl.ds(64, 64)])
    zb[pl.ds(128, 64)], za[pl.ds(128, 64)] = in_order("gz", left, right)


def pack(adj, vel, visc):
    return pl.pallas_call(
        pack_kernel,
        in_specs=[ANY, ANY, ANY],
        out_specs=[VM] * 7,
        out_shape=[in_vmem(STATE[k]) for k in ("adj", "visc", "vel")]
        + [in_vmem((192, 128))] * 2
        + [in_vmem((4, 128, 128))] * 2,
        scratch_shapes=[
            *[pltpu.VMEM((128, 128), F32)] * 4,
            pltpu.SemaphoreType.DMA((GROUPS, 3)),
        ],
        compiler_params=params(4),
        name="pack",
    )(hbm(adj), hbm(vel), hbm(visc))


def spread(a, group):
    kept = jnp.where((lanes(a.shape) >> 5) == group, a, 0.0)
    kept = kept + roll(kept, 32, 1)
    return kept + roll(kept, 64, 1)


def shift_rows(a, by):
    row = lax.broadcasted_iota(jnp.int32, a.shape, 0)
    moved = roll(a, by, 0)
    edge = 0 if by > 0 else a.shape[0] - 1
    return jnp.where(row == edge, 0.0, moved)


def edge_centre(hl, hr):
    odd = (lanes((128, 128)) & 1) == 1
    return jnp.where(odd, hl[:128], hr[:128])


def edge_velocity(message):
    both = message[128:]
    odd = (lanes(both.shape) & 1) == 1
    upper = jnp.where(odd, roll(both, 1, 1), both)
    lower = jnp.where(odd, both, roll(both, -1, 1))
    return jnp.concatenate([upper, lower], axis=0)


def edge_middle(hl, hr, zl, zr, low=None, high=None):
    lane = lanes((128, 128))
    odd = (lane & 1) == 1
    x = (lane >> 1) & 15
    left, right = hl[:128], hr[:128]
    centre = jnp.where(odd, left, right)
    minus = jnp.where(odd, roll(left, 1, 1), roll(zl[:128], -1, 1))
    plus = jnp.where(odd, roll(zr[:128], 1, 1), roll(right, -1, 1))
    velocity = jnp.where(odd, edge_velocity(hl), edge_velocity(hr))
    west = roll(centre, 2, 1)
    east = roll(centre, -2, 1)
    west = jnp.where(x == 0, 0.0 if low is None else roll(low, -30, 1), west)
    east = jnp.where(x == 15, 0.0 if high is None else roll(high, 30, 1), east)
    north = shift_rows(centre, -1)
    south = shift_rows(centre, 1)
    visc = spread(centre, 3)
    total = 0.0
    result = 0.0
    for d, (up, down) in enumerate(((east, west), (north, south), (plus, minus))):
        v = spread(velocity, d)
        a_up = 0.5 * ((visc + spread(up, 3)) + v)
        a_down = 0.5 * ((visc + spread(down, 3)) - v)
        total = total + (a_up + a_down)
        result = result + (a_up * up + a_down * down)
    return result + (1.0 - total) * centre


def ends(edge, r, m):
    return roll(edge[pl.ds(r, ROWS), :], 127 - 2 * m, 1)


def first_step(adj_s, visc_s, vel_s, mid_s, coef_s, edge, x, ex):
    lane = lanes((ROWS, 128))
    q, t = x + 2, x + 1
    for r in range(0, 128, ROWS):
        rows, here = pl.ds(r, ROWS), pl.ds(8 + r, ROWS)
        above, below = pl.ds(9 + r, ROWS), pl.ds(7 + r, ROWS)

        def sides(plane, m):
            end = ends(edge, r, m)
            up = jnp.where(lane == 127, end, roll(plane, -1, 1))
            return up, jnp.where(lane == 0, end, roll(plane, 1, 1))

        centre = visc_s[q, here, :]
        pairs = (
            (visc_s[q + 1, here, :], visc_s[q - 1, here, :]),
            (visc_s[q, above, :], visc_s[q, below, :]),
            sides(centre, 48 + ex),
        )
        a = []
        for d, (plus, minus) in enumerate(pairs):
            v = vel_s[d, t, rows, :]
            a.append(0.5 * ((centre + plus) + v))
            a.append(0.5 * ((centre + minus) - v))
        a.append(1.0 - (((a[0] + a[1]) + (a[2] + a[3])) + (a[4] + a[5])))
        for k in range(7):
            coef_s[k, t, rows, :] = a[k]
        for c in range(3):
            centre = adj_s[c, q, here, :]
            up, down = sides(centre, c * 16 + ex)
            out = a[6] * centre
            out = out + a[0] * adj_s[c, q + 1, here, :]
            out = out + a[1] * adj_s[c, q - 1, here, :]
            out = out + a[2] * adj_s[c, q, above, :]
            out = out + a[3] * adj_s[c, q, below, :]
            out = out + a[4] * up
            mid_s[c, t, here, :] = out + a[5] * down
    for c in range(3):
        mid_s[c, t, pl.ds(0, 8), :] = jnp.zeros((8, 128), F32)
        mid_s[c, t, pl.ds(136, 8), :] = jnp.zeros((8, 128), F32)


def second_step(mid_s, coef_s, edge, x, store):
    lane = lanes((ROWS, 128))
    t = x + 1
    for r in range(0, 128, ROWS):
        rows, here = pl.ds(r, ROWS), pl.ds(8 + r, ROWS)
        above, below = pl.ds(9 + r, ROWS), pl.ds(7 + r, ROWS)
        a = [coef_s[k, t, rows, :] for k in range(7)]
        for c in range(3):
            centre = mid_s[c, t, here, :]
            end = ends(edge, r, c * 16 + x)
            out = a[6] * centre
            out = out + a[0] * mid_s[c, t + 1, here, :]
            out = out + a[1] * mid_s[c, t - 1, here, :]
            out = out + a[2] * mid_s[c, t, above, :]
            out = out + a[3] * mid_s[c, t, below, :]
            out = out + a[4] * jnp.where(lane == 127, end, roll(centre, -1, 1))
            store(c, rows, out + a[5] * jnp.where(lane == 0, end, roll(centre, 1, 1)))


def face_kernel(
    adj_s, visc_s, vel_s, ra, rb, za, zb, face, mid_s, coef_s, centre, middle
):
    hl, hr = in_order("gz", ra[...], rb[...])
    zr, zl = in_order("gz", za[...], zb[...])
    centre[...] = edge_centre(hl, hr)
    middle[...] = edge_middle(hl, hr, zl, zr)
    for c in range(3):
        mid_s[c, 0] = jnp.zeros((144, 128), F32)
    for x in range(2):
        first_step(adj_s, visc_s, vel_s, mid_s, coef_s, centre, x, x)
    own = jnp.where(lax.axis_index("gx") == 0, 1.0, 0.0)

    def store(c, rows, v):
        face[c, rows, :] = v * own

    second_step(mid_s, coef_s, middle, 0, store)


def face_call(state, ha, hb, za, zb):
    return pl.pallas_call(
        face_kernel,
        in_specs=[VM] * 7,
        out_specs=[VM] * 5,
        out_shape=[
            in_vmem((3, 128, 128)),
            in_vmem(STATE["mid"]),
            in_vmem(STATE["coef"]),
            in_vmem((128, 128)),
            in_vmem((128, 128)),
        ],
        compiler_params=params(4),
        cost_estimate=cost(3),
        name="face",
    )(*[vmem(a) for a in (*state, ha, hb, za, zb)])


def choose(lists, place):
    gx, gz = lax.axis_index("gx"), lax.axis_index("gz")
    half = lists[:, pl.ds(pl.multiple_of((gz // 4) * 128, 128), 128)]
    tile = lax.broadcasted_iota(jnp.int32, (512, 128), 0)
    listed = jnp.zeros((512, 128), F32)
    for k in range(8):
        listed = listed + jnp.where(half[k : k + 1] == tile, 1.0, 0.0)
    row = lax.broadcasted_iota(jnp.int32, (128, 512), 0)
    wanted = gx * 32 + ((row >> 4) ^ gz) * 4 + ((row >> 2) & 3)
    sits = jnp.where(place[...] == wanted, 1.0, 0.0).astype(BF16)
    count = jnp.dot(sits, listed.astype(BF16), preferred_element_type=F32)
    row = lax.broadcasted_iota(jnp.int32, (128, 128), 0)
    column = lanes((128, 128))
    ours = jnp.where(row == (gz % 4) * 32 + (column >> 2), 1.0, 0.0).astype(BF16)
    wide = jnp.dot(count.astype(BF16), ours, preferred_element_type=F32)
    return jnp.where((row & 3) == (column & 3), wide, 0.0)


FIELD = (3, 16, 128, 128)


def run_first(cells, state, mid_s, coef_s, edge):
    for x in cells:
        first_step(*state, mid_s, coef_s, edge, x, x)


def run_second(cells, mid_s, coef_s, edge, done):
    for x in cells:

        def store(c, rows, v, x=x):
            done[c, x, rows, :] = v

        second_step(mid_s, coef_s, edge, x, store)


def inner_kernel(
    adj_s, visc_s, vel_s, centre, middle, lists, place, _, __, mid_s, coef_s, done, chosen
):
    chosen[...] = choose(lists, place)
    run_first(range(2, 9), (adj_s, visc_s, vel_s), mid_s, coef_s, centre)
    run_second(range(2, 8), mid_s, coef_s, middle, done)


def inner(state, centre, middle, lists, place, mid, coef):
    return pl.pallas_call(
        inner_kernel,
        in_specs=[VM] * 9,
        out_specs=[VM] * 4,
        out_shape=[in_vmem(STATE["mid"]), in_vmem(STATE["coef"]), in_vmem(FIELD), in_vmem((128, 128))],
        input_output_aliases={7: 0, 8: 1},
        compiler_params=params(4),
        cost_estimate=cost(13),
        name="inner",
    )(*[vmem(a) for a in (*state, centre, middle)], lists, place, *[vmem(a) for a in (mid, coef)])


def ends_kernel(
    adj_i, visc_i, vel_s, centre, middle, ra, rb, _, __, ___, ____,
    adj_s, visc_s, mid_s, coef_s, done, out, msg_a, msg_b, sems,
):
    started = begin([(done.at[:, pl.ds(8, 6)], out.at[:, pl.ds(8, 6)])], sems)
    beyond = jnp.where(even("gx"), 18, 1)
    for msg, q in ((ra, beyond), (rb, 19 - beyond)):
        for c in range(3):
            adj_s[c, q, pl.ds(8, 128)] = msg[c]
        visc_s[q, pl.ds(8, 128)] = msg[3]
    run_first((0, 15), (adj_s, visc_s, vel_s), mid_s, coef_s, centre)
    near = jnp.where(even("gx"), 16, 1)
    for msg, t in ((msg_a, near), (msg_b, 17 - near)):
        for c in range(3):
            msg[c] = mid_s[c, t, pl.ds(8, 128)]
        msg[3] = centre[...]
    run_second((1, 14), mid_s, coef_s, middle, done)
    for copy in started:
        copy.wait()


def ends_call(state, centre, middle, ra, rb, mid, coef, done, out):
    held = [vmem(a) for a in (*state, centre, middle, ra, rb, mid, coef, done)]
    return pl.pallas_call(
        ends_kernel,
        in_specs=[VM] * 10 + [ANY],
        out_specs=[VM] * 5 + [ANY, VM, VM],
        out_shape=[in_vmem(STATE[k]) for k in ("adj", "visc", "mid", "coef")]
        + [in_vmem(FIELD), pltpu.HBM(FIELD, F32)]
        + [in_vmem((4, 128, 128))] * 2,
        scratch_shapes=[pltpu.SemaphoreType.DMA((1,))],
        input_output_aliases={0: 0, 1: 1, 7: 2, 8: 3, 9: 4, 10: 5},
        compiler_params=params(4),
        cost_estimate=cost(4),
        name="ends",
    )(*held, hbm(out))[2:]


def middle_kernel(
    adj_s, visc_s, vel_s, centre, middle, _, __, ___, filters, mid_s, coef_s, done, out, kept, sems
):
    started = begin([(done.at[:, pl.ds(2, 6)], out.at[:, pl.ds(2, 6)]), (filters, kept)], sems)
    run_first(range(9, 15), (adj_s, visc_s, vel_s), mid_s, coef_s, centre)
    run_second(range(8, 14), mid_s, coef_s, middle, done)
    for copy in started:
        copy.wait()


def middle_call(state, centre, middle, mid, coef, done, filters):
    held = [vmem(a) for a in (*state, centre, middle, mid, coef, done)]
    return pl.pallas_call(
        middle_kernel,
        in_specs=[VM] * 8 + [ANY],
        out_specs=[VM] * 3 + [ANY, VM],
        out_shape=[in_vmem(STATE["mid"]), in_vmem(STATE["coef"]), in_vmem(FIELD)]
        + [pltpu.HBM(FIELD, F32), pltpu.VMEM(filters.shape, BF16)],
        scratch_shapes=[pltpu.SemaphoreType.DMA((2,))],
        input_output_aliases={5: 0, 6: 1, 7: 2},
        compiler_params=params(4),
        cost_estimate=cost(12),
        name="middle",
    )(*held, hbm(filters))


def last_kernel(
    ha, hb, za, zb, ra, rb, _, coef_s, __, ___, mid_s, done, out, edges, sems
):
    copies = [
        pltpu.make_async_copy(done.at[:, pl.ds(x, n)], out.at[:, pl.ds(x, n)], sems.at[i])
        for i, (x, n) in enumerate(((1, 1), (14, 1), (0, 1), (15, 1)))
    ]
    copies[0].start()
    copies[1].start()
    hl, hr = in_order("gz", ha[...], hb[...])
    zr, zl = in_order("gz", za[...], zb[...])
    low, high = in_order("gx", ra[3], rb[3])
    edges[...] = edge_middle(hl, hr, zl, zr, low, high)
    beyond = jnp.where(even("gx"), 17, 0)
    for msg, t in ((ra, beyond), (rb, 17 - beyond)):
        for c in range(3):
            mid_s[c, t, pl.ds(8, 128)] = msg[c]
    for i, x in ((2, 0), (3, 15)):
        run_second((x,), mid_s, coef_s, edges, done)
        copies[i].start()
    for copy in copies:
        copy.wait()


def last_call(ha, hb, za, zb, ra, rb, mid, coef, done, out):
    held = [vmem(a) for a in (ha, hb, za, zb, ra, rb, mid, coef, done)]
    return pl.pallas_call(
        last_kernel,
        in_specs=[VM] * 9 + [ANY],
        out_specs=[VM] * 2 + [ANY],
        out_shape=[in_vmem(STATE["mid"]), in_vmem(FIELD), pltpu.HBM(FIELD, F32)],
        scratch_shapes=[pltpu.VMEM((128, 128), F32), pltpu.SemaphoreType.DMA((4,))],
        input_output_aliases={6: 0, 8: 1, 9: 2},
        compiler_params=params(4),
        cost_estimate=cost(4),
        name="last",
    )(*held, hbm(out))[-1]


def join_kernel(*refs):
    total = refs[0][...]
    for ref in refs[1:-1]:
        total = total + ref[...]
    refs[-1][...] = total


def join(*parts):
    return pl.pallas_call(
        join_kernel,
        in_specs=[VM] * len(parts),
        out_specs=VM,
        out_shape=in_vmem(parts[0].shape),
        compiler_params=params(2),
        name="join",
    )(*[vmem(a) for a in parts])


def pieces(a):
    high = a.astype(BF16)
    rest = a - high.astype(F32)
    mid = rest.astype(BF16)
    low = (rest - mid.astype(F32)).astype(BF16)
    return high, mid, low


PART = (3, 16, 128)


def sums_kernel(chosen, face, more, *pairs):
    matrix = chosen[...].astype(BF16)
    for c in range(3):
        total = 0.0
        for piece in pieces(face[c] + more[c]):
            total = total + jnp.dot(matrix, piece, preferred_element_type=F32)
        for k in range(8):
            pairs[k // 2][k % 2, c] = total[k * 16 : k * 16 + 16]


def partial_sums(chosen, face, more):
    return pl.pallas_call(
        sums_kernel,
        in_specs=[VM] * 3,
        out_specs=[VM] * 4,
        out_shape=[in_vmem((2, *PART))] * 4,
        compiler_params=params(2),
        name="sums",
    )(vmem(chosen), vmem(face), vmem(more))


def gather_kernel(a, b, c, d, kept, given):
    kept[...] = (a[0] + b[0]) + (c[0] + d[0])
    given[...] = (a[1] + b[1]) + (c[1] + d[1])


def gather(pairs):
    return pl.pallas_call(
        gather_kernel,
        in_specs=[VM] * 4,
        out_specs=[VM] * 2,
        out_shape=[in_vmem(PART)] * 2,
        compiler_params=params(2),
        name="gather",
    )(*[vmem(a) for a in pairs])


def product_kernel(kept, came, filters, out, sums):
    sums[...] = kept[...] + came[...]
    for p in range(4):
        view = jnp.concatenate([sums[:, p * 4 + i, :] for i in range(4)], axis=1)
        stacked = jnp.concatenate(pieces(view), axis=0)
        wide = jnp.dot(stacked, filters[p], preferred_element_type=F32)
        out[:, p, :] = wide[0:3] + (wide[3:6] + wide[6:9])


def product(parts, filters):
    return pl.pallas_call(
        product_kernel,
        in_specs=[VM] * 3,
        out_specs=VM,
        out_shape=jax.ShapeDtypeStruct((3, 4, 512), F32),
        scratch_shapes=[pltpu.VMEM(PART, F32)],
        compiler_params=params(4),
        name="product",
    )(*[vmem(a) for a in (*parts, filters)])


def shards(adjoint, velocity, viscosity, filters, block_tiles, tile_place):
    nx = lax.axis_size("gx")
    nz = lax.axis_size("gz")
    inside_z = [(i, i ^ 1) for i in range(nz)]
    across_z = [(i, (i + 1 if i % 2 else i - 1) % nz) for i in range(nz)]
    inside_x = [(i, i ^ 1) for i in range(nx)]
    across_x = [(i, i + 1 if i % 2 else i - 1) for i in range(1, nx - 1)]

    *state, za, zb, msg_a, msg_b = pack(adjoint, velocity, viscosity)
    ha = lax.ppermute(za, "gz", inside_z)
    hb = lax.ppermute(zb, "gz", across_z)
    face, mid, coef, centre, middle = face_call(state, ha, hb, za, zb)

    face, msg_a, msg_b = lax.optimization_barrier((face, msg_a, msg_b))
    ra = lax.ppermute(msg_a, "gx", inside_x)
    rb = lax.ppermute(msg_b, "gx", across_x)
    got = [lax.ppermute(face, "gx", [(0, k)]) for k in (8, 2, 6)]
    mid, coef, done, chosen = inner(
        state, centre, middle, block_tiles.T, tile_place.reshape(1, -1), mid, coef
    )
    *got, mid, coef, done = lax.optimization_barrier((*got, mid, coef, done))
    face = join(face, *got)
    far = lax.ppermute(face, "gx", [(0, 4), (2, 10), (6, 14), (8, 12)])
    mid, coef, done, out, near = middle_call(state, centre, middle, mid, coef, done, filters)
    mid, coef, done, out, msg_a, msg_b = ends_call(
        state, centre, middle, ra, rb, mid, coef, done, out
    )
    ra = lax.ppermute(msg_a, "gx", inside_x)
    rb = lax.ppermute(msg_b, "gx", across_x)
    far, mid, coef, done = lax.optimization_barrier((far, mid, coef, done))
    face = join(face, far)
    other = lax.ppermute(face, "gx", [(i, i + 1) for i in range(0, nx, 2)])
    own, *pairs = partial_sums(chosen, face, other)
    pairs = [
        lax.ppermute(pairs[k // 2 - 1], "gz", [(i, i ^ k) for i in range(nz)]) for k in (4, 2, 6)
    ]
    out = last_call(ha, hb, za, zb, ra, rb, mid, coef, done, out)
    *pairs, out = lax.optimization_barrier((*pairs, out))
    kept, given = gather((own, *pairs))
    came = lax.ppermute(given, "gz", inside_z)
    gradient = product((kept, came), near).transpose(1, 0, 2)
    return out, gradient


def solution(mesh):
    placed = (
        P(None, "gx", None, "gz"),
        P(None, "gx", None, "gz"),
        P("gx", None, "gz"),
        P(("gx", "gz"), None, None),
        P(),
        P(),
    )
    return jax.shard_map(
        shards,
        mesh=mesh,
        in_specs=placed,
        out_specs=(P(None, "gx", None, "gz"), P(("gx", "gz"), None, None)),
        check_vma=False,
    )
```

```python
import jax
import jax.numpy as jnp
from jax import lax
from jax.experimental import pallas as pl
from jax.experimental.pallas import tpu as pltpu
from jax.sharding import PartitionSpec as P

F32 = jnp.float32
BF16 = jnp.bfloat16
ANY = pl.BlockSpec(memory_space=pl.ANY)
VM = pl.BlockSpec(memory_space=pltpu.VMEM)
MIB = 1024 * 1024
ROWS = 16
GROUPS = 4


def lanes(shape):
    return lax.broadcasted_iota(jnp.int32, shape, len(shape) - 1)


def roll(x, shift, axis):
    if isinstance(shift, int):
        shift = shift % x.shape[axis]
    return pltpu.roll(x, shift, axis)


def in_vmem(shape):
    return pltpu.VMEM(shape, F32)


STATE = {
    "adj": (3, 20, 144, 128),
    "visc": (20, 144, 128),
    "vel": (3, 18, 128, 128),
    "mid": (3, 18, 144, 128),
    "coef": (7, 18, 128, 128),
}


def cost(planes):
    return pl.CostEstimate(flops=planes * 3 * 16384 * 20, transcendentals=0, bytes_accessed=planes * 16384 * 4 * 22)


def params(mib):
    return pltpu.CompilerParams(vmem_limit_bytes=mib * MIB)


def hbm(x):
    return pltpu.with_memory_space_constraint(x, pltpu.HBM)


def vmem(x):
    return pltpu.with_memory_space_constraint(x, pltpu.VMEM)


def clear_walls(ref, lead):
    for index in lead:
        ref[(*index, pl.ds(0, 8), slice(None))] = jnp.zeros((8, 128), F32)
        ref[(*index, pl.ds(136, 8), slice(None))] = jnp.zeros((8, 128), F32)


def begin(copies, sems):
    started = [pltpu.make_async_copy(s, t, sems.at[i]) for i, (s, t) in enumerate(copies)]
    for copy in started:
        copy.start()
    return started


def even(axis):
    return lax.axis_index(axis) % 2 == 0


def in_order(axis, a, b):
    return jnp.where(even(axis), b, a), jnp.where(even(axis), a, b)


def pack_kernel(adj, vel, visc, adj_s, visc_s, vel_s, za, zb, msg_a, msg_b, *rest):
    acc_l, acc_r, vel_l, vel_r, sems = rest
    inside = pl.ds(8, 128)
    n = 16 // GROUPS

    def copies(g):
        xs = pl.ds(g * n, n)
        return (
            (adj.at[:, xs], adj_s.at[:, pl.ds(2 + g * n, n), inside]),
            (visc.at[xs], visc_s.at[pl.ds(2 + g * n, n), inside]),
            (vel.at[:, xs], vel_s.at[:, pl.ds(1 + g * n, n)]),
        )

    started = [begin(copies(g), sems.at[g]) for g in range(GROUPS)]
    clear_walls(adj_s, [(c, q) for c in range(3) for q in range(1, 20)])
    clear_walls(visc_s, [(q,) for q in range(1, 20)])
    zero = jnp.zeros((144, 128), F32)
    visc_s[1] = zero
    for c in range(3):
        adj_s[c, 1] = zero
    lane = lanes((32, 128))
    pair = lane >> 1
    pair_l = ((lane + 2) & 127) >> 1
    for g in range(GROUPS):
        for copy in started[g]:
            copy.wait()
        for r in range(4):
            rows = pl.ds(r * 32, 32)
            padded = pl.ds(8 + r * 32, 32)
            half = r // 2
            if g == 0:
                left = right = vleft = vright = jnp.zeros((32, 128), F32)
            else:
                left, right, vleft, vright = (ref[rows] for ref in (acc_l, acc_r, vel_l, vel_r))
            for c in range(4):
                for x in range(g * n, g * n + n):
                    m = c * 16 + x
                    plane = adj_s[c, x + 2, padded] if c < 3 else visc_s[x + 2, padded]
                    turned = roll(plane, 2 * m, 1)
                    right = jnp.where(pair == m, turned, right)
                    left = jnp.where(pair_l == m, turned, left)
            for d in range(3):
                for x in range(g * n, g * n + n):
                    at = 2 * (d * 16 + x) + half
                    turned = roll(vel_s[d, x + 1, rows], at, 1)
                    vright = jnp.where(lane == at, turned, vright)
                    vleft = jnp.where(lane == (at - 1) % 128, turned, vleft)
            if g < GROUPS - 1:
                acc_l[rows] = left
                acc_r[rows] = right
            else:
                zb[rows], za[rows] = in_order("gz", roll(left, 2, 1), right)
                vleft = roll(vleft, 1, 1)
            vel_l[rows] = vleft
            vel_r[rows] = vright
    near = jnp.where(even("gx"), 17, 2)
    for msg, q in ((msg_a, near), (msg_b, 19 - near)):
        for c in range(3):
            msg[c] = adj_s[c, q, inside]
        msg[3] = visc_s[q, inside]
    first = (lanes((64, 128)) & 1) == 0
    right = jnp.where(first, vel_r[pl.ds(0, 64)], vel_r[pl.ds(64, 64)])
    left = jnp.where(first, vel_l[pl.ds(0, 64)], vel_l[pl.ds(64, 64)])
    zb[pl.ds(128, 64)], za[pl.ds(128, 64)] = in_order("gz", left, right)


def pack(adj, vel, visc):
    return pl.pallas_call(
        pack_kernel,
        in_specs=[ANY, ANY, ANY],
        out_specs=[VM] * 7,
        out_shape=[in_vmem(STATE[k]) for k in ("adj", "visc", "vel")]
        + [in_vmem((192, 128))] * 2
        + [in_vmem((4, 128, 128))] * 2,
        scratch_shapes=[
            *[pltpu.VMEM((128, 128), F32)] * 4,
            pltpu.SemaphoreType.DMA((GROUPS, 3)),
        ],
        compiler_params=params(4),
        name="pack",
    )(hbm(adj), hbm(vel), hbm(visc))


def spread(a, group):
    kept = jnp.where((lanes(a.shape) >> 5) == group, a, 0.0)
    kept = kept + roll(kept, 32, 1)
    return kept + roll(kept, 64, 1)


def shift_rows(a, by):
    row = lax.broadcasted_iota(jnp.int32, a.shape, 0)
    moved = roll(a, by, 0)
    edge = 0 if by > 0 else a.shape[0] - 1
    return jnp.where(row == edge, 0.0, moved)


def edge_centre(hl, hr):
    odd = (lanes((128, 128)) & 1) == 1
    return jnp.where(odd, hl[:128], hr[:128])


def edge_velocity(message):
    both = message[128:]
    odd = (lanes(both.shape) & 1) == 1
    upper = jnp.where(odd, roll(both, 1, 1), both)
    lower = jnp.where(odd, both, roll(both, -1, 1))
    return jnp.concatenate([upper, lower], axis=0)


def edge_middle(hl, hr, zl, zr, low=None, high=None):
    lane = lanes((128, 128))
    odd = (lane & 1) == 1
    x = (lane >> 1) & 15
    left, right = hl[:128], hr[:128]
    centre = jnp.where(odd, left, right)
    minus = jnp.where(odd, roll(left, 1, 1), roll(zl[:128], -1, 1))
    plus = jnp.where(odd, roll(zr[:128], 1, 1), roll(right, -1, 1))
    velocity = jnp.where(odd, edge_velocity(hl), edge_velocity(hr))
    west = roll(centre, 2, 1)
    east = roll(centre, -2, 1)
    west = jnp.where(x == 0, 0.0 if low is None else roll(low, -30, 1), west)
    east = jnp.where(x == 15, 0.0 if high is None else roll(high, 30, 1), east)
    north = shift_rows(centre, -1)
    south = shift_rows(centre, 1)
    visc = spread(centre, 3)
    total = 0.0
    result = 0.0
    for d, (up, down) in enumerate(((east, west), (north, south), (plus, minus))):
        v = spread(velocity, d)
        a_up = 0.5 * ((visc + spread(up, 3)) + v)
        a_down = 0.5 * ((visc + spread(down, 3)) - v)
        total = total + (a_up + a_down)
        result = result + (a_up * up + a_down * down)
    return result + (1.0 - total) * centre


def ends(edge, r, m):
    return roll(edge[pl.ds(r, ROWS), :], 127 - 2 * m, 1)


def first_step(adj_s, visc_s, vel_s, mid_s, coef_s, edge, x, ex):
    lane = lanes((ROWS, 128))
    q, t = x + 2, x + 1
    for r in range(0, 128, ROWS):
        rows, here = pl.ds(r, ROWS), pl.ds(8 + r, ROWS)
        above, below = pl.ds(9 + r, ROWS), pl.ds(7 + r, ROWS)

        def sides(plane, m):
            end = ends(edge, r, m)
            up = jnp.where(lane == 127, end, roll(plane, -1, 1))
            return up, jnp.where(lane == 0, end, roll(plane, 1, 1))

        centre = visc_s[q, here, :]
        pairs = (
            (visc_s[q + 1, here, :], visc_s[q - 1, here, :]),
            (visc_s[q, above, :], visc_s[q, below, :]),
            sides(centre, 48 + ex),
        )
        a = []
        for d, (plus, minus) in enumerate(pairs):
            v = vel_s[d, t, rows, :]
            a.append(0.5 * ((centre + plus) + v))
            a.append(0.5 * ((centre + minus) - v))
        a.append(1.0 - (((a[0] + a[1]) + (a[2] + a[3])) + (a[4] + a[5])))
        for k in range(7):
            coef_s[k, t, rows, :] = a[k]
        for c in range(3):
            centre = adj_s[c, q, here, :]
            up, down = sides(centre, c * 16 + ex)
            out = a[6] * centre
            out = out + a[0] * adj_s[c, q + 1, here, :]
            out = out + a[1] * adj_s[c, q - 1, here, :]
            out = out + a[2] * adj_s[c, q, above, :]
            out = out + a[3] * adj_s[c, q, below, :]
            out = out + a[4] * up
            mid_s[c, t, here, :] = out + a[5] * down
    for c in range(3):
        mid_s[c, t, pl.ds(0, 8), :] = jnp.zeros((8, 128), F32)
        mid_s[c, t, pl.ds(136, 8), :] = jnp.zeros((8, 128), F32)


def second_step(mid_s, coef_s, edge, x, store):
    lane = lanes((ROWS, 128))
    t = x + 1
    for r in range(0, 128, ROWS):
        rows, here = pl.ds(r, ROWS), pl.ds(8 + r, ROWS)
        above, below = pl.ds(9 + r, ROWS), pl.ds(7 + r, ROWS)
        a = [coef_s[k, t, rows, :] for k in range(7)]
        for c in range(3):
            centre = mid_s[c, t, here, :]
            end = ends(edge, r, c * 16 + x)
            out = a[6] * centre
            out = out + a[0] * mid_s[c, t + 1, here, :]
            out = out + a[1] * mid_s[c, t - 1, here, :]
            out = out + a[2] * mid_s[c, t, above, :]
            out = out + a[3] * mid_s[c, t, below, :]
            out = out + a[4] * jnp.where(lane == 127, end, roll(centre, -1, 1))
            store(c, rows, out + a[5] * jnp.where(lane == 0, end, roll(centre, 1, 1)))


def face_kernel(
    adj_s, visc_s, vel_s, ra, rb, za, zb, face, mid_s, coef_s, centre, middle
):
    hl, hr = in_order("gz", ra[...], rb[...])
    zr, zl = in_order("gz", za[...], zb[...])
    centre[...] = edge_centre(hl, hr)
    middle[...] = edge_middle(hl, hr, zl, zr)
    for c in range(3):
        mid_s[c, 0] = jnp.zeros((144, 128), F32)
    for x in range(2):
        first_step(adj_s, visc_s, vel_s, mid_s, coef_s, centre, x, x)
    own = jnp.where(lax.axis_index("gx") == 0, 1.0, 0.0)

    def store(c, rows, v):
        face[c, rows, :] = v * own

    second_step(mid_s, coef_s, middle, 0, store)


def face_call(state, ha, hb, za, zb):
    return pl.pallas_call(
        face_kernel,
        in_specs=[VM] * 7,
        out_specs=[VM] * 5,
        out_shape=[
            in_vmem((3, 128, 128)),
            in_vmem(STATE["mid"]),
            in_vmem(STATE["coef"]),
            in_vmem((128, 128)),
            in_vmem((128, 128)),
        ],
        compiler_params=params(4),
        cost_estimate=cost(3),
        name="face",
    )(*[vmem(a) for a in (*state, ha, hb, za, zb)])


def choose(lists, place):
    gx, gz = lax.axis_index("gx"), lax.axis_index("gz")
    half = lists[:, pl.ds(pl.multiple_of((gz // 4) * 128, 128), 128)]
    tile = lax.broadcasted_iota(jnp.int32, (512, 128), 0)
    listed = jnp.zeros((512, 128), F32)
    for k in range(8):
        listed = listed + jnp.where(half[k : k + 1] == tile, 1.0, 0.0)
    row = lax.broadcasted_iota(jnp.int32, (128, 512), 0)
    wanted = gx * 32 + ((row >> 4) ^ gz) * 4 + ((row >> 2) & 3)
    sits = jnp.where(place[...] == wanted, 1.0, 0.0).astype(BF16)
    count = jnp.dot(sits, listed.astype(BF16), preferred_element_type=F32)
    row = lax.broadcasted_iota(jnp.int32, (128, 128), 0)
    column = lanes((128, 128))
    ours = jnp.where(row == (gz % 4) * 32 + (column >> 2), 1.0, 0.0).astype(BF16)
    wide = jnp.dot(count.astype(BF16), ours, preferred_element_type=F32)
    return jnp.where((row & 3) == (column & 3), wide, 0.0)


FIELD = (3, 16, 128, 128)


def run_first(cells, state, mid_s, coef_s, edge):
    for x in cells:
        first_step(*state, mid_s, coef_s, edge, x, x)


def run_second(cells, mid_s, coef_s, edge, done):
    for x in cells:

        def store(c, rows, v, x=x):
            done[c, x, rows, :] = v

        second_step(mid_s, coef_s, edge, x, store)


def inner_kernel(
    adj_s, visc_s, vel_s, centre, middle, lists, place, _, __, mid_s, coef_s, done, chosen
):
    chosen[...] = choose(lists, place)
    run_first(range(2, 9), (adj_s, visc_s, vel_s), mid_s, coef_s, centre)
    run_second(range(2, 8), mid_s, coef_s, middle, done)


def inner(state, centre, middle, lists, place, mid, coef):
    return pl.pallas_call(
        inner_kernel,
        in_specs=[VM] * 9,
        out_specs=[VM] * 4,
        out_shape=[in_vmem(STATE["mid"]), in_vmem(STATE["coef"]), in_vmem(FIELD), in_vmem((128, 128))],
        input_output_aliases={7: 0, 8: 1},
        compiler_params=params(4),
        cost_estimate=cost(13),
        name="inner",
    )(*[vmem(a) for a in (*state, centre, middle)], lists, place, *[vmem(a) for a in (mid, coef)])


def ends_kernel(
    adj_i, visc_i, vel_s, centre, middle, ra, rb, _, __, ___, ____,
    adj_s, visc_s, mid_s, coef_s, done, out, msg_a, msg_b, sems,
):
    started = begin([(done.at[:, pl.ds(8, 6)], out.at[:, pl.ds(8, 6)])], sems)
    beyond = jnp.where(even("gx"), 18, 1)
    for msg, q in ((ra, beyond), (rb, 19 - beyond)):
        for c in range(3):
            adj_s[c, q, pl.ds(8, 128)] = msg[c]
        visc_s[q, pl.ds(8, 128)] = msg[3]
    run_first((0, 15), (adj_s, visc_s, vel_s), mid_s, coef_s, centre)
    near = jnp.where(even("gx"), 16, 1)
    for msg, t in ((msg_a, near), (msg_b, 17 - near)):
        for c in range(3):
            msg[c] = mid_s[c, t, pl.ds(8, 128)]
        msg[3] = centre[...]
    run_second((1, 14), mid_s, coef_s, middle, done)
    for copy in started:
        copy.wait()


def ends_call(state, centre, middle, ra, rb, mid, coef, done, out):
    held = [vmem(a) for a in (*state, centre, middle, ra, rb, mid, coef, done)]
    return pl.pallas_call(
        ends_kernel,
        in_specs=[VM] * 10 + [ANY],
        out_specs=[VM] * 5 + [ANY, VM, VM],
        out_shape=[in_vmem(STATE[k]) for k in ("adj", "visc", "mid", "coef")]
        + [in_vmem(FIELD), pltpu.HBM(FIELD, F32)]
        + [in_vmem((4, 128, 128))] * 2,
        scratch_shapes=[pltpu.SemaphoreType.DMA((1,))],
        input_output_aliases={0: 0, 1: 1, 7: 2, 8: 3, 9: 4, 10: 5},
        compiler_params=params(4),
        cost_estimate=cost(4),
        name="ends",
    )(*held, hbm(out))[2:]


def middle_kernel(
    adj_s, visc_s, vel_s, centre, middle, _, __, ___, filters, mid_s, coef_s, done, out, kept, sems
):
    started = begin([(done.at[:, pl.ds(2, 6)], out.at[:, pl.ds(2, 6)]), (filters, kept)], sems)
    run_first(range(9, 15), (adj_s, visc_s, vel_s), mid_s, coef_s, centre)
    run_second(range(8, 14), mid_s, coef_s, middle, done)
    for copy in started:
        copy.wait()


def middle_call(state, centre, middle, mid, coef, done, filters):
    held = [vmem(a) for a in (*state, centre, middle, mid, coef, done)]
    return pl.pallas_call(
        middle_kernel,
        in_specs=[VM] * 8 + [ANY],
        out_specs=[VM] * 3 + [ANY, VM],
        out_shape=[in_vmem(STATE["mid"]), in_vmem(STATE["coef"]), in_vmem(FIELD)]
        + [pltpu.HBM(FIELD, F32), pltpu.VMEM(filters.shape, BF16)],
        scratch_shapes=[pltpu.SemaphoreType.DMA((2,))],
        input_output_aliases={5: 0, 6: 1, 7: 2},
        compiler_params=params(4),
        cost_estimate=cost(12),
        name="middle",
    )(*held, hbm(filters))


def last_kernel(
    ha, hb, za, zb, ra, rb, _, coef_s, __, ___, mid_s, done, out, edges, sems
):
    copies = [
        pltpu.make_async_copy(done.at[:, pl.ds(x, n)], out.at[:, pl.ds(x, n)], sems.at[i])
        for i, (x, n) in enumerate(((1, 1), (14, 1), (0, 1), (15, 1)))
    ]
    copies[0].start()
    copies[1].start()
    hl, hr = in_order("gz", ha[...], hb[...])
    zr, zl = in_order("gz", za[...], zb[...])
    low, high = in_order("gx", ra[3], rb[3])
    edges[...] = edge_middle(hl, hr, zl, zr, low, high)
    beyond = jnp.where(even("gx"), 17, 0)
    for msg, t in ((ra, beyond), (rb, 17 - beyond)):
        for c in range(3):
            mid_s[c, t, pl.ds(8, 128)] = msg[c]
    for i, x in ((2, 0), (3, 15)):
        run_second((x,), mid_s, coef_s, edges, done)
        copies[i].start()
    for copy in copies:
        copy.wait()


def last_call(ha, hb, za, zb, ra, rb, mid, coef, done, out):
    held = [vmem(a) for a in (ha, hb, za, zb, ra, rb, mid, coef, done)]
    return pl.pallas_call(
        last_kernel,
        in_specs=[VM] * 9 + [ANY],
        out_specs=[VM] * 2 + [ANY],
        out_shape=[in_vmem(STATE["mid"]), in_vmem(FIELD), pltpu.HBM(FIELD, F32)],
        scratch_shapes=[pltpu.VMEM((128, 128), F32), pltpu.SemaphoreType.DMA((4,))],
        input_output_aliases={6: 0, 8: 1, 9: 2},
        compiler_params=params(4),
        cost_estimate=cost(4),
        name="last",
    )(*held, hbm(out))[-1]


def join_kernel(*refs):
    total = refs[0][...]
    for ref in refs[1:-1]:
        total = total + ref[...]
    refs[-1][...] = total


def join(*parts):
    return pl.pallas_call(
        join_kernel,
        in_specs=[VM] * len(parts),
        out_specs=VM,
        out_shape=in_vmem(parts[0].shape),
        compiler_params=params(2),
        name="join",
    )(*[vmem(a) for a in parts])


def pieces(a):
    high = a.astype(BF16)
    rest = a - high.astype(F32)
    mid = rest.astype(BF16)
    low = (rest - mid.astype(F32)).astype(BF16)
    return high, mid, low


PART = (3, 16, 128)


def sums_kernel(chosen, face, more, *pairs):
    matrix = chosen[...].astype(BF16)
    for c in range(3):
        total = 0.0
        for piece in pieces(face[c] + more[c]):
            total = total + jnp.dot(matrix, piece, preferred_element_type=F32)
        for k in range(8):
            pairs[k // 2][k % 2, c] = total[k * 16 : k * 16 + 16]


def partial_sums(chosen, face, more):
    return pl.pallas_call(
        sums_kernel,
        in_specs=[VM] * 3,
        out_specs=[VM] * 4,
        out_shape=[in_vmem((2, *PART))] * 4,
        compiler_params=params(2),
        name="sums",
    )(vmem(chosen), vmem(face), vmem(more))


def gather_kernel(a, b, c, d, kept, given):
    kept[...] = (a[0] + b[0]) + (c[0] + d[0])
    given[...] = (a[1] + b[1]) + (c[1] + d[1])


def gather(pairs):
    return pl.pallas_call(
        gather_kernel,
        in_specs=[VM] * 4,
        out_specs=[VM] * 2,
        out_shape=[in_vmem(PART)] * 2,
        compiler_params=params(2),
        name="gather",
    )(*[vmem(a) for a in pairs])


def product_kernel(kept, came, filters, out, sums):
    sums[...] = kept[...] + came[...]
    for p in range(4):
        view = jnp.concatenate([sums[:, p * 4 + i, :] for i in range(4)], axis=1)
        stacked = jnp.concatenate(pieces(view), axis=0)
        wide = jnp.dot(stacked, filters[p], preferred_element_type=F32)
        out[:, p, :] = wide[0:3] + (wide[3:6] + wide[6:9])


def product(parts, filters):
    return pl.pallas_call(
        product_kernel,
        in_specs=[VM] * 3,
        out_specs=VM,
        out_shape=jax.ShapeDtypeStruct((3, 4, 512), F32),
        scratch_shapes=[pltpu.VMEM(PART, F32)],
        compiler_params=params(4),
        name="product",
    )(*[vmem(a) for a in (*parts, filters)])


def shards(adjoint, velocity, viscosity, filters, block_tiles, tile_place):
    nx = lax.axis_size("gx")
    nz = lax.axis_size("gz")
    inside_z = [(i, i ^ 1) for i in range(nz)]
    across_z = [(i, (i + 1 if i % 2 else i - 1) % nz) for i in range(nz)]
    inside_x = [(i, i ^ 1) for i in range(nx)]
    across_x = [(i, i + 1 if i % 2 else i - 1) for i in range(1, nx - 1)]

    *state, za, zb, msg_a, msg_b = pack(adjoint, velocity, viscosity)
    ha = lax.ppermute(za, "gz", inside_z)
    hb = lax.ppermute(zb, "gz", across_z)
    face, mid, coef, centre, middle = face_call(state, ha, hb, za, zb)

    face, msg_a, msg_b = lax.optimization_barrier((face, msg_a, msg_b))
    ra = lax.ppermute(msg_a, "gx", inside_x)
    rb = lax.ppermute(msg_b, "gx", across_x)
    got = [lax.ppermute(face, "gx", [(0, k)]) for k in (6, 2, 8)]
    mid, coef, done, chosen = inner(
        state, centre, middle, block_tiles.T, tile_place.reshape(1, -1), mid, coef
    )
    *got, mid, coef, done = lax.optimization_barrier((*got, mid, coef, done))
    face = join(face, *got)
    far = lax.ppermute(face, "gx", [(0, 4), (2, 10), (6, 14), (8, 12)])
    mid, coef, done, out, near = middle_call(state, centre, middle, mid, coef, done, filters)
    mid, coef, done, out, msg_a, msg_b = ends_call(
        state, centre, middle, ra, rb, mid, coef, done, out
    )
    ra = lax.ppermute(msg_a, "gx", inside_x)
    rb = lax.ppermute(msg_b, "gx", across_x)
    far, mid, coef, done = lax.optimization_barrier((far, mid, coef, done))
    face = join(face, far)
    other = lax.ppermute(face, "gx", [(i, i + 1) for i in range(0, nx, 2)])
    own, *pairs = partial_sums(chosen, face, other)
    pairs = [
        lax.ppermute(pairs[k // 2 - 1], "gz", [(i, i ^ k) for i in range(nz)]) for k in (4, 2, 6)
    ]
    kept, given = gather((own, *pairs))
    came = lax.ppermute(given, "gz", inside_z)
    out = last_call(ha, hb, za, zb, ra, rb, mid, coef, done, out)
    came, out = lax.optimization_barrier((came, out))
    gradient = product((kept, came), near).transpose(1, 0, 2)
    return out, gradient


def solution(mesh):
    placed = (
        P(None, "gx", None, "gz"),
        P(None, "gx", None, "gz"),
        P("gx", None, "gz"),
        P(("gx", "gz"), None, None),
        P(),
        P(),
    )
    return jax.shard_map(
        shards,
        mesh=mesh,
        in_specs=placed,
        out_specs=(P(None, "gx", None, "gz"), P(("gx", "gz"), None, None)),
        check_vma=False,
    )
```
